32 devices in a mesh: fsdp: 32 (over z, y, x, core).
Axes of the slice: x: 2, y: 2, z: 4, core: 2. Of those that a mesh axis runs over, the one named last changes fastest.
Arguments:
- inputs: bfloat16 [32768, 768], P('fsdp'), may hold values from -6 to 6
- cotangent: bfloat16 [32768, 768], P('fsdp'), may hold values from -6 to 6
- lengths: int32 [64, 8], P('fsdp'), may hold values from 0 to 128, as said below
- timesteps: int32 [64, 8], P('fsdp'), may hold values from 0 to 1999
- time_weight: bfloat16 [128, 768], P(None, 'fsdp'), may hold values from -0.5 to 0.5
- time_bias: bfloat16 [768], P('fsdp'), may hold values from -1.1953125 to 1.1953125
- query_weight: bfloat16 [768, 768], P('fsdp'), may hold values from -0.21875 to 0.21875
- query_bias: bfloat16 [768], P('fsdp'), may hold values from -1.1953125 to 1.1953125
- key_weight: bfloat16 [768, 768], P('fsdp'), may hold values from -0.21875 to 0.21875
- value_weight: bfloat16 [768, 768], P('fsdp'), may hold values from -0.21875 to 0.21875
- value_bias: bfloat16 [768], P('fsdp'), may hold values from -1.1953125 to 1.1953125
- out_weight: bfloat16 [768, 768], P('fsdp'), may hold values from -0.875 to 0.875
- out_bias: bfloat16 [768], P('fsdp'), may hold values from -1.1953125 to 1.1953125
- mid_gain: bfloat16 [768], P('fsdp'), may hold values from 0.5 to 1.5
- mid_shift: bfloat16 [768], P('fsdp'), may hold values from -1.1953125 to 1.1953125
- up_weight: bfloat16 [768, 3072], P('fsdp'), may hold values from -0.21875 to 0.21875
- up_bias: bfloat16 [3072], P('fsdp'), may hold values from -1.1953125 to 1.1953125
- down_weight: bfloat16 [3072, 768], P('fsdp'), may hold values from -0.109375 to 0.109375
- down_bias: bfloat16 [768], P('fsdp'), may hold values from -1.1953125 to 1.1953125
- last_gain: bfloat16 [768], P('fsdp'), may hold values from 0.5 to 1.5
- last_shift: bfloat16 [768], P('fsdp'), may hold values from -1.1953125 to 1.1953125
Outputs:
- layer_out: bfloat16 [32768, 768], P('fsdp')
- input_grad: float32 [32768, 768], P('fsdp')
- time_weight_grad: float32 [128, 768], P(None, 'fsdp')
- query_weight_grad: float32 [768, 768], P('fsdp')
- key_weight_grad: float32 [768, 768], P('fsdp')
- value_weight_grad: float32 [768, 768], P('fsdp')
- out_weight_grad: float32 [768, 768], P('fsdp')
- up_weight_grad: float32 [768, 3072], P('fsdp')
- down_weight_grad: float32 [3072, 768], P('fsdp')
- time_bias_grad: float32 [768], P('fsdp')
- query_bias_grad: float32 [768], P('fsdp')
- value_bias_grad: float32 [768], P('fsdp')
- out_bias_grad: float32 [768], P('fsdp')
- mid_gain_grad: float32 [768], P('fsdp')
- mid_shift_grad: float32 [768], P('fsdp')
- up_bias_grad: float32 [3072], P('fsdp')
- down_bias_grad: float32 [768], P('fsdp')
- last_gain_grad: float32 [768], P('fsdp')
- last_shift_grad: float32 [768], P('fsdp')
The draws below stay inside these ranges and needn't reach their ends.
Inputs may be any that keep to these rules, and one draw needn't show every extreme that they name: Each row gives the lengths of the sequences packed in order into one block of 512 rows; every entry is 0, 64 or 128, the row sums to 512, and every row holds at least one entry of each nonzero length. `timesteps`: the diffusion step of the sequence in each slot; slots of length 0 carry a step too.
All inputs are finite; a program needn't handle non-finite values.
Results may differ from the reference program's by a relative error of at most 0.017.
Values may be sent and summed in bfloat16 or wider, within the bound.
No kernel may reach another device: no remote copies, remote signals or barrier semaphores. Data moves between devices by JAX's collectives and lax.ppermute only.
A program may use at most 128 MiB of HBM per device.

```python
import math
import jax
import jax.numpy as jnp
from jax import lax

D = 768
HEADS = 12
HEAD = 64
FF = 3072
TDIM = 128
SLOTS = 8
SHORT = 64
TOK_DEV = 512
BLOCKS = 64
TOKENS = 32768


def draw_lengths(key, part):
    longer = jax.random.randint(jax.random.fold_in(key, 11), (BLOCKS, 1), 1, SLOTS // 2)
    index = jnp.arange(SLOTS, dtype=jnp.int32)[None, :]
    base = jnp.where(index < longer, 2 * SHORT, jnp.where(index < SLOTS - longer, SHORT, 0)).astype(jnp.int32)
    noise = jax.random.randint(jax.random.fold_in(key, 12), (BLOCKS, SLOTS), 0, 1 << 20) * SLOTS + index
    order = jnp.argsort(noise, axis=1)
    return jnp.take_along_axis(base, order, axis=1).astype(jnp.int32)


def touch_ends(entries, own_key, least, top_value):
    shape = entries.shape
    index_at = [jax.random.randint(jax.random.fold_in(own_key, axis), (), 0, shape[axis]) for axis in range(len(shape))]
    entries = entries.at[tuple(index_at)].set(least)
    longest = shape.index(max(shape))
    index_at[longest] = (index_at[longest] + 1) % shape[longest]
    return entries.at[tuple(index_at)].set(top_value)


def levels(rng, dims, cuts, least, top_value):
    gain, own = 1.0, jax.random.fold_in(rng, 6)
    for axis_at, parts in cuts:
        steps = jnp.exp(jax.random.uniform(jax.random.fold_in(own, axis_at), (parts,), jnp.float32, least / len(cuts), top_value / len(cuts)))
        gain = gain * jnp.repeat(steps, dims[axis_at] // parts).reshape([-1 if axis == axis_at else 1 for axis in range(len(dims))])
    return gain


def scatter_about(own_key, extent, deviation, limit, shards=(), kind=jnp.bfloat16):
    drawn = deviation * jax.random.normal(own_key, extent, jnp.float32)
    if shards:
        drawn = drawn * levels(own_key, extent, shards, -0.22, 0.18)
    return jnp.clip(drawn, -limit, limit).astype(kind)


def setup_inputs(seed: int = 0) -> dict:
    splits = jax.random.split(jax.random.key(seed), 22)
    inputs = scatter_about(splits[0], (TOKENS, D), 1.0, 6.0, ((0, 32),))
    cotangent = scatter_about(splits[1], (TOKENS, D), 1.0, 6.0, ((0, 32),))
    lengths = draw_lengths(jax.random.fold_in(splits[21], 71), 0)
    timesteps = touch_ends(jax.random.randint(splits[3], (BLOCKS, SLOTS), 0, 2000), jax.random.fold_in(splits[3], 1), 0, 1999).astype(jnp.int32)
    time_weight = scatter_about(splits[4], (TDIM, D), TDIM ** -0.5, 0.5, ((1, 32),))
    time_bias = scatter_about(splits[5], (D,), 0.2, 1.1953125, ((0, 32),))
    query_weight = scatter_about(splits[6], (D, D), D ** -0.5, 0.21875, ((0, 32),))
    query_bias = scatter_about(splits[7], (D,), 0.2, 1.1953125, ((0, 32),))
    key_weight = scatter_about(splits[8], (D, D), D ** -0.5, 0.21875, ((0, 32),))
    value_weight = scatter_about(splits[9], (D, D), D ** -0.5, 0.21875, ((0, 32),))
    value_bias = scatter_about(splits[10], (D,), 0.2, 1.1953125, ((0, 32),))
    out_weight = scatter_about(splits[11], (D, D), (D // 16) ** -0.5, 0.875, ((0, 32),))
    out_bias = scatter_about(splits[12], (D,), 0.2, 1.1953125, ((0, 32),))
    mid_gain = jnp.clip(1.0 + 0.1 * jax.random.normal(splits[13], (D,), jnp.float32), 0.5, 1.5).astype(jnp.bfloat16)
    mid_shift = scatter_about(splits[14], (D,), 0.2, 1.1953125, ((0, 32),))
    up_weight = scatter_about(splits[15], (D, FF), D ** -0.5, 0.21875, ((0, 32),))
    up_bias = scatter_about(splits[16], (FF,), 0.2, 1.1953125, ((0, 32),))
    down_weight = scatter_about(splits[17], (FF, D), FF ** -0.5, 0.109375, ((0, 32),))
    down_bias = scatter_about(splits[18], (D,), 0.2, 1.1953125, ((0, 32),))
    last_gain = jnp.clip(1.0 + 0.1 * jax.random.normal(splits[19], (D,), jnp.float32), 0.5, 1.5).astype(jnp.bfloat16)
    last_shift = scatter_about(splits[20], (D,), 0.2, 1.1953125, ((0, 32),))
    return {"inputs": inputs, "cotangent": cotangent, "lengths": lengths, "timesteps": timesteps, "time_weight": time_weight, "time_bias": time_bias, "query_weight": query_weight, "query_bias": query_bias, "key_weight": key_weight, "value_weight": value_weight, "value_bias": value_bias, "out_weight": out_weight, "out_bias": out_bias, "mid_gain": mid_gain, "mid_shift": mid_shift, "up_weight": up_weight, "up_bias": up_bias, "down_weight": down_weight, "down_bias": down_bias, "last_gain": last_gain, "last_shift": last_shift}


@jax.custom_vjp
def low(v):
    return lax.optimization_barrier(v.astype(jnp.bfloat16)).astype(jnp.float32)

@jax.custom_vjp
def low_back(v):
    return v

def low_keep(v):
    return (low(v), None)

def low_pass(kept, grad):
    return (grad,)

def back_keep(v):
    return (v, None)

def back_low(kept, grad):
    return (low(grad),)
low.defvjp(low_keep, low_pass)
low_back.defvjp(back_keep, back_low)
EPS = 1e-05
NEG = -1e+30
HIGH = lax.Precision.HIGHEST

def sinusoid(steps, width):
    half = width // 2
    freqs = jnp.exp(-math.log(10000.0) * jnp.arange(half, dtype=jnp.float32) / half)
    angles = steps.astype(jnp.float32)[:, None] * freqs[None, :]
    return jnp.concatenate([jnp.cos(angles), jnp.sin(angles)], axis=1)

def slot_table(slot_lengths, rows):
    ends = jnp.cumsum(slot_lengths)
    position = jnp.arange(rows, dtype=jnp.int32)
    owner = lax.optimization_barrier(jnp.sum((position[:, None] >= ends[None, :]).astype(jnp.int32), axis=1))
    table = (owner[:, None] == jnp.arange(slot_lengths.shape[0], dtype=jnp.int32)[None, :]).astype(jnp.float32)
    return (owner, table)

def layer_norm(values):
    center = values - lax.optimization_barrier(jnp.mean(values, axis=-1, keepdims=True))
    inverse = lax.rsqrt(lax.optimization_barrier(jnp.mean(center * center, axis=-1, keepdims=True)) + EPS)
    return center * inverse

def attend(pieces):
    queries, keyset, valueset, owner = pieces
    raw = jnp.einsum('qhd,khd->hqk', queries, keyset, precision=HIGH) * HEAD ** (-0.5)
    scores = low_back(raw)
    same = owner[:, None] == owner[None, :]
    scores = jnp.where(same[None, :, :], scores, NEG)
    probs = low(jax.nn.softmax(scores, axis=-1))
    mixed = jnp.einsum('hqk,khd->qhd', probs, valueset, precision=HIGH)
    return mixed.reshape(TOK_DEV, D)

def reference(inputs, cotangent, lengths, timesteps, time_weight, time_bias, query_weight, query_bias, key_weight, value_weight, value_bias, out_weight, out_bias, mid_gain, mid_shift, up_weight, up_bias, down_weight, down_bias, last_gain, last_shift):
    owners, tables = jax.vmap(lambda row: slot_table(row, TOK_DEV))(lengths)
    embed_in = low(sinusoid(timesteps.reshape(-1), TDIM))

    def forward(rows_in, time_w, time_b, query_w, query_b, key_w, value_w, value_b, output_w, output_b, mid_g, mid_s, upper_w, upper_b, lower_w, lower_b, last_g, last_s):
        slot_embed = low_back(jnp.dot(embed_in, time_w, precision=HIGH) + time_b)
        per_row = jnp.einsum('brs,bsd->brd', tables, slot_embed.reshape(BLOCKS, SLOTS, D), precision=HIGH)
        hidden0 = rows_in + per_row.reshape(TOKENS, D)
        operand = low(hidden0)
        queries = low(low_back(jnp.dot(operand, query_w, precision=HIGH) + query_b))
        keyset = low(low_back(jnp.dot(operand, key_w, precision=HIGH)))
        valueset = low(low_back(jnp.dot(operand, value_w, precision=HIGH) + value_b))
        shaped = (queries.reshape(BLOCKS, TOK_DEV, HEADS, HEAD), keyset.reshape(BLOCKS, TOK_DEV, HEADS, HEAD), valueset.reshape(BLOCKS, TOK_DEV, HEADS, HEAD), owners)
        mixed = lax.map(jax.checkpoint(attend), shaped).reshape(TOKENS, D)
        mixed = low(low_back(mixed))
        attended = low_back(jnp.dot(mixed, output_w, precision=HIGH) + output_b)
        first_sum = hidden0 + attended
        middle = layer_norm(first_sum) * mid_g + mid_s
        expanded = low_back(jnp.dot(low(middle), upper_w, precision=HIGH) + upper_b)
        activated = low(jax.nn.gelu(expanded, approximate=False))
        lowered = low_back(jnp.dot(activated, lower_w, precision=HIGH) + lower_b)
        second_sum = middle + lowered
        return layer_norm(second_sum) * last_g + last_s
    params = (time_weight, time_bias, query_weight, query_bias, key_weight, value_weight, value_bias, out_weight, out_bias, mid_gain, mid_shift, up_weight, up_bias, down_weight, down_bias, last_gain, last_shift)
    params32 = tuple((item.astype(jnp.float32) for item in params))
    final, pullback = jax.vjp(forward, inputs.astype(jnp.float32), *params32)
    grads = pullback(cotangent.astype(jnp.float32))
    return (final.astype(jnp.bfloat16), grads[0], grads[1], grads[3], grads[5], grads[6], grads[8], grads[12], grads[14], grads[2], grads[4], grads[7], grads[9], grads[10], grads[11], grads[13], grads[15], grads[16], grads[17])
```

```python
import functools
import math

import jax
import jax.numpy as jnp
from jax import lax
from jax.experimental import pallas as pl
from jax.experimental.pallas import tpu as pltpu
from jax.sharding import PartitionSpec as P

D = 768
HEAD = 64
HEADS = 12
FF = 3072
TDIM = 128
SLOTS = 8
BLOCK = 512
HALF = D // 2
QKV = 3 * HALF
CHIPS = 16
EPS = 1e-05
NEG = -1e30
HIGH = lax.Precision.HIGHEST
SQRT_HALF = 0.7071067811865476
INV_ROOT_TAU = 0.3989422804014327
WINDOWS = (0, 64, 192, 256)
F32 = jnp.float32
BF16 = jnp.bfloat16
ANY = pl.BlockSpec(memory_space=pl.ANY)
OWN_ROW, OTHER_ROW, OWN_POS, OTHER_POS, CORE_AT = 0, 16, 32, 48, 64


def nn(left, right):
    return lax.dot_general(left, right, (((1,), (0,)), ((), ())), preferred_element_type=F32)


def nt(left, right):
    return lax.dot_general(left, right, (((1,), (1,)), ((), ())), preferred_element_type=F32)


def tn(left, right):
    return lax.dot_general(left, right, (((0,), (0,)), ((), ())), preferred_element_type=F32)


def mean(values):
    return jnp.sum(values, axis=-1, keepdims=True) * (1.0 / D)


def normalize(values):
    center = values - mean(values)
    inverse = lax.rsqrt(mean(center * center) + EPS)
    return center * inverse, inverse


def norm_back(grad, normed, inverse):
    return inverse * (grad - mean(grad) - normed * mean(grad * normed))


def column_sum(values):
    return jnp.sum(values, axis=0, keepdims=True)


def piece_copies(tbl, refs, weight, sems, rows, cols):
    own_low, own_high, other_low, other_high = refs
    core = tbl[CORE_AT]
    copies = []
    for kind, (low, high) in enumerate(((own_low, own_high), (other_low, other_high))):
        half = core if kind == 0 else 1 - core
        for j in range(CHIPS):
            src = (low if j < CHIPS // 2 else high).at[j % (CHIPS // 2)]
            at = pl.multiple_of(tbl[kind * CHIPS + j] * rows, rows)
            dst = weight.at[pl.ds(at, rows), pl.ds(pl.multiple_of(half * cols, cols), cols)]
            copies.append(pltpu.make_async_copy(src, dst, sems.at[kind * CHIPS + j]))
    return copies


def lane_masks():
    lane = lax.broadcasted_iota(jnp.int32, (1, 2 * HEAD), 1)
    first = jnp.where(lane < HEAD, 1.0, 0.0)
    return first.astype(BF16), (1.0 - first).astype(BF16), lane < HEAD


def attention_forward_kernel(
    tbl, x_ref, pick_ref, slot_ref, segc_ref, segr_ref, vec_ref, own_low, own_high, other_low, other_high,
    low_ref, qkv_ref, mix_ref, n1_ref, i1_ref, w_ref, weight, bias, hidden, sems, out_sem,
):
    step = pl.program_id(0)
    save = pltpu.make_async_copy(weight, w_ref, out_sem.at[0])

    @pl.when(step == 0)
    def _():
        copies = piece_copies(tbl, (own_low, own_high, other_low, other_high), weight, sems, 48, 4 * HALF)
        for copy in copies:
            copy.start()
        for copy in copies:
            copy.wait()
        save.start()

    slot = lax.dot_general(
        pick_ref[...], slot_ref[...], (((1,), (0,)), ((), ())), precision=HIGH, preferred_element_type=F32
    )
    hidden[...] = x_ref[...].astype(F32) + slot
    low_ref[...] = hidden[...].astype(BF16)
    for t in range(4):
        same = segc_ref[128 * t : 128 * t + 128, :] == segr_ref[0, :, WINDOWS[t] : WINDOWS[t] + 256]
        bias[t] = jnp.where(same, 0.0, NEG)
    for h in range(2):
        y = nn(low_ref[...], weight[:, 4 * HALF * h : 4 * HALF * h + QKV])
        at = QKV * h
        cols = slice(HALF * h, HALF * h + HALF)
        q = (y[:, :HALF] + vec_ref[0:1, cols]).astype(BF16)
        qkv_ref[:, at : at + HALF] = q * jnp.asarray(HEAD**-0.5, BF16)
        qkv_ref[:, at + HALF : at + 2 * HALF] = y[:, HALF : 2 * HALF].astype(BF16)
        qkv_ref[:, at + 2 * HALF : at + QKV] = (y[:, 2 * HALF :] + vec_ref[1:2, cols]).astype(BF16)

    first, second, choose = lane_masks()

    def pair(p, carry):
        at = pl.multiple_of((p // 3) * QKV + (p % 3) * 128, 128)
        for t in range(4):
            rows = slice(128 * t, 128 * t + 128)
            window = slice(WINDOWS[t], WINDOWS[t] + 256)
            q = qkv_ref[rows, pl.ds(at, 128)]
            k = qkv_ref[window, pl.ds(at + HALF, 128)]
            v = qkv_ref[window, pl.ds(at + 2 * HALF, 128)]
            outs = []
            for mask in (first, second):
                s = nt(q * mask, k) + bias[t]
                e = jnp.exp(s - jnp.max(s, axis=1, keepdims=True))
                probs = e * (1.0 / jnp.sum(e, axis=1, keepdims=True))
                outs.append(nn(probs.astype(BF16), v))
            mix_ref[rows, pl.ds(pl.multiple_of(p * 128, 128), 128)] = jnp.where(choose, outs[0], outs[1]).astype(BF16)
        return carry

    lax.fori_loop(0, HEADS // 2, pair, 0)
    for h in range(2):
        at = 4 * HALF * h + QKV
        cols = slice(HALF * h, HALF * h + HALF)
        hidden[:, cols] += nn(mix_ref[...], weight[:, at : at + HALF]) + vec_ref[2:3, cols]
    normed, inverse = normalize(hidden[...])
    n1_ref[...] = normed
    i1_ref[...] = inverse

    @pl.when(step == pl.num_programs(0) - 1)
    def _():
        save.wait()


def upper_tail(values):
    squeezed = 1.0 / (1.0 + (0.3275911 * SQRT_HALF) * jnp.abs(values))
    bell = jnp.exp(values * values * -0.5)
    poly = 0.5 * 1.061405429
    for coefficient in (-1.453152027, 1.421413741, -0.284496736, 0.254829592):
        poly = poly * squeezed + 0.5 * coefficient
    return bell, poly * squeezed * bell


def feed_forward_kernel(
    tbl, n1_ref, i1_ref, cot_ref, vec_ref, upb_ref, ua, ub, uc, ud, da, db, dc, dd,
    res_ref, act_ref, dexp_ref, mlow_ref, din_ref, df_ref, ain_ref, vg_ref, gup_ref,
    up, down, slope, usems, dsems,
):
    step = pl.program_id(0)

    @pl.when(step == 0)
    def _():
        copies = piece_copies(tbl, (ua, ub, uc, ud), up, usems, 48, FF // 2)
        copies += piece_copies(tbl, (da, db, dc, dd), down, dsems, FF // CHIPS, HALF)
        for copy in copies:
            copy.start()
        for copy in copies:
            copy.wait()
        vg_ref[...] = jnp.zeros_like(vg_ref)
        gup_ref[...] = jnp.zeros_like(gup_ref)

    def vec(i):
        return vec_ref[i : i + 1, :]

    normed1 = n1_ref[...]
    middle = normed1 * vec(3) + vec(4)
    mlow_ref[...] = middle.astype(BF16)

    def forward(j, carry):
        at = pl.ds(pl.multiple_of(j * D, D), D)
        u = nn(mlow_ref[...], up[:, at]) + upb_ref[:, at]
        bell, tail = upper_tail(u)
        phi = jnp.where(u >= 0.0, 1.0 - tail, tail)
        act_ref[:, at] = (u * phi).astype(BF16)
        slope[:, at] = (phi + u * bell * INV_ROOT_TAU).astype(BF16)
        return carry

    lax.fori_loop(0, FF // D, forward, 0)
    second = n1_ref[...] * vec(3) + vec(4) + nn(act_ref[...], down[...]) + vec(5)
    normed2, inverse2 = normalize(second)
    res_ref[...] = (normed2 * vec(6) + vec(7)).astype(BF16)
    upstream = cot_ref[...].astype(F32)
    vg_ref[0:1, :] += column_sum(upstream * normed2)
    vg_ref[1:2, :] += column_sum(upstream)
    d_second = norm_back(upstream * vec(6), normed2, inverse2)
    down_in = d_second.astype(BF16)
    din_ref[...] = down_in
    vg_ref[2:3, :] += column_sum(down_in.astype(F32))

    def backward(j, carry):
        at = pl.ds(pl.multiple_of(j * D, D), D)
        d_act = nt(din_ref[...], down[at, :])
        d_exp = (d_act * slope[:, at].astype(F32)).astype(BF16)
        dexp_ref[:, at] = d_exp
        gup_ref[:, at] += column_sum(d_exp.astype(F32))
        return carry

    lax.fori_loop(0, FF // D, backward, 0)
    d_middle = nt(dexp_ref[...], up[...]) + d_second
    normed1 = n1_ref[...]
    vg_ref[3:4, :] += column_sum(d_middle * normed1)
    vg_ref[4:5, :] += column_sum(d_middle)
    d_first = norm_back(d_middle * vec(3), normed1, i1_ref[...])
    df_ref[...] = d_first
    attn_in = d_first.astype(BF16)
    ain_ref[...] = attn_in
    vg_ref[5:6, :] += column_sum(attn_in.astype(F32))


def down_grad_kernel(tbl, act_ref, din_ref, own, other, hold, sems):
    step = pl.program_id(0)
    core = tbl[CORE_AT]
    rows = FF // CHIPS
    hold[step] = tn(act_ref[...], din_ref[...]).astype(BF16)

    def copies(j):
        made = []
        for k in range(4):
            chip = 4 * j + k
            for kind, (target, table) in enumerate(((own, OWN_POS), (other, OTHER_POS))):
                half = core if kind == 0 else 1 - core
                src = hold.at[j, pl.ds(k * rows, rows), pl.ds(pl.multiple_of(half * HALF, HALF), HALF)]
                made.append(pltpu.make_async_copy(src, target.at[tbl[table + chip]], sems.at[j, 2 * k + kind]))
        return made

    for copy in copies(step):
        copy.start()

    @pl.when(step == pl.num_programs(0) - 1)
    def _():
        for j in range(4):
            for copy in copies(j):
                copy.wait()


def up_grad_kernel(tbl, mlow_ref, dexp_ref, mix_ref, ain_ref, own, other, hold, sems):
    step = pl.program_id(0)
    core = tbl[CORE_AT]

    def panel_copy(j, chip, target, table):
        src = hold.at[j, pl.ds(48 * chip, 48), :]
        dst = target.at[tbl[table + chip], :, pl.ds(pl.multiple_of((j % 2) * D, D), D)]
        return pltpu.make_async_copy(src, dst, sems.at[j, chip])

    def each_panel(j, act):
        @pl.when(j // 2 == core)
        def _():
            for chip in range(CHIPS):
                act(panel_copy(j, chip, own, OWN_POS))

        @pl.when(j // 2 != core)
        def _():
            for chip in range(CHIPS):
                act(panel_copy(j, chip, other, OTHER_POS))

    @pl.when(step < 4)
    def _():
        hold[step] = tn(mlow_ref[...], dexp_ref[...]).astype(BF16)
        each_panel(step, lambda copy: copy.start())

    @pl.when(step == 4)
    def _():
        hold[4] = tn(mix_ref[...], ain_ref[...]).astype(BF16)
        out_copies = []
        for chip in range(CHIPS):
            for kind, (target, table) in enumerate(((own, OWN_POS), (other, OTHER_POS))):
                half = core if kind == 0 else 1 - core
                src = hold.at[4, pl.ds(48 * chip, 48), pl.ds(pl.multiple_of(half * HALF, HALF), HALF)]
                dst = target.at[tbl[table + chip], :, pl.ds(2 * D, HALF)]
                out_copies.append(pltpu.make_async_copy(src, dst, sems.at[4 + kind, chip]))
        for copy in out_copies:
            copy.start()
        for copy in out_copies:
            copy.wait()
        for j in range(4):
            each_panel(j, lambda copy: copy.wait())


def attention_backward_kernel(
    tbl, ain_ref, mix_ref, qkv_ref, segc_ref, segr_ref, w_ref, low_ref,
    dqkv_ref, own, other, vg_ref, d_mix, delta, bias, dk, dv, hold, sems,
):
    step = pl.program_id(0)
    base = pl.multiple_of(step * BLOCK, BLOCK)

    @pl.when(step == 0)
    def _():
        vg_ref[...] = jnp.zeros_like(vg_ref)

    ain = ain_ref[...]
    d_mixed = nt(ain[:, :HALF], w_ref[:, QKV : 4 * HALF]) + nt(ain[:, HALF:], w_ref[:, 4 * HALF + QKV :])
    d_mix[...] = d_mixed.astype(BF16)
    product = d_mix[...].astype(F32) * mix_ref[...].astype(F32)
    high = product.astype(BF16)
    rest = (product - high.astype(F32)).astype(BF16)
    head = lax.broadcasted_iota(jnp.int32, (16, D), 0)
    column = lax.broadcasted_iota(jnp.int32, (16, D), 1)
    ones = jnp.where(column // HEAD == head, 1.0, 0.0).astype(BF16)
    dots = nt(ones, high) + nt(ones, rest)
    for h in range(HEADS):
        delta[h] = dots[h : h + 1, :]
    for t in range(4):
        same = segc_ref[WINDOWS[t] : WINDOWS[t] + 256, :] == segr_ref[0, :, 128 * t : 128 * t + 128]
        bias[t] = jnp.where(same, 0.0, NEG)
    first, second, _ = lane_masks()

    def pair(p, carry):
        at = pl.multiple_of((p // 3) * QKV + (p % 3) * 128, 128)
        dk[...] = jnp.zeros_like(dk)
        dv[...] = jnp.zeros_like(dv)
        for t in range(4):
            rows = slice(128 * t, 128 * t + 128)
            window = slice(WINDOWS[t], WINDOWS[t] + 256)
            q = qkv_ref[rows, pl.ds(at, 128)]
            do = d_mix[rows, pl.ds(pl.multiple_of(p * 128, 128), 128)]
            k = qkv_ref[window, pl.ds(at + HALF, 128)]
            v = qkv_ref[window, pl.ds(at + 2 * HALF, 128)]
            queries, outs, keys, scores, weights = [], [], [], [], []
            for h, mask in enumerate((first, second)):
                qm, dom = q * mask, do * mask
                s = nt(k, qm) + bias[t]
                e = jnp.exp(s - jnp.max(s, axis=0, keepdims=True))
                probs = e * (1.0 / jnp.sum(e, axis=0, keepdims=True))
                d_probs = nt(v, dom)
                d_scores = probs * (d_probs - delta[2 * p + h, :, rows])
                queries.append(qm)
                outs.append(dom)
                keys.append(k * mask)
                scores.append(d_scores.astype(BF16))
                weights.append(probs.astype(BF16))
            dk[window, :] += nn(jnp.concatenate(scores, axis=1), jnp.concatenate(queries, axis=0))
            dv[window, :] += nn(jnp.concatenate(weights, axis=1), jnp.concatenate(outs, axis=0))
            dq = tn(jnp.concatenate(scores, axis=0), jnp.concatenate(keys, axis=0)) * HEAD**-0.5
            dqkv_ref[pl.ds(base + 128 * t, 128), pl.ds(at, 128)] = dq.astype(BF16)
        dqkv_ref[pl.ds(base, BLOCK), pl.ds(at + HALF, 128)] = dk[...].astype(BF16)
        dqkv_ref[pl.ds(base, BLOCK), pl.ds(at + 2 * HALF, 128)] = dv[...].astype(BF16)
        return carry

    lax.fori_loop(0, HEADS // 2, pair, 0)
    for h in range(2):
        cols = slice(HALF * h, HALF * h + HALF)
        for row, shift in ((0, 0), (1, 2 * HALF)):
            part = dqkv_ref[pl.ds(base, BLOCK), QKV * h + shift : QKV * h + shift + HALF]
            vg_ref[row : row + 1, cols] += column_sum(part.astype(F32))

    @pl.when(step == pl.num_programs(0) - 1)
    def _():
        core = tbl[CORE_AT]

        def copy_of(half, chip, target, table):
            src = hold.at[half, pl.ds(48 * chip, 48), :]
            return pltpu.make_async_copy(src, target.at[tbl[table + chip]], sems.at[half, chip])

        def each(half, act):
            @pl.when(core == half)
            def _():
                for chip in range(CHIPS):
                    act(copy_of(half, chip, own, OWN_POS))

            @pl.when(core != half)
            def _():
                for chip in range(CHIPS):
                    act(copy_of(half, chip, other, OTHER_POS))

        for half in range(2):
            hold[half] = tn(low_ref[...], dqkv_ref[:, QKV * half : QKV * half + QKV]).astype(BF16)
            each(half, lambda copy: copy.start())
        for half in range(2):
            each(half, lambda copy: copy.wait())


def input_grad_kernel(df_ref, dqkv_ref, w_ref, pick_ref, ig_ref, slot_ref):
    @pl.when(pl.program_id(0) == 0)
    def _():
        slot_ref[...] = jnp.zeros_like(slot_ref)

    grad = df_ref[...] + nt(dqkv_ref[:, :QKV], w_ref[:, :QKV])
    grad += nt(dqkv_ref[:, QKV:], w_ref[:, 4 * HALF : 4 * HALF + QKV])
    ig_ref[...] = grad
    slot_ref[...] += lax.dot_general(
        pick_ref[...], grad, (((0,), (0,)), ((), ())), precision=HIGH, preferred_element_type=F32
    )


def call(kernel, name, grid, in_specs, out_specs, out_shape, scratch, flops, moved, args, prefetch=1, limit=60 << 20):
    return pl.pallas_call(
        kernel,
        name=name,
        grid_spec=pltpu.PrefetchScalarGridSpec(
            num_scalar_prefetch=prefetch, grid=grid, in_specs=in_specs, out_specs=out_specs, scratch_shapes=scratch
        ),
        out_shape=out_shape,
        compiler_params=pltpu.CompilerParams(dimension_semantics=("arbitrary",) * len(grid), vmem_limit_bytes=limit),
        cost_estimate=pl.CostEstimate(flops=flops, bytes_accessed=moved, transcendentals=0),
    )(*args)


def rows_spec(rows, cols):
    return pl.BlockSpec((rows, cols), lambda i, *_: (i, 0))


def whole_spec(shape):
    return pl.BlockSpec(shape, lambda i, *_: (0,) * len(shape))


def cols_spec(rows, cols, top):
    return pl.BlockSpec((rows, cols), lambda i, *_: (0, jnp.minimum(i, top)))


def sds(shape, dtype):
    return jax.ShapeDtypeStruct(shape, dtype)


def attention_forward(tbl, x, pick, slot, segc, segr, vec, pieces):
    rows = x.shape[0]
    return call(
        attention_forward_kernel, "attention_forward", (rows // BLOCK,),
        [rows_spec(BLOCK, D), rows_spec(BLOCK, SLOTS), rows_spec(SLOTS, D), rows_spec(BLOCK, 1),
         pl.BlockSpec((1, 1, BLOCK), lambda i, *_: (i, 0, 0)), whole_spec((8, D))] + [ANY] * 4,
        [rows_spec(BLOCK, D), rows_spec(BLOCK, 2 * QKV), rows_spec(BLOCK, D), rows_spec(BLOCK, D), rows_spec(BLOCK, 1), ANY],
        [sds((rows, D), BF16), sds((rows, 2 * QKV), BF16), sds((rows, D), BF16), sds((rows, D), F32), sds((rows, 1), F32),
         sds((D, 8 * HALF), BF16)],
        [pltpu.VMEM((D, 8 * HALF), BF16), pltpu.VMEM((4, 128, 256), F32), pltpu.VMEM((BLOCK, D), F32),
         pltpu.SemaphoreType.DMA((32,)), pltpu.SemaphoreType.DMA((1,))],
        8 * rows * D * D, 20 << 20, (tbl, x, pick, slot, segc, segr, vec, *pieces),
    )


def feed_forward(tbl, n1, i1, cot, vec, upb, up, down):
    rows = n1.shape[0]
    tile = 256
    return call(
        feed_forward_kernel, "feed_forward", (rows // tile,),
        [rows_spec(tile, D), rows_spec(tile, 1), rows_spec(tile, D), whole_spec((8, D)), whole_spec((1, FF))] + [ANY] * 8,
        [rows_spec(tile, D), rows_spec(tile, FF), rows_spec(tile, FF), rows_spec(tile, D), rows_spec(tile, D),
         rows_spec(tile, D), rows_spec(tile, D), whole_spec((8, D)), whole_spec((1, FF))],
        [sds((rows, D), BF16), sds((rows, FF), BF16), sds((rows, FF), BF16), sds((rows, D), BF16), sds((rows, D), BF16),
         sds((rows, D), F32), sds((rows, D), BF16), sds((8, D), F32), sds((1, FF), F32)],
        [pltpu.VMEM((D, FF), BF16), pltpu.VMEM((FF, D), BF16), pltpu.VMEM((tile, FF), BF16),
         pltpu.SemaphoreType.DMA((32,)), pltpu.SemaphoreType.DMA((32,))],
        8 * rows * D * FF, 30 << 20, (tbl, n1, i1, cot, vec, upb, *up, *down),
    )


def down_grad(tbl, act, din):
    rows = act.shape[0]
    shape = sds((CHIPS, FF // CHIPS, HALF), BF16)
    return call(
        down_grad_kernel, "down_grad", (4,), [cols_spec(rows, D, 3), whole_spec((rows, D))], [ANY, ANY], [shape, shape],
        [pltpu.VMEM((4, D, D), BF16), pltpu.SemaphoreType.DMA((4, 8))],
        2 * rows * D * FF, 12 << 20, (tbl, act, din),
    )


def up_grad(tbl, mlow, dexp, mix, ain):
    rows = mlow.shape[0]
    shape = sds((CHIPS, 48, 2 * D + HALF), BF16)
    return call(
        up_grad_kernel, "up_grad", (5,),
        [whole_spec((rows, D)), cols_spec(rows, D, 3), whole_spec((rows, D)), whole_spec((rows, D))], [ANY, ANY],
        [shape, shape], [pltpu.VMEM((5, D, D), BF16), pltpu.SemaphoreType.DMA((6, CHIPS))],
        2 * rows * D * (FF + D), 16 << 20, (tbl, mlow, dexp, mix, ain),
    )


def attention_backward(tbl, ain, mix, qkv, segc, segr, weight, low):
    rows = ain.shape[0]
    shape = sds((CHIPS, 48, QKV), BF16)
    return call(
        attention_backward_kernel, "attention_backward", (rows // BLOCK,),
        [rows_spec(BLOCK, D), rows_spec(BLOCK, D), rows_spec(BLOCK, 2 * QKV), rows_spec(BLOCK, 1),
         pl.BlockSpec((1, 1, BLOCK), lambda i, *_: (i, 0, 0)), whole_spec((D, 8 * HALF)), whole_spec((rows, D))],
        [whole_spec((rows, 2 * QKV)), ANY, ANY, whole_spec((8, D))],
        [sds((rows, 2 * QKV), BF16), shape, shape, sds((8, D), F32)],
        [pltpu.VMEM((BLOCK, D), BF16), pltpu.VMEM((HEADS, 1, BLOCK), F32), pltpu.VMEM((4, 256, 128), F32),
         pltpu.VMEM((BLOCK, 128), F32), pltpu.VMEM((BLOCK, 128), F32), pltpu.VMEM((2, D, QKV), BF16),
         pltpu.SemaphoreType.DMA((2, CHIPS))],
        10 * rows * D * D, 24 << 20, (tbl, ain, mix, qkv, segc, segr, weight, low),
    )


def input_gradient(df, dqkv, weight, pick):
    rows = df.shape[0]
    tile = 256
    slots = pick.shape[1]
    return call(
        input_grad_kernel, "input_grad", (rows // tile,),
        [rows_spec(tile, D), rows_spec(tile, 2 * QKV), whole_spec((D, 8 * HALF)), rows_spec(tile, slots)],
        [rows_spec(tile, D), whole_spec((slots, D))],
        [sds((rows, D), F32), sds((slots, D), F32)], [],
        6 * rows * D * D, 16 << 20, (df, dqkv, weight, pick), prefetch=0,
    )


def flip(n, even_bit, odd_bit):
    return [(i, i ^ (odd_bit if i & 1 else even_bit)) for i in range(n)]


def tiled_route(n):
    return {"core": flip(n, 1, 1), "z2": flip(n, 16, 16), "z1": flip(n, 8, 8), "a": flip(n, 2, 4), "b": flip(n, 4, 2)}


def tables(n):
    me = lax.axis_index("fsdp")
    core = me % 2
    chips = jnp.arange(CHIPS, dtype=jnp.int32)
    if n == 32:
        here = me // 2

        def order(kind):
            low, high = jnp.where(kind == 0, 1, 2), jnp.where(kind == 0, 2, 1)
            bits = (chips & 1) * 8 + ((chips >> 1) & 1) * 4 + ((chips >> 2) & 1) * low + (chips >> 3) * high
            return here ^ bits

        def place(kind):
            diff = here ^ chips
            x, y = diff & 1, (diff >> 1) & 1
            low, high = jnp.where(kind == 0, x, y), jnp.where(kind == 0, y, x)
            return (diff >> 3) + ((diff >> 2) & 1) * 2 + low * 4 + high * 8

        parts = [order(core), order(1 - core), place(core), place(1 - core)]
    else:
        parts = [chips] * 4
    return jnp.concatenate(parts + [jnp.full((16,), core, jnp.int32)]).astype(jnp.int32)


def own_half(halves, core):
    return jnp.where(core == 0, halves[0], halves[1]), jnp.where(core == 0, halves[1], halves[0])


def gather_group(halves, n):
    core = lax.axis_index("fsdp") % 2
    if n == 32:
        route = tiled_route(n)
        send = functools.partial(lax.ppermute, axis_name="fsdp")
        mine, theirs = own_half(halves, core)
        got = send(theirs, perm=route["core"])
        first, second = own_half((mine, got), core)
        held = jnp.concatenate([first, second], axis=0)[None]
        for step in ("z2", "z1", "a"):
            held = jnp.concatenate([held, send(held, perm=route[step])], axis=0)
        far = send(held, perm=route["b"])
        return held, far, send(held, perm=route["core"]), send(far, perm=route["core"])
    full = [lax.all_gather(half, "fsdp", axis=0, tiled=True) for half in halves]
    full = [item.reshape(CHIPS, -1, item.shape[1]) for item in full]
    own, other = own_half(full, core)
    middle = CHIPS // 2
    return own[:middle], own[middle:], other[:middle], other[middle:]


def add(left, right):
    return (left.astype(F32) + right.astype(F32)).astype(BF16)


def reduce_group(own, other, n):
    core = lax.axis_index("fsdp") % 2
    if n == 32:
        route = tiled_route(n)
        send = functools.partial(lax.ppermute, axis_name="fsdp")
        got = send(other, perm=route["core"])
        keep = own
        for step in ("b", "a", "z1", "z2"):
            middle = keep.shape[0] // 2
            away = add(keep[middle:], got[middle:])
            keep = add(keep[:middle], got[:middle])
            got = send(away, perm=route[step])
        total = keep[0].astype(F32) + got[0].astype(F32)
        rows = total.shape[0] // 2
        mine, theirs = own_half((total[:rows], total[rows:]), core)
        got = send(theirs.astype(BF16), perm=route["core"]).astype(F32)
        return own_half((mine, got), core)
    first, second = own_half((own, other), core)
    sums = []
    for item in (first, second):
        item = item.reshape(-1, item.shape[2])
        sums.append(lax.psum_scatter(item, "fsdp", scatter_dimension=0, tiled=True).astype(F32))
    return sums


def exchange_all(items):
    return lax.all_to_all(items, "fsdp", 0, 0, tiled=True)


def sinusoid(steps):
    half = TDIM // 2
    freqs = jnp.exp(-math.log(10000.0) * jnp.arange(half, dtype=F32) / half)
    angles = steps.astype(F32)[:, None] * freqs[None, :]
    return jnp.concatenate([jnp.cos(angles), jnp.sin(angles)], axis=1)


def small_rows(n):
    used = TDIM * D // n // D + 1
    return used + (-used % 8)


def body(
    inputs, cotangent, lengths, timesteps, time_weight, time_bias, query_weight, query_bias, key_weight,
    value_weight, value_bias, out_weight, out_bias, mid_gain, mid_shift, up_weight, up_bias, down_weight,
    down_bias, last_gain, last_shift,
):
    n = lax.axis_size("fsdp")
    rows = inputs.shape[0]
    blocks = rows // BLOCK
    tbl = tables(n)
    shard = D // n

    vectors = [query_bias, value_bias, out_bias, mid_gain, mid_shift, down_bias, last_gain, last_shift, time_bias, up_bias]
    flat = jnp.concatenate(vectors)
    time_rows = TDIM * shard // D
    small = jnp.concatenate([time_weight.reshape(-1), flat])
    small = jnp.pad(small, (0, small_rows(n) * D - small.shape[0])).reshape(1, small_rows(n), D)
    small = exchange_all(jnp.broadcast_to(small, (n,) + small.shape[1:]))
    time_full = small[:, :time_rows].reshape(n, TDIM, shard).transpose(1, 0, 2).reshape(TDIM, D)
    gathered = small.reshape(n, -1)[:, TDIM * shard : TDIM * shard + flat.shape[0]].astype(F32)
    vec = gathered[:, : 8 * shard].reshape(n, 8, shard).transpose(1, 0, 2).reshape(8, D)
    time_offset = gathered[:, 8 * shard : 9 * shard].reshape(1, D)
    up_offset = gathered[:, 9 * shard :].reshape(1, FF)
    first_group = [
        jnp.concatenate([w[:, HALF * h : HALF * h + HALF] for w in (query_weight, key_weight, value_weight, out_weight)], axis=1)
        for h in range(2)
    ]
    attn_pieces = gather_group(first_group, n)
    up_pieces = gather_group([up_weight[:, : FF // 2], up_weight[:, FF // 2 :]], n)
    down_pieces = gather_group([down_weight[:, :HALF], down_weight[:, HALF:]], n)

    ends = jnp.cumsum(lengths, axis=1)
    position = jnp.arange(BLOCK, dtype=jnp.int32)
    owner = jnp.sum((position[None, :, None] >= ends[:, None, :]).astype(jnp.int32), axis=2)
    pick = (owner[:, :, None] == jnp.arange(SLOTS, dtype=jnp.int32)).astype(F32)
    pick_all = (pick[:, :, None, :] * jnp.eye(blocks, dtype=F32)[:, None, :, None]).reshape(rows, blocks * SLOTS)
    pick = pick.reshape(rows, SLOTS)
    segc = owner.reshape(rows, 1)
    segr = owner.reshape(blocks, 1, BLOCK)
    embed_in = sinusoid(timesteps.reshape(-1)).astype(BF16)
    slot_embed = nn(embed_in, time_full) + time_offset

    low, qkv, mix, n1, i1, weight = attention_forward(tbl, inputs, pick, slot_embed, segc, segr, vec, attn_pieces)
    res, act, dexp, mlow, din, df, ain, ff_vecs, up_vec = feed_forward(
        tbl, n1, i1, cotangent, vec, up_offset, up_pieces, down_pieces
    )
    down_own, down_other = down_grad(tbl, act, din)
    up_own, up_other = up_grad(tbl, mlow, dexp, mix, ain)
    dqkv, qkv_own, qkv_other, attn_vecs = attention_backward(tbl, ain, mix, qkv, segc, segr, weight, low)
    input_grad, slot_sum = input_gradient(df, dqkv, weight, pick_all)

    down_sum = reduce_group(down_own, down_other, n)
    up_sum = reduce_group(up_own, up_other, n)
    qkv_sum = reduce_group(qkv_own, qkv_other, n)

    slot_low = slot_sum.astype(BF16)
    grad_time = tn(embed_in, slot_low)
    shift_time = jnp.sum(slot_low.astype(F32), axis=0, keepdims=True)
    nine = jnp.concatenate([shift_time, attn_vecs[:2], ff_vecs[:6]], axis=0)
    nine = nine.reshape(9, n, shard).transpose(1, 0, 2).reshape(n, 9 * shard)
    timed = grad_time.reshape(TDIM, n, shard).transpose(1, 0, 2).reshape(n, TDIM * shard)
    small = jnp.concatenate([timed, nine, up_vec.reshape(n, FF // n)], axis=1)
    small = jnp.pad(small, ((0, 0), (0, small_rows(n) * D - small.shape[1]))).astype(BF16)
    small = exchange_all(small.reshape(n, small_rows(n), D))
    small = jnp.sum(small.astype(F32), axis=0).reshape(-1)
    out_time = small[: TDIM * shard].reshape(TDIM, shard)
    at = TDIM * shard
    v = [small[at + shard * i : at + shard * (i + 1)] for i in range(9)]
    v_up = small[at + 9 * shard : at + 9 * shard + FF // n]

    def both(pair, start, stop):
        return jnp.concatenate([half[:, start:stop] for half in pair], axis=1)

    out_query = both(qkv_sum, 0, HALF)
    out_key = both(qkv_sum, HALF, 2 * HALF)
    out_value = both(qkv_sum, 2 * HALF, QKV)
    out_up = both(up_sum, 0, 2 * D)
    out_out = both(up_sum, 2 * D, 2 * D + HALF)
    out_down = both(down_sum, 0, HALF)
    return (
        res, input_grad, out_time, out_query, out_key, out_value, out_out, out_up, out_down,
        v[0], v[1], v[2], v[8], v[6], v[7], v_up, v[5], v[3], v[4],
    )


def solution(mesh):
    row, col, vec = P("fsdp", None), P(None, "fsdp"), P("fsdp")
    in_specs = (
        row, row, row, row, col, vec, row, vec, row, row, vec, row, vec, vec, vec, row, vec, row, vec, vec, vec,
    )
    out_specs = (row, row, col, row, row, row, row, row, row) + (vec,) * 10
    return jax.shard_map(body, mesh=mesh, in_specs=in_specs, out_specs=out_specs, check_vma=False)
```

```python
import functools
import math

import jax
import jax.numpy as jnp
from jax import lax
from jax.experimental import pallas as pl
from jax.experimental.pallas import tpu as pltpu
from jax.sharding import PartitionSpec as P

D = 768
HEAD = 64
HEADS = 12
FF = 3072
TDIM = 128
SLOTS = 8
BLOCK = 512
HALF = D // 2
QKV = 3 * HALF
CHIPS = 16
EPS = 1e-05
NEG = -1e30
HIGH = lax.Precision.HIGHEST
SQRT_HALF = 0.7071067811865476
INV_ROOT_TAU = 0.3989422804014327
WINDOWS = (0, 64, 192, 256)
F32 = jnp.float32
BF16 = jnp.bfloat16
ANY = pl.BlockSpec(memory_space=pl.ANY)
OWN_ROW, OTHER_ROW, OWN_POS, OTHER_POS, CORE_AT = 0, 16, 32, 48, 64


def nn(left, right):
    return lax.dot_general(left, right, (((1,), (0,)), ((), ())), preferred_element_type=F32)


def nt(left, right):
    return lax.dot_general(left, right, (((1,), (1,)), ((), ())), preferred_element_type=F32)


def tn(left, right):
    return lax.dot_general(left, right, (((0,), (0,)), ((), ())), preferred_element_type=F32)


def mean(values):
    return jnp.sum(values, axis=-1, keepdims=True) * (1.0 / D)


def normalize(values):
    center = values - mean(values)
    inverse = lax.rsqrt(mean(center * center) + EPS)
    return center * inverse, inverse


def norm_back(grad, normed, inverse):
    return inverse * (grad - mean(grad) - normed * mean(grad * normed))


def column_sum(values):
    return jnp.sum(values, axis=0, keepdims=True)


def piece_copies(tbl, refs, weight, sems, rows, parts):
    own_low, own_high, other_low, other_high = refs
    core = tbl[CORE_AT]
    copies = []
    for kind, (low, high) in enumerate(((own_low, own_high), (other_low, other_high))):
        half = core if kind == 0 else 1 - core
        for j in range(CHIPS):
            piece = (low if j < CHIPS // 2 else high).at[j % (CHIPS // 2)]
            at = pl.ds(pl.multiple_of(tbl[kind * CHIPS + j] * rows, rows), rows)
            for k, (start, width, base) in enumerate(parts):
                cols = pl.ds(pl.multiple_of(base + half * width, 128), width)
                copies.append(
                    pltpu.make_async_copy(piece.at[:, pl.ds(start, width)], weight.at[at, cols], sems.at[k, kind * CHIPS + j])
                )
    return copies


def lane_masks():
    lane = lax.broadcasted_iota(jnp.int32, (1, 2 * HEAD), 1)
    first = jnp.where(lane < HEAD, 1.0, 0.0)
    return first.astype(BF16), (1.0 - first).astype(BF16), lane < HEAD


def split_bf16(values):
    high = values.astype(BF16)
    rest = values - high.astype(F32)
    return high, rest.astype(BF16), rest


def project_kernel(
    tbl, x_ref, pick_ref, embed_ref, own_low, own_high, other_low, other_high,
    hidden_ref, low_ref, qkv_ref, vec_ref, w_ref, weight, sems, out_sem,
):
    step = pl.program_id(0)
    save = pltpu.make_async_copy(weight.at[:, pl.ds(0, 2 * QKV)], w_ref, out_sem.at[0])

    @pl.when(step == 0)
    def _():
        parts = ((0, QKV, 0), (QKV, TDIM, 2 * QKV))
        copies = piece_copies(tbl, (own_low, own_high, other_low, other_high), weight, sems, 48, parts)
        for copy in copies:
            copy.start()
        for copy in copies:
            copy.wait()
        save.start()
        vec_ref[...] = weight[:, 2 * QKV + TDIM :].astype(F32).T[:16, :]

    slots = nt(embed_ref[...], weight[:, 2 * QKV : 2 * QKV + TDIM]) + vec_ref[8:9, :]
    high, middle, rest = split_bf16(slots)
    low = (rest - middle.astype(F32)).astype(BF16)
    picks = pick_ref[...]
    slot = nn(jnp.concatenate([picks, picks, picks], axis=1), jnp.concatenate([high, middle, low], axis=0))
    hidden_ref[...] = x_ref[...].astype(F32) + slot
    low_ref[...] = hidden_ref[...].astype(BF16)

    def place(y, run):
        half, kind = divmod(run, 3)
        cols = slice(HALF * half, HALF * half + HALF)
        if kind == 0:
            y = (y + vec_ref[0:1, cols]).astype(BF16) * jnp.asarray(HEAD**-0.5, BF16)
        elif kind == 2:
            y = y + vec_ref[1:2, cols]
        qkv_ref[:, HALF * run : HALF * run + HALF] = y.astype(BF16)

    for chunk in range(3):
        y = nn(low_ref[...], weight[:, D * chunk : D * chunk + D])
        place(y[:, :HALF], 2 * chunk)
        place(y[:, HALF:], 2 * chunk + 1)

    @pl.when(step == pl.num_programs(0) - 1)
    def _():
        save.wait()


def attend_kernel(qkv_ref, segc_ref, segr_ref, *rest):
    mix_ref, probs_ref, bias, scores = rest[-4:]
    for t in range(4):
        same = segc_ref[WINDOWS[t] : WINDOWS[t] + 256, :] == segr_ref[0, :, 128 * t : 128 * t + 128]
        bias[t] = jnp.where(same, 0.0, NEG)
    first, second, _ = lane_masks()

    def operands(p, t):
        at = pl.multiple_of((p // 3) * QKV + (p % 3) * 128, 128)
        window = slice(WINDOWS[t], WINDOWS[t] + 256)
        return at, window

    def scores_of(p, t):
        at, window = operands(p, t)
        q = qkv_ref[128 * t : 128 * t + 128, pl.ds(at, 128)]
        k = qkv_ref[window, pl.ds(at + HALF, 128)]
        s = nt(k, jnp.concatenate([q * first, q * second], axis=0)) + jnp.concatenate([bias[t], bias[t]], axis=1)
        scores[t % 2] = s
        return jnp.max(s, axis=0, keepdims=True)

    def pair(p, peak):
        for t in range(4):
            ahead = scores_of(p, t + 1) if t < 3 else scores_of(jnp.minimum(p + 1, HEADS // 2 - 1), 0)
            at, window = operands(p, t)
            v = qkv_ref[window, pl.ds(at + 2 * HALF, 128)]
            e = jnp.exp(scores[t % 2] - peak)
            probs = (e * (1.0 / jnp.sum(e, axis=0, keepdims=True))).astype(BF16)
            probs_ref[0, p, t] = probs
            out = tn(v, probs)
            out = jnp.concatenate([out[:HEAD, :128], out[HEAD:, 128:]], axis=0)
            mix_ref[128 * t : 128 * t + 128, pl.ds(pl.multiple_of(p * 128, 128), 128)] = out.T.astype(BF16)
            peak = ahead
        return peak

    lax.fori_loop(0, HEADS // 2, pair, scores_of(0, 0))

def expand_kernel(
    tbl, hidden_ref, mix_ref, vec_ref, upb_ref, ua, ub, uc, ud,
    n1_ref, i1_ref, act_ref, slope_ref, mlow_ref, up_ref, up, wide, sems, out_sem,
):
    step = pl.program_id(0)
    save = pltpu.make_async_copy(up, up_ref, out_sem.at[0])

    @pl.when(step == 0)
    def _():
        copies = piece_copies(tbl, (ua, ub, uc, ud), up, sems, 48, ((0, FF // 2, 0), (FF // 2, HALF, FF)))
        for copy in copies:
            copy.start()
        for copy in copies:
            copy.wait()
        save.start()

    normed, inverse = normalize(hidden_ref[...] + nn(mix_ref[...], up[:, FF:]) + vec_ref[2:3, :])
    n1_ref[...] = normed
    i1_ref[...] = inverse
    mlow_ref[...] = (normed * vec_ref[3:4, :] + vec_ref[4:5, :]).astype(BF16)

    def expand(j):
        at = slice(j * D, j * D + D)
        wide[j % 2] = nn(mlow_ref[...], up[:, at]) + upb_ref[:, at]

    def activate(j):
        at = slice(j * D, j * D + D)
        u = wide[j % 2]
        scaled = u * SQRT_HALF
        twice = 1.0 + lax.erf(scaled)
        act_ref[:, at] = ((u * 0.5) * twice).astype(BF16)
        slope_ref[:, at] = (0.5 * twice + (u * INV_ROOT_TAU) * jnp.exp(-(scaled * scaled))).astype(BF16)

    expand(0)
    for j in range(FF // D):
        if j + 1 < FF // D:
            expand(j + 1)
        activate(j)

    @pl.when(step == pl.num_programs(0) - 1)
    def _():
        save.wait()


def contract_kernel(
    tbl, n1_ref, i1_ref, cot_ref, vec_ref, act_ref, slope_ref, up_ref, pick_ref, da, db, dc, dd,
    res_ref, dexp_ref, din_ref, df_ref, ain_ref, vg_ref, gup_ref, slot_ref, down, wide, sems,
):
    step = pl.program_id(0)

    @pl.when(step == 0)
    def _():
        copies = piece_copies(tbl, (da, db, dc, dd), down, sems, FF // CHIPS, ((0, HALF, 0),))
        for copy in copies:
            copy.start()
        for copy in copies:
            copy.wait()
        vg_ref[...] = jnp.zeros_like(vg_ref)
        gup_ref[...] = jnp.zeros_like(gup_ref)
        slot_ref[...] = jnp.zeros_like(slot_ref)

    def vec(i):
        return vec_ref[i : i + 1, :]

    second = n1_ref[...] * vec(3) + vec(4) + nn(act_ref[...], down[...]) + vec(5)
    normed2, inverse2 = normalize(second)
    res_ref[...] = (normed2 * vec(6) + vec(7)).astype(BF16)
    upstream = cot_ref[...].astype(F32)
    vg_ref[0:1, :] += column_sum(upstream * normed2)
    vg_ref[1:2, :] += column_sum(upstream)
    d_second = norm_back(upstream * vec(6), normed2, inverse2)
    down_in = d_second.astype(BF16)
    din_ref[...] = down_in
    vg_ref[2:3, :] += column_sum(down_in.astype(F32))

    def contract(j):
        wide[j % 2] = nt(din_ref[...], down[j * D : j * D + D, :])

    contract(0)
    for j in range(FF // D):
        if j + 1 < FF // D:
            contract(j + 1)
        at = slice(j * D, j * D + D)
        d_exp = (wide[j % 2] * slope_ref[:, at].astype(F32)).astype(BF16)
        dexp_ref[:, at] = d_exp
        gup_ref[:, at] += column_sum(d_exp.astype(F32))
    d_middle = nt(dexp_ref[...], up_ref[...]) + d_second
    normed1 = n1_ref[...]
    vg_ref[3:4, :] += column_sum(d_middle * normed1)
    vg_ref[4:5, :] += column_sum(d_middle)
    d_first = norm_back(d_middle * vec(3), normed1, i1_ref[...])
    df_ref[...] = d_first
    attn_in = d_first.astype(BF16)
    ain_ref[...] = attn_in
    vg_ref[5:6, :] += column_sum(attn_in.astype(F32))
    rest = (d_first - attn_in.astype(F32)).astype(BF16)
    slot_ref[...] += tn(pick_ref[...], attn_in) + tn(pick_ref[...], rest)


def down_grad_kernel(tbl, act_ref, din_ref, own, other, hold, sems):
    step = pl.program_id(0)
    core = tbl[CORE_AT]
    rows = FF // CHIPS
    hold[step] = tn(act_ref[...], din_ref[...]).astype(BF16)

    def copies(j):
        made = []
        for k in range(4):
            chip = 4 * j + k
            for kind, (target, table) in enumerate(((own, OWN_POS), (other, OTHER_POS))):
                half = core if kind == 0 else 1 - core
                src = hold.at[j, pl.ds(k * rows, rows), pl.ds(pl.multiple_of(half * HALF, HALF), HALF)]
                made.append(pltpu.make_async_copy(src, target.at[tbl[table + chip]], sems.at[j, 2 * k + kind]))
        return made

    for copy in copies(step):
        copy.start()

    @pl.when(step == pl.num_programs(0) - 1)
    def _():
        for j in range(4):
            for copy in copies(j):
                copy.wait()


def product_for(step, mlow_ref, dexp_ref, mix_ref, ain_ref, give):
    @pl.when(step < 2)
    def _():
        give(tn(mlow_ref[...], dexp_ref[...]), pl.ds(pl.multiple_of(step * D, D), D), D)

    @pl.when(step == 2)
    def _():
        give(tn(mix_ref[...], ain_ref[...]), pl.ds(2 * D, HALF), HALF)


def up_other_kernel(tbl, mlow_ref, dexp_ref, mix_ref, ain_ref, other, hold, sems):
    step = pl.program_id(0)

    def copies(j, width):
        made = []
        for chip in range(CHIPS):
            src = hold.at[j, pl.ds(48 * chip, 48), pl.ds(0, width)]
            cols = pl.ds(pl.multiple_of(j * D, D), width)
            made.append(pltpu.make_async_copy(src, other.at[tbl[OTHER_POS + chip], :, cols], sems.at[j, chip]))
        return made

    def give(grad, cols, width):
        hold[step, :, :width] = grad.astype(BF16)
        for copy in copies(step, width):
            copy.start()

    product_for(step, mlow_ref, dexp_ref, mix_ref, ain_ref, give)

    @pl.when(step == 2)
    def _():
        for j in range(3):
            for copy in copies(j, D if j < 2 else HALF):
                copy.wait()


def arrivals(tbl, got, came, rows, sems):
    made = []
    for chip in range(CHIPS):
        dst = came.at[pl.ds(rows * chip, rows), :]
        made.append(pltpu.make_async_copy(got.at[tbl[OWN_POS + chip]], dst, sems.at[chip]))
    return made


def leave(tbl, src, chip, keep, away, cols, sem, act):
    at = tbl[OWN_POS + chip]

    @pl.when(at < CHIPS // 2)
    def _():
        act(pltpu.make_async_copy(src, keep.at[at, :, cols], sem))

    @pl.when(at >= CHIPS // 2)
    def _():
        act(pltpu.make_async_copy(src, away.at[at - CHIPS // 2, :, cols], sem))


def start(copy):
    copy.start()


def wait(copy):
    copy.wait()


def up_own_kernel(tbl, mlow_ref, dexp_ref, mix_ref, ain_ref, got, keep, away, hold, came, sems, came_sems):
    step = pl.program_id(0)

    @pl.when(step == 0)
    def _():
        for copy in arrivals(tbl, got, came, 48, came_sems):
            copy.start()

    def each(j, width, act):
        for chip in range(CHIPS):
            src = hold.at[j, pl.ds(48 * chip, 48), pl.ds(0, width)]
            leave(tbl, src, chip, keep, away, pl.ds(pl.multiple_of(j * D, D), width), sems.at[j, chip], act)

    def give(grad, cols, width):
        hold[step, :, :width] = (grad + came[:, cols].astype(F32)).astype(BF16)
        each(step, width, start)

    @pl.when(step == 0)
    def _():
        for copy in arrivals(tbl, got, came, 48, came_sems):
            copy.wait()

    product_for(step, mlow_ref, dexp_ref, mix_ref, ain_ref, give)

    @pl.when(step == 2)
    def _():
        for j in range(3):
            each(j, D if j < 2 else HALF, wait)


def attention_backward_kernel(ain_ref, mix_ref, qkv_ref, probs_ref, w_ref, pick_ref, *rest):
    dqkv_ref, vg_ref, slot_ref, d_mix, delta, d_probs, dk, dv = rest[-8:]
    d_mix[...] = nt(ain_ref[...], w_ref[...]).astype(BF16)
    product = d_mix[...].astype(F32) * mix_ref[...].astype(F32)
    high, low, _ = split_bf16(product)
    head = lax.broadcasted_iota(jnp.int32, (16, D), 0)
    column = lax.broadcasted_iota(jnp.int32, (16, D), 1)
    ones = jnp.where(column // HEAD == head, 1.0, 0.0).astype(BF16)
    dots = nt(ones, high) + nt(ones, low)
    for p in range(HEADS // 2):
        for t in range(4):
            rows = slice(128 * t, 128 * t + 128)
            delta[p, t] = jnp.concatenate([dots[2 * p : 2 * p + 1, rows], dots[2 * p + 1 : 2 * p + 2, rows]], axis=1)
    first, second, choose = lane_masks()

    def offsets(p):
        return pl.multiple_of((p // 3) * QKV + (p % 3) * 128, 128)

    def outs_of(p, t):
        do = d_mix[128 * t : 128 * t + 128, pl.ds(pl.multiple_of(p * 128, 128), 128)]
        return jnp.concatenate([do * first, do * second], axis=0)

    def d_probs_of(p, t):
        v = qkv_ref[WINDOWS[t] : WINDOWS[t] + 256, pl.ds(offsets(p) + 2 * HALF, 128)]
        d_probs[t % 2] = nt(v, outs_of(p, t))

    def pair(p, carry):
        at = offsets(p)
        dk[...] = jnp.zeros_like(dk)
        dv[...] = jnp.zeros_like(dv)
        for t in range(4):
            if t < 3:
                d_probs_of(p, t + 1)
            else:
                d_probs_of(jnp.minimum(p + 1, HEADS // 2 - 1), 0)
            window = slice(WINDOWS[t], WINDOWS[t] + 256)
            q = qkv_ref[128 * t : 128 * t + 128, pl.ds(at, 128)]
            k = qkv_ref[window, pl.ds(at + HALF, 128)]
            queries = jnp.concatenate([q * first, q * second], axis=0)
            probs = probs_ref[0, p, t]
            dv[window, :] += nn(probs, outs_of(p, t))
            scores = (probs.astype(F32) * (d_probs[t % 2] - delta[p, t])).astype(BF16)
            dk[window, :] += nn(scores, queries)
            dq = tn(scores, k) * HEAD**-0.5
            dqkv_ref[128 * t : 128 * t + 128, pl.ds(at, 128)] = jnp.where(choose, dq[:128], dq[128:]).astype(BF16)
        dqkv_ref[:, pl.ds(at + HALF, 128)] = dk[...].astype(BF16)
        dqkv_ref[:, pl.ds(at + 2 * HALF, 128)] = dv[...].astype(BF16)
        return carry

    d_probs_of(0, 0)
    lax.fori_loop(0, HEADS // 2, pair, 0)
    for h in range(2):
        cols = slice(HALF * h, HALF * h + HALF)
        for row, shift in ((0, 0), (1, 2 * HALF)):
            part = dqkv_ref[:, QKV * h + shift : QKV * h + shift + HALF]
            vg_ref[row : row + 1, cols] = column_sum(part.astype(F32))
    slot_ref[...] = tn(pick_ref[...], dqkv_ref[...])


def small_grads(first_ref, second_ref, w_ref, embed_ref, ff_ref, va_ref, vb_ref, up_ref):
    high, low, _ = split_bf16(second_ref[...])
    slots = first_ref[...] + nt(high, w_ref[...]) + nt(low, w_ref[...])
    slot_low = slots.astype(BF16)
    rows = [column_sum(slot_low.astype(F32)), va_ref[0:2, :] + vb_ref[0:2, :], ff_ref[0:6, :], up_ref[0:4, :]]
    rows.append(jnp.zeros((TDIM - 13, D), F32))
    vectors = jnp.concatenate(rows, axis=0).T
    return jnp.concatenate([tn(slot_low, embed_ref[...]), vectors], axis=1).astype(BF16)


def qkv_other_kernel(
    tbl, low_ref, dqkv_ref, first_ref, second_ref, w_ref, embed_ref, ff_ref, va_ref, vb_ref, up_ref,
    small_ref, other, hold, extra, sems, small_sems,
):
    step = pl.program_id(0)
    off = 1 - tbl[CORE_AT]

    def small_copies():
        made = []
        for chip in range(CHIPS):
            src = extra.at[pl.ds(48 * chip, 48), pl.ds(pl.multiple_of(off * TDIM, TDIM), TDIM)]
            dst = other.at[tbl[OTHER_POS + chip], :, pl.ds(QKV, TDIM)]
            made.append(pltpu.make_async_copy(src, dst, small_sems.at[chip]))
        return made

    @pl.when(step == 0)
    def _():
        small = small_grads(first_ref, second_ref, w_ref, embed_ref, ff_ref, va_ref, vb_ref, up_ref)
        small_ref[...] = small
        extra[...] = small
        for copy in small_copies():
            copy.start()

    hold[step] = tn(low_ref[...], dqkv_ref[...]).astype(BF16)

    def copies(j):
        made = []
        for k in range(CHIPS // 2):
            src = hold.at[j, pl.ds(48 * k, 48), :]
            at = tbl[OTHER_POS + j * (CHIPS // 2) + k]
            made.append(pltpu.make_async_copy(src, other.at[at, :, pl.ds(0, QKV)], sems.at[j, k]))
        return made

    for copy in copies(step):
        copy.start()

    @pl.when(step == 1)
    def _():
        for j in range(2):
            for copy in copies(j):
                copy.wait()
        for copy in small_copies():
            copy.wait()


def qkv_own_kernel(tbl, low_ref, dqkv_ref, small_ref, got, keep, away, hold, came, sems, came_sems):
    step = pl.program_id(0)

    @pl.when(step == 0)
    def _():
        for copy in arrivals(tbl, got, came, 48, came_sems):
            copy.start()
        for copy in arrivals(tbl, got, came, 48, came_sems):
            copy.wait()

    rows = pl.ds(pl.multiple_of(step * HALF, HALF), HALF)
    cols = pl.ds(pl.multiple_of(tbl[CORE_AT] * TDIM, TDIM), TDIM)
    hold[step, :, :QKV] = (tn(low_ref[...], dqkv_ref[...]) + came[rows, :QKV].astype(F32)).astype(BF16)
    hold[step, :, QKV:] = (small_ref[rows, cols].astype(F32) + came[rows, QKV:].astype(F32)).astype(BF16)

    def each(j, act):
        for k in range(CHIPS // 2):
            src = hold.at[j, pl.ds(48 * k, 48), :]
            leave(tbl, src, j * (CHIPS // 2) + k, keep, away, pl.ds(0, QKV + TDIM), sems.at[j, k], act)

    each(step, start)

    @pl.when(step == 1)
    def _():
        for j in range(2):
            each(j, wait)


def input_grad_kernel(df_ref, dqkv_ref, w_ref, ig_ref):
    ig_ref[...] = df_ref[...] + nt(dqkv_ref[...], w_ref[...])


def call(kernel, name, grid, in_specs, out_specs, out_shape, scratch, flops, moved, args, prefetch=1, alias=None):
    return pl.pallas_call(
        kernel,
        name=name,
        grid_spec=pltpu.PrefetchScalarGridSpec(
            num_scalar_prefetch=prefetch, grid=grid, in_specs=in_specs, out_specs=out_specs, scratch_shapes=scratch
        ),
        out_shape=out_shape,
        input_output_aliases=alias or {},
        compiler_params=pltpu.CompilerParams(dimension_semantics=("arbitrary",) * len(grid), vmem_limit_bytes=63 << 20),
        cost_estimate=pl.CostEstimate(flops=flops, bytes_accessed=moved, transcendentals=0),
    )(*args)


def rows_spec(rows, cols):
    return pl.BlockSpec((rows, cols), lambda i, *_: (i, 0))


def whole_spec(shape):
    return pl.BlockSpec(shape, lambda i, *_: (0,) * len(shape))


def cols_spec(rows, cols, top):
    return pl.BlockSpec((rows, cols), lambda i, *_: (0, jnp.minimum(i, top)))


def sds(shape, dtype):
    return jax.ShapeDtypeStruct(shape, dtype)


def block_spec(shape, block):
    return pl.BlockSpec(shape, lambda i, *_: (block,) + (0,) * (len(shape) - 1))


def project(tbl, x, pick, embed, pieces):
    rows = x.shape[0]
    slots = pick.shape[1]
    return call(
        project_kernel, "project", (rows // BLOCK,),
        [rows_spec(BLOCK, D), rows_spec(BLOCK, slots), whole_spec((slots, TDIM))] + [ANY] * 4,
        [rows_spec(BLOCK, D), rows_spec(BLOCK, D), rows_spec(BLOCK, 2 * QKV), whole_spec((16, D)), ANY],
        [sds((rows, D), F32), sds((rows, D), BF16), sds((rows, 2 * QKV), BF16), sds((16, D), F32), sds((D, 2 * QKV), BF16)],
        [pltpu.VMEM((D, 2 * QKV + 2 * TDIM), BF16), pltpu.SemaphoreType.DMA((2, 32)), pltpu.SemaphoreType.DMA((1,))],
        6 * rows * D * D, 20 << 20, (tbl, x, pick, embed, *pieces),
    )


def attend(block, qkv, segc, segr, before):
    rows = qkv.shape[0]
    return call(
        attend_kernel, "attend", (1,),
        [block_spec((BLOCK, 2 * QKV), block), block_spec((BLOCK, 1), block), block_spec((1, 1, BLOCK), block)]
        + [ANY] * len(before),
        [block_spec((BLOCK, D), block), block_spec((1, HEADS // 2, 4, 256, 256), block)],
        [sds((rows, D), BF16), sds((rows // BLOCK, HEADS // 2, 4, 256, 256), BF16)],
        [pltpu.VMEM((4, 256, 128), F32), pltpu.VMEM((2, 256, 256), F32)],
        4 * BLOCK * D * D, 20 << 20, (qkv, segc, segr, *before), prefetch=0,
        alias={3 + i: i for i in range(len(before))},
    )


def expand(tbl, hidden, mix, vec, upb, up):
    rows = mix.shape[0]
    tile = 256
    return call(
        expand_kernel, "expand", (rows // tile,),
        [rows_spec(tile, D), rows_spec(tile, D), whole_spec((16, D)), whole_spec((1, FF))] + [ANY] * 4,
        [rows_spec(tile, D), rows_spec(tile, 1), rows_spec(tile, FF), rows_spec(tile, FF), rows_spec(tile, D), ANY],
        [sds((rows, D), F32), sds((rows, 1), F32), sds((rows, FF), BF16), sds((rows, FF), BF16), sds((rows, D), BF16),
         sds((D, FF + D), BF16)],
        [pltpu.VMEM((D, FF + D), BF16), pltpu.VMEM((2, tile, D), F32), pltpu.SemaphoreType.DMA((2, 32)),
         pltpu.SemaphoreType.DMA((1,))],
        2 * rows * D * (FF + D), 20 << 20, (tbl, hidden, mix, vec, upb, *up),
    )


def contract(tbl, n1, i1, cot, vec, act, slope, up, pick, down):
    rows = n1.shape[0]
    tile = 256
    slots = pick.shape[1]
    return call(
        contract_kernel, "contract", (rows // tile,),
        [rows_spec(tile, D), rows_spec(tile, 1), rows_spec(tile, D), whole_spec((16, D)), rows_spec(tile, FF),
         rows_spec(tile, FF), whole_spec((D, FF)), rows_spec(tile, slots)] + [ANY] * 4,
        [rows_spec(tile, D), rows_spec(tile, FF), rows_spec(tile, D), rows_spec(tile, D), rows_spec(tile, D),
         whole_spec((8, D)), whole_spec((1, FF)), whole_spec((slots, D))],
        [sds((rows, D), BF16), sds((rows, FF), BF16), sds((rows, D), BF16), sds((rows, D), F32), sds((rows, D), BF16),
         sds((8, D), F32), sds((1, FF), F32), sds((slots, D), F32)],
        [pltpu.VMEM((FF, D), BF16), pltpu.VMEM((2, tile, D), F32), pltpu.SemaphoreType.DMA((1, 32))],
        6 * rows * D * FF, 20 << 20, (tbl, n1, i1, cot, vec, act, slope, up, pick, *down),
    )


def down_grad(tbl, act, din):
    rows = act.shape[0]
    shape = sds((CHIPS, FF // CHIPS, HALF), BF16)
    return call(
        down_grad_kernel, "down_grad", (4,), [cols_spec(rows, D, 3), whole_spec((rows, D))], [ANY, ANY], [shape, shape],
        [pltpu.VMEM((4, D, D), BF16), pltpu.SemaphoreType.DMA((4, 8))],
        2 * rows * D * FF, 20 << 20, (tbl, act, din),
    )


def up_specs(rows, kind):
    def half(tbl):
        return jnp.where(kind == 0, tbl[CORE_AT], 1 - tbl[CORE_AT])

    return [whole_spec((rows, D)), pl.BlockSpec((rows, D), lambda i, tbl: (0, 2 * half(tbl) + jnp.minimum(i, 1))),
            whole_spec((rows, D)), pl.BlockSpec((rows, HALF), lambda i, tbl: (0, half(tbl)))]


def up_other(tbl, mlow, dexp, mix, ain):
    rows = mlow.shape[0]
    return call(
        up_other_kernel, "up_other", (3,), up_specs(rows, 1), ANY, sds((CHIPS, 48, 2 * D + HALF), BF16),
        [pltpu.VMEM((3, D, D), BF16), pltpu.SemaphoreType.DMA((3, CHIPS))],
        rows * D * (FF + D), 20 << 20, (tbl, mlow, dexp, mix, ain),
    )


def up_own(tbl, mlow, dexp, mix, ain, got):
    rows = mlow.shape[0]
    shape = sds((CHIPS // 2, 48, 2 * D + HALF), BF16)
    return call(
        up_own_kernel, "up_own", (3,), up_specs(rows, 0) + [ANY], [ANY, ANY], [shape, shape],
        [pltpu.VMEM((3, D, D), BF16), pltpu.VMEM((D, 2 * D + HALF), BF16), pltpu.SemaphoreType.DMA((3, CHIPS)),
         pltpu.SemaphoreType.DMA((CHIPS,))],
        rows * D * (FF + D), 20 << 20, (tbl, mlow, dexp, mix, ain, got),
    )


def qkv_specs(rows, kind):
    def half(tbl):
        return jnp.where(kind == 0, tbl[CORE_AT], 1 - tbl[CORE_AT])

    return [pl.BlockSpec((rows, HALF), lambda i, tbl: (0, i)), pl.BlockSpec((rows, QKV), lambda i, tbl: (0, half(tbl)))]


def qkv_other(tbl, low, dqkv, first, second, weight, embed, ff, va, vb, up):
    rows = low.shape[0]
    slots = first.shape[0]
    return call(
        qkv_other_kernel, "qkv_other", (2,),
        qkv_specs(rows, 1) + [whole_spec((slots, D)), whole_spec((slots, 2 * QKV)), whole_spec((D, 2 * QKV)),
                              whole_spec((slots, TDIM)), whole_spec((8, D)), whole_spec((8, D)), whole_spec((8, D)),
                              whole_spec((4, D))],
        [whole_spec((D, 2 * TDIM)), ANY], [sds((D, 2 * TDIM), BF16), sds((CHIPS, 48, QKV + TDIM), BF16)],
        [pltpu.VMEM((2, HALF, QKV), BF16), pltpu.VMEM((D, 2 * TDIM), BF16), pltpu.SemaphoreType.DMA((2, CHIPS // 2)),
         pltpu.SemaphoreType.DMA((CHIPS,))],
        3 * rows * D * D, 20 << 20, (tbl, low, dqkv, first, second, weight, embed, ff, va, vb, up),
    )


def qkv_own(tbl, low, dqkv, small, got):
    rows = low.shape[0]
    shape = sds((CHIPS // 2, 48, QKV + TDIM), BF16)
    return call(
        qkv_own_kernel, "qkv_own", (2,), qkv_specs(rows, 0) + [whole_spec((D, 2 * TDIM)), ANY], [ANY, ANY], [shape, shape],
        [pltpu.VMEM((2, HALF, QKV + TDIM), BF16), pltpu.VMEM((D, QKV + TDIM), BF16),
         pltpu.SemaphoreType.DMA((2, CHIPS // 2)), pltpu.SemaphoreType.DMA((CHIPS,))],
        3 * rows * D * D, 20 << 20, (tbl, low, dqkv, small, got),
    )


def attention_backward(block, ain, mix, qkv, probs, weight, pick, before):
    rows = ain.shape[0]
    slots = pick.shape[1]
    return call(
        attention_backward_kernel, "attention_backward", (1,),
        [block_spec((BLOCK, D), block), block_spec((BLOCK, D), block), block_spec((BLOCK, 2 * QKV), block),
         block_spec((1, HEADS // 2, 4, 256, 256), block), pl.BlockSpec((D, D), lambda i, *_: (0, 4)),
         block_spec((BLOCK, slots), block)] + [ANY] * len(before),
        [block_spec((BLOCK, 2 * QKV), block), whole_spec((8, D)), whole_spec((slots, 2 * QKV))],
        [sds((rows, 2 * QKV), BF16), sds((8, D), F32), sds((slots, 2 * QKV), F32)],
        [pltpu.VMEM((BLOCK, D), BF16), pltpu.VMEM((HEADS // 2, 4, 1, 256), F32), pltpu.VMEM((2, 256, 256), F32),
         pltpu.VMEM((BLOCK, 128), F32), pltpu.VMEM((BLOCK, 128), F32)],
        4 * BLOCK * D * D, 20 << 20, (ain, mix, qkv, probs, weight, pick, *before), prefetch=0,
        alias={6 + i: i for i in range(len(before))},
    )


def input_gradient(df, dqkv, weight):
    rows = df.shape[0]
    tile = 256
    return call(
        input_grad_kernel, "input_grad", (rows // tile,),
        [rows_spec(tile, D), rows_spec(tile, 2 * QKV), whole_spec((D, 2 * QKV))], rows_spec(tile, D), sds((rows, D), F32), [],
        6 * rows * D * D, 20 << 20, (df, dqkv, weight), prefetch=0,
    )


def flip(n, even_bit, odd_bit):
    return [(i, i ^ (odd_bit if i & 1 else even_bit)) for i in range(n)]


def tiled_route(n):
    return {"core": flip(n, 1, 1), "z2": flip(n, 16, 16), "z1": flip(n, 8, 8), "a": flip(n, 2, 4), "b": flip(n, 4, 2)}


def tables(n):
    me = lax.axis_index("fsdp")
    core = me % 2
    chips = jnp.arange(CHIPS, dtype=jnp.int32)
    if n == 32:
        here = me // 2

        def order(kind):
            low, high = jnp.where(kind == 0, 1, 2), jnp.where(kind == 0, 2, 1)
            bits = (chips & 1) * 8 + ((chips >> 1) & 1) * 4 + ((chips >> 2) & 1) * low + (chips >> 3) * high
            return here ^ bits

        def place(kind):
            diff = here ^ chips
            x, y = diff & 1, (diff >> 1) & 1
            low, high = jnp.where(kind == 0, x, y), jnp.where(kind == 0, y, x)
            return (diff >> 3) + ((diff >> 2) & 1) * 2 + low * 4 + high * 8

        parts = [order(core), order(1 - core), place(core), place(1 - core)]
    else:
        parts = [chips] * 4
    return jnp.concatenate(parts + [jnp.full((16,), core, jnp.int32)]).astype(jnp.int32)


def own_half(halves, core):
    return jnp.where(core == 0, halves[0], halves[1]), jnp.where(core == 0, halves[1], halves[0])


def tie(*values):
    return lax.optimization_barrier(values)


def follow(first, *values):
    return lax.optimization_barrier((first,) + values)[1:]


def send_on(value, step, n):
    return lax.ppermute(value, "fsdp", perm=tiled_route(n)[step])


def chip_shards(halves_of_groups, n):
    core = lax.axis_index("fsdp") % 2
    mine, theirs = own_half(
        [jnp.concatenate([halves[h].reshape(-1, HALF) for halves in halves_of_groups], axis=0) for h in range(2)], core
    )
    got = send_on(theirs, "core", n)
    first, second = own_half((mine, got), core)
    shards, at = [], 0
    for halves in halves_of_groups:
        rows, cols = halves[0].shape
        count = rows * cols // HALF
        parts = [item[at : at + count].reshape(rows, cols) for item in (first, second)]
        shards.append(jnp.concatenate(parts, axis=0)[None])
        at += count
    return shards


def whole_gather(halves, core):
    full = [lax.all_gather(half, "fsdp", axis=0, tiled=True) for half in halves]
    full = [item.reshape(CHIPS, -1, item.shape[1]) for item in full]
    own, other = own_half(full, core)
    middle = CHIPS // 2
    return own[:middle], own[middle:], other[:middle], other[middle:]


def widen(held, step, n):
    return jnp.concatenate([held, send_on(held, step, n)], axis=0)


def add(left, right):
    return (left.astype(F32) + right.astype(F32)).astype(BF16)


def halve(keep, got):
    middle = keep.shape[0] // 2
    return add(keep[:middle], got[:middle]), add(keep[middle:], got[middle:])


def finish(keep, got, n):
    core = lax.axis_index("fsdp") % 2
    total = keep[0].astype(F32) + got[0].astype(F32)
    rows = total.shape[0] // 2
    mine, theirs = own_half((total[:rows], total[rows:]), core)
    got = send_on(theirs.astype(BF16), "core", n).astype(F32)
    return own_half((mine, got), core)


def whole_reduce(own, other, core):
    sums = []
    for item in own_half((own, other), core):
        item = item.reshape(-1, item.shape[2])
        sums.append(lax.psum_scatter(item, "fsdp", scatter_dimension=0, tiled=True).astype(F32))
    return sums


def sinusoid(steps):
    half = TDIM // 2
    freqs = jnp.exp(-math.log(10000.0) * jnp.arange(half, dtype=F32) / half)
    angles = steps.astype(F32)[:, None] * freqs[None, :]
    return jnp.concatenate([jnp.cos(angles), jnp.sin(angles)], axis=1)


def body(
    inputs, cotangent, lengths, timesteps, time_weight, time_bias, query_weight, query_bias, key_weight,
    value_weight, value_bias, out_weight, out_bias, mid_gain, mid_shift, up_weight, up_bias, down_weight,
    down_bias, last_gain, last_shift,
):
    n = lax.axis_size("fsdp")
    rows = inputs.shape[0]
    blocks = rows // BLOCK
    tbl = tables(n)
    shard = D // n

    vectors = [query_bias, value_bias, out_bias, mid_gain, mid_shift, down_bias, last_gain, last_shift, time_bias]
    vectors += [up_bias[shard * k : shard * (k + 1)] for k in range(FF // D)]
    lane = lax.broadcasted_iota(jnp.int32, (shard, TDIM), 1)
    columns = jnp.zeros((shard, TDIM), F32)
    for k, item in enumerate(vectors):
        columns = jnp.where(lane == k, item.astype(F32)[:, None], columns)
    columns = columns.astype(BF16)
    small_halves = [time_weight.T, columns]
    attn_halves = [
        jnp.concatenate(
            [w[:, HALF * h : HALF * h + HALF] for w in (query_weight, key_weight, value_weight)] + [small_halves[h]], axis=1
        )
        for h in range(2)
    ]
    up_halves = [
        jnp.concatenate([up_weight[:, FF // 2 * h : FF // 2 * (h + 1)], out_weight[:, HALF * h : HALF * h + HALF]], axis=1)
        for h in range(2)
    ]
    down_halves = [down_weight[:, :HALF], down_weight[:, HALF:]]

    ends = jnp.cumsum(lengths, axis=1)
    position = jnp.arange(BLOCK, dtype=jnp.int32)
    owner = jnp.sum((position[None, :, None] >= ends[:, None, :]).astype(jnp.int32), axis=2)
    pick = (owner[:, :, None] == jnp.arange(SLOTS, dtype=jnp.int32)).astype(BF16)
    pick = (pick[:, :, None, :] * jnp.eye(blocks, dtype=BF16)[:, None, :, None]).reshape(rows, blocks * SLOTS)
    segc = owner.reshape(rows, 1)
    segr = owner.reshape(blocks, 1, BLOCK)
    embed_in = sinusoid(timesteps.reshape(-1)).astype(BF16)
    core = lax.axis_index("fsdp") % 2
    tiled = n == 32

    if tiled:
        a0, u0, d0 = chip_shards((attn_halves, up_halves, down_halves), n)
        a0 = widen(a0, "z2", n)
        a0 = widen(a0, "z1", n)
        (u0,) = follow(a0, u0)
        a0 = widen(a0, "a", n)
        u0 = widen(u0, "z2", n)
        a0, u0 = tie(a0, u0)
        a1 = send_on(a0, "b", n)
        a2 = send_on(a0, "core", n)
        u0 = widen(u0, "z1", n)
        a1, u0, d0 = tie(a1, u0, d0)
        a3 = send_on(a1, "core", n)
        u_got = send_on(u0, "a", n)
        d_got = send_on(d0, "z2", n)
        hidden, low, qkv, vec, weight = project(tbl, inputs, pick, embed_in, (a0, a1, a2, a3))
        qkv, u0, u_got, d0, d_got = tie(qkv, u0, u_got, d0, d_got)
        u0 = jnp.concatenate([u0, u_got], axis=0)
        d0 = jnp.concatenate([d0, d_got], axis=0)
        u1 = send_on(u0, "b", n)
        d_got = send_on(d0, "z1", n)
        u2 = send_on(u0, "core", n)
        parts = attend(0, qkv, segc, segr, ())
        *parts, qkv, u0, u2, d0, d_got = tie(*parts, qkv, u0, u2, d0, d_got)
        d0 = jnp.concatenate([d0, d_got], axis=0)
        d_got = send_on(d0, "a", n)
        mix, probs = attend(1, qkv, segc, segr, parts)
        mix, u1, d0, d_got = tie(mix, u1, d0, d_got)
        u3 = send_on(u1, "core", n)
        d0 = jnp.concatenate([d0, d_got], axis=0)
        d1 = send_on(d0, "b", n)
        d2 = send_on(d0, "core", n)
        up_offset = vec[9:13].reshape(FF // D, n, shard).transpose(1, 0, 2).reshape(1, FF)
        n1, i1, act, slope, mlow, up_full = expand(tbl, hidden, mix, vec, up_offset, (u0, u1, u2, u3))
        act, d1 = tie(act, d1)
        d3 = send_on(d1, "core", n)
        down_pieces = (d0, d1, d2, d3)
    else:
        hidden, low, qkv, vec, weight = project(tbl, inputs, pick, embed_in, whole_gather(attn_halves, core))
        mix, probs = attend(1, qkv, segc, segr, attend(0, qkv, segc, segr, ()))
        up_offset = vec[9:13].reshape(FF // D, n, shard).transpose(1, 0, 2).reshape(1, FF)
        n1, i1, act, slope, mlow, up_full = expand(tbl, hidden, mix, vec, up_offset, whole_gather(up_halves, core))
        down_pieces = whole_gather(down_halves, core)

    res, dexp, din, df, ain, ff_vecs, up_vec, slot_first = contract(
        tbl, n1, i1, cotangent, vec, act, slope, up_full, pick, down_pieces
    )
    up_vec = up_vec.reshape(n, FF // D, shard).transpose(1, 0, 2).reshape(FF // D, D)
    d_own, d_other = down_grad(tbl, act, din)
    mlow, d_own, d_other = tie(mlow, d_own, d_other)
    u_other = up_other(tbl, mlow, dexp, mix, ain)
    if tiled:
        d_got = send_on(d_other, "core", n)
        u_other, d_own, d_got, mlow = tie(u_other, d_own, d_got, mlow)
        u_got = send_on(u_other, "core", n)
        d_keep, d_away = halve(d_own, d_got)
        d_keep, d_away, u_got = tie(d_keep, d_away, u_got)
        d_got = send_on(d_away, "b", n)
        u_keep, u_away = up_own(tbl, mlow, dexp, mix, ain, u_got)
        ain, u_keep, u_away = tie(ain, u_keep, u_away)
        u_got = send_on(u_away, "b", n)
        dqkv, vg0, slot0 = attention_backward(0, ain, mix, qkv, probs, up_full, pick, ())
        dqkv, d_keep, d_got = tie(dqkv, d_keep, d_got)
        d_keep, d_away = halve(d_keep, d_got)
        ain, dqkv, d_keep, d_away = tie(ain, dqkv, d_keep, d_away)
        d_got = send_on(d_away, "a", n)
        dqkv, vg1, slot1 = attention_backward(1, ain, mix, qkv, probs, up_full, pick, (dqkv,))
        dqkv, d_keep, d_got, u_keep, u_got = tie(dqkv, d_keep, d_got, u_keep, u_got)
        u_keep, u_away = halve(u_keep, u_got)
        d_keep, d_away = halve(d_keep, d_got)
        low, dqkv, d_keep, d_away, u_keep, u_away = tie(low, dqkv, d_keep, d_away, u_keep, u_away)
        u_got = send_on(u_away, "a", n)
        d_got = send_on(d_away, "z1", n)
        small, q_other = qkv_other(
            tbl, low, dqkv, slot_first, slot0 + slot1, weight, embed_in, ff_vecs, vg0, vg1, up_vec
        )
        q_other, u_keep, u_got, d_keep, d_got, low = tie(q_other, u_keep, u_got, d_keep, d_got, low)
        q_got = send_on(q_other, "core", n)
        u_keep, u_away = halve(u_keep, u_got)
        d_keep, d_away = halve(d_keep, d_got)
        q_got, u_keep, u_away, d_keep, d_away = tie(q_got, u_keep, u_away, d_keep, d_away)
        u_got = send_on(u_away, "z1", n)
        q_keep, q_away = qkv_own(tbl, low, dqkv, small, q_got)
        df, q_keep, q_away, u_keep, u_got = tie(df, q_keep, q_away, u_keep, u_got)
        q_got = send_on(q_away, "b", n)
        u_keep, u_away = halve(u_keep, u_got)
        df, d_away, u_keep, u_away = tie(df, d_away, u_keep, u_away)
        d_got = send_on(d_away, "z2", n)
        u_got = send_on(u_away, "z2", n)
        input_grad = input_gradient(df, dqkv, weight)
        input_grad, q_keep, q_got = tie(input_grad, q_keep, q_got)
        q_keep, q_away = halve(q_keep, q_got)
        u_keep, u_got, d_keep, d_got = follow(q_away, u_keep, u_got, d_keep, d_got)
        q_got = send_on(q_away, "a", n)
        down_sum = finish(d_keep, d_got, n)
        q_keep, q_away = halve(q_keep, q_got)
        q_got = send_on(q_away, "z1", n)
        up_sum = finish(u_keep, u_got, n)
        q_keep, q_away = halve(q_keep, q_got)
        q_got = send_on(q_away, "z2", n)
        qkv_sum = finish(q_keep, q_got, n)
    else:
        dqkv, vg0, slot0 = attention_backward(0, ain, mix, qkv, probs, up_full, pick, ())
        dqkv, vg1, slot1 = attention_backward(1, ain, mix, qkv, probs, up_full, pick, (dqkv,))
        small, q_other = qkv_other(
            tbl, low, dqkv, slot_first, slot0 + slot1, weight, embed_in, ff_vecs, vg0, vg1, up_vec
        )
        input_grad = input_gradient(df, dqkv, weight)
        down_sum = whole_reduce(d_own, d_other, core)
        zero_u, zero_q = jnp.zeros_like(u_other), jnp.zeros_like(q_other)
        u_own = jnp.concatenate(up_own(tbl, mlow, dexp, mix, ain, zero_u), axis=0)
        q_own = jnp.concatenate(qkv_own(tbl, low, dqkv, small, zero_q), axis=0)
        up_sum = whole_reduce(u_own, u_other, core)
        qkv_sum = whole_reduce(q_own, q_other, core)
    def both(pair, start, stop):
        return jnp.concatenate([half[:, start:stop] for half in pair], axis=1)

    out_query = both(qkv_sum, 0, HALF)
    out_key = both(qkv_sum, HALF, 2 * HALF)
    out_value = both(qkv_sum, 2 * HALF, QKV)
    out_up = both(up_sum, 0, 2 * D)
    out_out = both(up_sum, 2 * D, 2 * D + HALF)
    out_down = both(down_sum, 0, HALF)
    out_time = qkv_sum[0][:, QKV:].T
    v = qkv_sum[1][:, QKV : QKV + 13].T
    v_up = v[9:13].reshape(-1)
    return (
        res, input_grad, out_time, out_query, out_key, out_value, out_out, out_up, out_down,
        v[0], v[1], v[2], v[8], v[6], v[7], v_up, v[5], v[3], v[4],
    )


def solution(mesh):
    row, col, vec = P("fsdp", None), P(None, "fsdp"), P("fsdp")
    in_specs = (
        row, row, row, row, col, vec, row, vec, row, row, vec, row, vec, vec, vec, row, vec, row, vec, vec, vec,
    )
    out_specs = (row, row, col, row, row, row, row, row, row) + (vec,) * 10
    return jax.shard_map(body, mesh=mesh, in_specs=in_specs, out_specs=out_specs, check_vma=False)
```

```python
import functools
import math

import jax
import jax.numpy as jnp
from jax import lax
from jax.experimental import pallas as pl
from jax.experimental.pallas import tpu as pltpu
from jax.sharding import PartitionSpec as P

D = 768
HEAD = 64
HEADS = 12
FF = 3072
TDIM = 128
SLOTS = 8
BLOCK = 512
HALF = D // 2
QKV = 3 * HALF
CHIPS = 16
EPS = 1e-05
NEG = -1e30
HIGH = lax.Precision.HIGHEST
SQRT_HALF = 0.7071067811865476
INV_ROOT_TAU = 0.3989422804014327
HALF_LOG = -0.5 / math.log(2.0)
WINDOWS = (0, 64, 192, 256)
F32 = jnp.float32
BF16 = jnp.bfloat16
ANY = pl.BlockSpec(memory_space=pl.ANY)
OWN_ROW, OTHER_ROW, OWN_POS, OTHER_POS, CORE_AT = 0, 16, 32, 48, 64


def nn(left, right):
    return lax.dot_general(left, right, (((1,), (0,)), ((), ())), preferred_element_type=F32)


def nt(left, right):
    return lax.dot_general(left, right, (((1,), (1,)), ((), ())), preferred_element_type=F32)


def tn(left, right):
    return lax.dot_general(left, right, (((0,), (0,)), ((), ())), preferred_element_type=F32)


def mean(values):
    return jnp.sum(values, axis=-1, keepdims=True) * (1.0 / D)


def normalize(values):
    center = values - mean(values)
    inverse = lax.rsqrt(mean(center * center) + EPS)
    return center * inverse, inverse


def norm_back(grad, normed, inverse):
    return inverse * (grad - mean(grad) - normed * mean(grad * normed))


def column_sum(values):
    return jnp.sum(values, axis=0, keepdims=True)


def piece_copies(tbl, refs, weight, sems, rows, parts):
    own_low, own_high, other_low, other_high = refs
    core = tbl[CORE_AT]
    copies = []
    for kind, (low, high) in enumerate(((own_low, own_high), (other_low, other_high))):
        half = core if kind == 0 else 1 - core
        for j in range(CHIPS):
            piece = (low if j < CHIPS // 2 else high).at[j % (CHIPS // 2)]
            at = pl.ds(pl.multiple_of(tbl[kind * CHIPS + j] * rows, rows), rows)
            for k, (start, width, base) in enumerate(parts):
                cols = pl.ds(pl.multiple_of(base + half * width, 128), width)
                copies.append(
                    pltpu.make_async_copy(piece.at[:, pl.ds(start, width)], weight.at[at, cols], sems.at[k, kind * CHIPS + j])
                )
    return copies


def lane_masks():
    lane = lax.broadcasted_iota(jnp.int32, (1, 2 * HEAD), 1)
    first = jnp.where(lane < HEAD, 1.0, 0.0)
    return first.astype(BF16), (1.0 - first).astype(BF16), lane < HEAD


def split_bf16(values):
    high = values.astype(BF16)
    rest = values - high.astype(F32)
    return high, rest.astype(BF16), rest


def project_kernel(
    tbl, x_ref, pick_ref, embed_ref, own_low, own_high, other_low, other_high,
    hidden_ref, low_ref, qkv_ref, vec_ref, w_ref, weight, offset, factor, sems, out_sem,
):
    step = pl.program_id(0)
    save = pltpu.make_async_copy(weight.at[:, pl.ds(0, 2 * QKV)], w_ref, out_sem.at[0])

    @pl.when(step == 0)
    def _():
        parts = ((0, QKV, 0), (QKV, TDIM, 2 * QKV))
        copies = piece_copies(tbl, (own_low, own_high, other_low, other_high), weight, sems, 48, parts)
        for copy in copies:
            copy.start()
        for copy in copies:
            copy.wait()
        save.start()
        vec_ref[...] = weight[:, 2 * QKV + TDIM :].astype(F32).T[:16, :]
        offset[...] = jnp.zeros_like(offset)
        factor[...] = jnp.ones_like(factor)
        for half in range(2):
            cols = slice(HALF * half, HALF * half + HALF)
            at = QKV * half
            offset[:, at : at + HALF] = vec_ref[0:1, cols]
            offset[:, at + 2 * HALF : at + QKV] = vec_ref[1:2, cols]
            factor[:, at : at + HALF] = jnp.full((1, HALF), HEAD**-0.5, F32)

    slots = nt(embed_ref[...], weight[:, 2 * QKV : 2 * QKV + TDIM]) + vec_ref[8:9, :]
    high, middle, rest = split_bf16(slots)
    low = (rest - middle.astype(F32)).astype(BF16)
    picks = pick_ref[...]
    slot = nn(jnp.concatenate([picks, picks, picks], axis=1), jnp.concatenate([high, middle, low], axis=0))
    hidden_ref[...] = x_ref[...].astype(F32) + slot
    low_ref[...] = hidden_ref[...].astype(BF16)

    def chunk(j, carry):
        at = pl.ds(pl.multiple_of(j * D, D), D)
        y = nn(low_ref[...], weight[:, at]) + offset[:, at]
        qkv_ref[:, at] = (y.astype(BF16).astype(F32) * factor[:, at]).astype(BF16)
        return carry

    lax.fori_loop(0, 3, chunk, 0)

    @pl.when(step == pl.num_programs(0) - 1)
    def _():
        save.wait()


def attend_kernel(block, qkv_ref, pick_ref, segr_ref, *rest):
    mix_ref, probs_ref, bias, scores, held, sems = rest[-6:]
    slot = lax.broadcasted_iota(jnp.int32, pick_ref.shape, 1).astype(F32)
    owner = jnp.sum(pick_ref[...].astype(F32) * slot, axis=1, keepdims=True)
    for t in range(4):
        same = owner[WINDOWS[t] : WINDOWS[t] + 256, :] == segr_ref[0, :, 128 * t : 128 * t + 128]
        bias[t] = jnp.where(same, 0.0, NEG)
    first, second, _ = lane_masks()

    def operands(p, t):
        at = pl.multiple_of((p // 3) * QKV + (p % 3) * 128, 128)
        window = slice(WINDOWS[t], WINDOWS[t] + 256)
        return at, window

    def scores_of(p, t):
        at, window = operands(p, t)
        q = qkv_ref[128 * t : 128 * t + 128, pl.ds(at, 128)]
        k = qkv_ref[window, pl.ds(at + HALF, 128)]
        s = nt(k, jnp.concatenate([q * first, q * second], axis=0)) + jnp.concatenate([bias[t], bias[t]], axis=1)
        scores[t % 2] = s
        return jnp.max(s, axis=0, keepdims=True)

    def out_copy(p):
        return pltpu.make_async_copy(held.at[p % 2], probs_ref.at[block, p], sems.at[p % 2])

    def pair(p, peak):
        @pl.when(p >= 2)
        def _():
            out_copy(p - 2).wait()

        for t in range(4):
            ahead = scores_of(p, t + 1) if t < 3 else scores_of(jnp.minimum(p + 1, HEADS // 2 - 1), 0)
            at, window = operands(p, t)
            v = qkv_ref[window, pl.ds(at + 2 * HALF, 128)]
            e = jnp.exp(scores[t % 2] - peak)
            probs = (e * (1.0 / jnp.sum(e, axis=0, keepdims=True))).astype(BF16)
            held[p % 2, t] = probs
            out = tn(v, probs)
            out = jnp.concatenate([out[:HEAD, :128], out[HEAD:, 128:]], axis=0)
            mix_ref[128 * t : 128 * t + 128, pl.ds(pl.multiple_of(p * 128, 128), 128)] = out.T.astype(BF16)
            peak = ahead
        out_copy(p).start()
        return peak

    lax.fori_loop(0, HEADS // 2, pair, scores_of(0, 0))
    out_copy(HEADS // 2 - 2).wait()
    out_copy(HEADS // 2 - 1).wait()

def expand_kernel(
    tbl, hidden_ref, mix_ref, vec_ref, upb_ref, ua, ub, uc, ud,
    n1_ref, i1_ref, act_ref, slope_ref, mlow_ref, up_ref, up, wide, sems, out_sem,
):
    step = pl.program_id(0)
    save = pltpu.make_async_copy(up, up_ref, out_sem.at[0])
    both = piece_copies(tbl, (ua, ub, uc, ud), up, sems, 48, ((FF // 2, HALF, FF), (0, FF // 2, 0)))
    copies = both[0::2], both[1::2]

    @pl.when(step == 0)
    def _():
        for copy in copies[0] + copies[1]:
            copy.start()
        for copy in copies[0]:
            copy.wait()

    normed, inverse = normalize(hidden_ref[...] + nn(mix_ref[...], up[:, FF:]) + vec_ref[2:3, :])
    n1_ref[...] = normed
    i1_ref[...] = inverse
    mlow_ref[...] = (normed * vec_ref[3:4, :] + vec_ref[4:5, :]).astype(BF16)

    def expand(j):
        at = slice(j * D, j * D + D)
        wide[j % 2] = nn(mlow_ref[...], up[:, at]) + upb_ref[:, at]

    def activate(j):
        at = slice(j * D, j * D + D)
        u = wide[j % 2]
        scaled = u * SQRT_HALF
        twice = 1.0 + lax.erf(scaled)
        act_ref[:, at] = ((u * 0.5) * twice).astype(BF16)
        slope_ref[:, at] = (0.5 * twice + (u * INV_ROOT_TAU) * jnp.exp2((u * u) * HALF_LOG)).astype(BF16)

    @pl.when(step == 0)
    def _():
        for copy in copies[1]:
            copy.wait()
        save.start()

    expand(0)
    for j in range(FF // D):
        if j + 1 < FF // D:
            expand(j + 1)
        activate(j)

    @pl.when(step == pl.num_programs(0) - 1)
    def _():
        save.wait()


def contract_kernel(
    tbl, n1_ref, i1_ref, cot_ref, vec_ref, act_ref, slope_ref, up_ref, pick_ref, da, db, dc, dd,
    res_ref, dexp_ref, din_ref, df_ref, ain_ref, vg_ref, gup_ref, slot_ref, down, up, wide, sems, up_sem,
):
    step = pl.program_id(0)
    fetch = pltpu.make_async_copy(up_ref.at[:, pl.ds(0, FF)], up, up_sem.at[0])

    @pl.when(step == 0)
    def _():
        copies = piece_copies(tbl, (da, db, dc, dd), down, sems, FF // CHIPS, ((0, HALF, 0),))
        for copy in copies:
            copy.start()
        for copy in copies:
            copy.wait()
        fetch.start()
        vg_ref[...] = jnp.zeros_like(vg_ref)
        gup_ref[...] = jnp.zeros_like(gup_ref)
        slot_ref[...] = jnp.zeros_like(slot_ref)

    def vec(i):
        return vec_ref[i : i + 1, :]

    second = n1_ref[...] * vec(3) + vec(4) + nn(act_ref[...], down[...]) + vec(5)
    normed2, inverse2 = normalize(second)
    res_ref[...] = (normed2 * vec(6) + vec(7)).astype(BF16)
    upstream = cot_ref[...].astype(F32)
    vg_ref[0:1, :] += column_sum(upstream * normed2)
    vg_ref[1:2, :] += column_sum(upstream)
    d_second = norm_back(upstream * vec(6), normed2, inverse2)
    down_in = d_second.astype(BF16)
    din_ref[...] = down_in
    vg_ref[2:3, :] += column_sum(down_in.astype(F32))

    def contract(j):
        wide[j % 2] = nt(din_ref[...], down[j * D : j * D + D, :])

    @pl.when(step == 0)
    def _():
        fetch.wait()

    contract(0)
    for j in range(FF // D):
        if j + 1 < FF // D:
            contract(j + 1)
        at = slice(j * D, j * D + D)
        d_exp = (wide[j % 2] * slope_ref[:, at].astype(F32)).astype(BF16)
        dexp_ref[:, at] = d_exp
        gup_ref[:, at] += column_sum(d_exp.astype(F32))
    d_middle = nt(dexp_ref[...], up[...]) + d_second
    normed1 = n1_ref[...]
    vg_ref[3:4, :] += column_sum(d_middle * normed1)
    vg_ref[4:5, :] += column_sum(d_middle)
    d_first = norm_back(d_middle * vec(3), normed1, i1_ref[...])
    df_ref[...] = d_first
    attn_in = d_first.astype(BF16)
    ain_ref[...] = attn_in
    vg_ref[5:6, :] += column_sum(attn_in.astype(F32))
    rest = (d_first - attn_in.astype(F32)).astype(BF16)
    slot_ref[...] += tn(pick_ref[...], attn_in) + tn(pick_ref[...], rest)


def down_grad_kernel(tbl, act_ref, din_ref, own, other, hold, sems):
    step = pl.program_id(0)
    core = tbl[CORE_AT]
    rows = FF // CHIPS
    hold[step] = tn(act_ref[...], din_ref[...]).astype(BF16)

    def copies(j):
        made = []
        for k in range(4):
            chip = 4 * j + k
            for kind, (target, table) in enumerate(((own, OWN_POS), (other, OTHER_POS))):
                half = core if kind == 0 else 1 - core
                src = hold.at[j, pl.ds(k * rows, rows), pl.ds(pl.multiple_of(half * HALF, HALF), HALF)]
                made.append(pltpu.make_async_copy(src, target.at[tbl[table + chip]], sems.at[j, 2 * k + kind]))
        return made

    for copy in copies(step):
        copy.start()

    @pl.when(step == pl.num_programs(0) - 1)
    def _():
        for j in range(4):
            for copy in copies(j):
                copy.wait()


def product_for(step, mlow_ref, dexp_ref, mix_ref, ain_ref, give):
    @pl.when(step < 2)
    def _():
        give(tn(mlow_ref[...], dexp_ref[...]), pl.ds(pl.multiple_of(step * D, D), D), D)

    @pl.when(step == 2)
    def _():
        give(tn(mix_ref[...], ain_ref[...]), pl.ds(2 * D, HALF), HALF)


def up_other_kernel(tbl, mlow_ref, dexp_ref, mix_ref, ain_ref, other, hold, sems):
    step = pl.program_id(0)

    def copies(j, width):
        made = []
        for chip in range(CHIPS):
            src = hold.at[j, pl.ds(48 * chip, 48), pl.ds(0, width)]
            cols = pl.ds(pl.multiple_of(j * D, D), width)
            made.append(pltpu.make_async_copy(src, other.at[tbl[OTHER_POS + chip], :, cols], sems.at[j, chip]))
        return made

    def give(grad, cols, width):
        hold[step, :, :width] = grad.astype(BF16)
        for copy in copies(step, width):
            copy.start()

    product_for(step, mlow_ref, dexp_ref, mix_ref, ain_ref, give)

    @pl.when(step == 2)
    def _():
        for j in range(3):
            for copy in copies(j, D if j < 2 else HALF):
                copy.wait()


def arrivals(tbl, got, came, rows, sems):
    made = []
    for chip in range(CHIPS):
        dst = came.at[pl.ds(rows * chip, rows), :]
        made.append(pltpu.make_async_copy(got.at[tbl[OWN_POS + chip]], dst, sems.at[chip]))
    return made


def leave(tbl, src, first, count, keep, away, cols):
    def one(k, carry):
        at = tbl[OWN_POS + first + k]
        rows = src[pl.ds(pl.multiple_of(48 * k, 48), 48), :]

        @pl.when(at < CHIPS // 2)
        def _():
            keep[at, :, cols] = rows

        @pl.when(at >= CHIPS // 2)
        def _():
            away[at - CHIPS // 2, :, cols] = rows

        return carry

    lax.fori_loop(0, count, one, 0)


def up_own_kernel(tbl, mlow_ref, dexp_ref, mix_ref, ain_ref, got, keep, away, hold, came, came_sems):
    step = pl.program_id(0)

    @pl.when(step == 0)
    def _():
        for copy in arrivals(tbl, got, came, 48, came_sems):
            copy.start()
        for copy in arrivals(tbl, got, came, 48, came_sems):
            copy.wait()

    def give(grad, cols, width):
        hold[:, :width] = (grad + came[:, cols].astype(F32)).astype(BF16)
        leave(tbl, hold.at[:, pl.ds(0, width)], 0, CHIPS, keep, away, cols)

    product_for(step, mlow_ref, dexp_ref, mix_ref, ain_ref, give)


def attention_backward_kernel(ain_ref, mix_ref, qkv_ref, probs_ref, w_ref, pick_ref, *rest):
    dqkv_ref, vg_ref, slot_ref, d_mix, delta, d_probs, dk, dv = rest[-8:]
    d_mix[...] = nt(ain_ref[...], w_ref[...]).astype(BF16)
    product = d_mix[...].astype(F32) * mix_ref[...].astype(F32)
    high, low, _ = split_bf16(product)
    head = lax.broadcasted_iota(jnp.int32, (16, D), 0)
    column = lax.broadcasted_iota(jnp.int32, (16, D), 1)
    ones = jnp.where(column // HEAD == head, 1.0, 0.0).astype(BF16)
    dots = nt(ones, high) + nt(ones, low)
    for p in range(HEADS // 2):
        for t in range(4):
            rows = slice(128 * t, 128 * t + 128)
            delta[p, t] = jnp.concatenate([dots[2 * p : 2 * p + 1, rows], dots[2 * p + 1 : 2 * p + 2, rows]], axis=1)
    first, second, choose = lane_masks()

    def offsets(p):
        return pl.multiple_of((p // 3) * QKV + (p % 3) * 128, 128)

    def outs_of(p, t):
        do = d_mix[128 * t : 128 * t + 128, pl.ds(pl.multiple_of(p * 128, 128), 128)]
        return jnp.concatenate([do * first, do * second], axis=0)

    def d_probs_of(p, t):
        v = qkv_ref[WINDOWS[t] : WINDOWS[t] + 256, pl.ds(offsets(p) + 2 * HALF, 128)]
        d_probs[t % 2] = nt(v, outs_of(p, t))

    def pair(p, carry):
        at = offsets(p)
        dk[...] = jnp.zeros_like(dk)
        dv[...] = jnp.zeros_like(dv)
        for t in range(4):
            if t < 3:
                d_probs_of(p, t + 1)
            else:
                d_probs_of(jnp.minimum(p + 1, HEADS // 2 - 1), 0)
            window = slice(WINDOWS[t], WINDOWS[t] + 256)
            q = qkv_ref[128 * t : 128 * t + 128, pl.ds(at, 128)]
            k = qkv_ref[window, pl.ds(at + HALF, 128)]
            queries = jnp.concatenate([q * first, q * second], axis=0)
            probs = probs_ref[0, p, t]
            dv[window, :] += nn(probs, outs_of(p, t))
            scores = (probs.astype(F32) * (d_probs[t % 2] - delta[p, t])).astype(BF16)
            dk[window, :] += nn(scores, queries)
            dq = tn(scores, k) * HEAD**-0.5
            dqkv_ref[128 * t : 128 * t + 128, pl.ds(at, 128)] = jnp.where(choose, dq[:128], dq[128:]).astype(BF16)
        dqkv_ref[:, pl.ds(at + HALF, 128)] = dk[...].astype(BF16)
        dqkv_ref[:, pl.ds(at + 2 * HALF, 128)] = dv[...].astype(BF16)
        return carry

    d_probs_of(0, 0)
    lax.fori_loop(0, HEADS // 2, pair, 0)
    for h in range(2):
        cols = slice(HALF * h, HALF * h + HALF)
        for row, shift in ((0, 0), (1, 2 * HALF)):
            part = dqkv_ref[:, QKV * h + shift : QKV * h + shift + HALF]
            vg_ref[row : row + 1, cols] = column_sum(part.astype(F32))
    slot_ref[...] = tn(pick_ref[...], dqkv_ref[...])


def small_grads(first_ref, sa_ref, sb_ref, w_ref, embed_ref, ff_ref, va_ref, vb_ref, up_ref):
    high, low, _ = split_bf16(sa_ref[...] + sb_ref[...])
    both = nt(jnp.concatenate([high, low], axis=0), w_ref[...])
    slots = first_ref[...] + both[: high.shape[0]] + both[high.shape[0] :]
    slot_low = slots.astype(BF16)
    rows = [column_sum(slot_low.astype(F32)), va_ref[0:2, :] + vb_ref[0:2, :], ff_ref[0:6, :], up_ref[0:4, :]]
    rows.append(jnp.zeros((TDIM - 13, D), F32))
    vectors = jnp.concatenate(rows, axis=0).T
    return jnp.concatenate([tn(slot_low, embed_ref[...]), vectors], axis=1).astype(BF16)


def qkv_other_kernel(
    tbl, low_ref, dqkv_ref, first_ref, sa_ref, sb_ref, w_ref, embed_ref, ff_ref, va_ref, vb_ref, up_ref,
    small_ref, other, hold, extra, sems, small_sems,
):
    step = pl.program_id(0)
    off = 1 - tbl[CORE_AT]

    def small_copies():
        made = []
        for chip in range(CHIPS):
            src = extra.at[pl.ds(48 * chip, 48), pl.ds(pl.multiple_of(off * TDIM, TDIM), TDIM)]
            dst = other.at[tbl[OTHER_POS + chip], :, pl.ds(QKV, TDIM)]
            made.append(pltpu.make_async_copy(src, dst, small_sems.at[chip]))
        return made

    @pl.when(step == 0)
    def _():
        small = small_grads(first_ref, sa_ref, sb_ref, w_ref, embed_ref, ff_ref, va_ref, vb_ref, up_ref)
        small_ref[...] = small
        extra[...] = small
        for copy in small_copies():
            copy.start()

    hold[step] = tn(low_ref[...], dqkv_ref[...]).astype(BF16)

    def copies(j):
        made = []
        for k in range(CHIPS // 2):
            src = hold.at[j, pl.ds(48 * k, 48), :]
            at = tbl[OTHER_POS + j * (CHIPS // 2) + k]
            made.append(pltpu.make_async_copy(src, other.at[at, :, pl.ds(0, QKV)], sems.at[j, k]))
        return made

    for copy in copies(step):
        copy.start()

    @pl.when(step == 1)
    def _():
        for j in range(2):
            for copy in copies(j):
                copy.wait()
        for copy in small_copies():
            copy.wait()


def qkv_own_kernel(tbl, low_ref, dqkv_ref, small_ref, got, keep, away, hold, came, came_sems):
    step = pl.program_id(0)

    @pl.when(step == 0)
    def _():
        for copy in arrivals(tbl, got, came, 48, came_sems):
            copy.start()
        for copy in arrivals(tbl, got, came, 48, came_sems):
            copy.wait()

    rows = pl.ds(pl.multiple_of(step * HALF, HALF), HALF)
    cols = pl.ds(pl.multiple_of(tbl[CORE_AT] * TDIM, TDIM), TDIM)
    hold[:, :QKV] = (tn(low_ref[...], dqkv_ref[...]) + came[rows, :QKV].astype(F32)).astype(BF16)
    hold[:, QKV:] = (small_ref[rows, cols].astype(F32) + came[rows, QKV:].astype(F32)).astype(BF16)
    leave(tbl, hold, step * (CHIPS // 2), CHIPS // 2, keep, away, pl.ds(0, QKV + TDIM))


def input_grad_kernel(df_ref, dqkv_ref, w_ref, ig_ref):
    ig_ref[...] = df_ref[...] + nt(dqkv_ref[...], w_ref[...])


def call(kernel, name, grid, in_specs, out_specs, out_shape, scratch, flops, moved, args, prefetch=1, alias=None):
    return pl.pallas_call(
        kernel,
        name=name,
        grid_spec=pltpu.PrefetchScalarGridSpec(
            num_scalar_prefetch=prefetch, grid=grid, in_specs=in_specs, out_specs=out_specs, scratch_shapes=scratch
        ),
        out_shape=out_shape,
        input_output_aliases=alias or {},
        compiler_params=pltpu.CompilerParams(dimension_semantics=("arbitrary",) * len(grid), vmem_limit_bytes=63 << 20),
        cost_estimate=pl.CostEstimate(flops=flops, bytes_accessed=moved, transcendentals=0),
    )(*args)


def rows_spec(rows, cols):
    return pl.BlockSpec((rows, cols), lambda i, *_: (i, 0))


def whole_spec(shape):
    return pl.BlockSpec(shape, lambda i, *_: (0,) * len(shape))


def cols_spec(rows, cols, top):
    return pl.BlockSpec((rows, cols), lambda i, *_: (0, jnp.minimum(i, top)))


def sds(shape, dtype):
    return jax.ShapeDtypeStruct(shape, dtype)


def block_spec(shape, block):
    return pl.BlockSpec(shape, lambda i, *_: (block,) + (0,) * (len(shape) - 1))


def project(tbl, x, pick, embed, pieces):
    rows = x.shape[0]
    slots = pick.shape[1]
    return call(
        project_kernel, "project", (rows // BLOCK,),
        [rows_spec(BLOCK, D), rows_spec(BLOCK, slots), whole_spec((slots, TDIM))] + [ANY] * 4,
        [rows_spec(BLOCK, D), rows_spec(BLOCK, D), rows_spec(BLOCK, 2 * QKV), whole_spec((16, D)), ANY],
        [sds((rows, D), F32), sds((rows, D), BF16), sds((rows, 2 * QKV), BF16), sds((16, D), F32), sds((D, 2 * QKV), BF16)],
        [pltpu.VMEM((D, 2 * QKV + 2 * TDIM), BF16), pltpu.VMEM((1, 2 * QKV), F32), pltpu.VMEM((1, 2 * QKV), F32),
         pltpu.SemaphoreType.DMA((2, 32)), pltpu.SemaphoreType.DMA((1,))],
        6 * rows * D * D, 20 << 20, (tbl, x, pick, embed, *pieces),
    )


def attend(block, qkv, pick, segr, before):
    rows = qkv.shape[0]
    return call(
        functools.partial(attend_kernel, block), "attend", (1,),
        [block_spec((BLOCK, 2 * QKV), block), block_spec((BLOCK, pick.shape[1]), block),
         block_spec((1, 1, BLOCK), block)] + [ANY] * len(before),
        [block_spec((BLOCK, D), block), ANY],
        [sds((rows, D), BF16), sds((rows // BLOCK, HEADS // 2, 4, 256, 256), BF16)],
        [pltpu.VMEM((4, 256, 128), F32), pltpu.VMEM((2, 256, 256), F32), pltpu.VMEM((2, 4, 256, 256), BF16),
         pltpu.SemaphoreType.DMA((2,))],
        4 * BLOCK * D * D, 20 << 20, (qkv, pick, segr, *before), prefetch=0,
        alias={3 + i: i for i in range(len(before))},
    )


def expand(tbl, hidden, mix, vec, upb, up):
    rows = mix.shape[0]
    tile = 256
    return call(
        expand_kernel, "expand", (rows // tile,),
        [rows_spec(tile, D), rows_spec(tile, D), whole_spec((16, D)), whole_spec((1, FF))] + [ANY] * 4,
        [rows_spec(tile, D), rows_spec(tile, 1), rows_spec(tile, FF), rows_spec(tile, FF), rows_spec(tile, D), ANY],
        [sds((rows, D), F32), sds((rows, 1), F32), sds((rows, FF), BF16), sds((rows, FF), BF16), sds((rows, D), BF16),
         sds((D, FF + D), BF16)],
        [pltpu.VMEM((D, FF + D), BF16), pltpu.VMEM((2, tile, D), F32), pltpu.SemaphoreType.DMA((2, 32)),
         pltpu.SemaphoreType.DMA((1,))],
        2 * rows * D * (FF + D), 20 << 20, (tbl, hidden, mix, vec, upb, *up),
    )


def contract(tbl, n1, i1, cot, vec, act, slope, up, pick, down):
    rows = n1.shape[0]
    tile = 256
    slots = pick.shape[1]
    return call(
        contract_kernel, "contract", (rows // tile,),
        [rows_spec(tile, D), rows_spec(tile, 1), rows_spec(tile, D), whole_spec((16, D)), rows_spec(tile, FF),
         rows_spec(tile, FF), ANY, rows_spec(tile, slots)] + [ANY] * 4,
        [rows_spec(tile, D), rows_spec(tile, FF), rows_spec(tile, D), rows_spec(tile, D), rows_spec(tile, D),
         whole_spec((8, D)), whole_spec((1, FF)), whole_spec((slots, D))],
        [sds((rows, D), BF16), sds((rows, FF), BF16), sds((rows, D), BF16), sds((rows, D), F32), sds((rows, D), BF16),
         sds((8, D), F32), sds((1, FF), F32), sds((slots, D), F32)],
        [pltpu.VMEM((FF, D), BF16), pltpu.VMEM((D, FF), BF16), pltpu.VMEM((2, tile, D), F32), pltpu.SemaphoreType.DMA((1, 32)),
         pltpu.SemaphoreType.DMA((1,))],
        6 * rows * D * FF, 20 << 20, (tbl, n1, i1, cot, vec, act, slope, up, pick, *down),
    )


def down_grad(tbl, act, din):
    rows = act.shape[0]
    shape = sds((CHIPS, FF // CHIPS, HALF), BF16)
    return call(
        down_grad_kernel, "down_grad", (4,), [cols_spec(rows, D, 3), whole_spec((rows, D))], [ANY, ANY], [shape, shape],
        [pltpu.VMEM((4, D, D), BF16), pltpu.SemaphoreType.DMA((4, 8))],
        2 * rows * D * FF, 20 << 20, (tbl, act, din),
    )


def up_specs(rows, kind):
    def half(tbl):
        return jnp.where(kind == 0, tbl[CORE_AT], 1 - tbl[CORE_AT])

    return [whole_spec((rows, D)), pl.BlockSpec((rows, D), lambda i, tbl: (0, 2 * half(tbl) + jnp.minimum(i, 1))),
            whole_spec((rows, D)), pl.BlockSpec((rows, HALF), lambda i, tbl: (0, half(tbl)))]


def up_other(tbl, mlow, dexp, mix, ain):
    rows = mlow.shape[0]
    return call(
        up_other_kernel, "up_other", (3,), up_specs(rows, 1), ANY, sds((CHIPS, 48, 2 * D + HALF), BF16),
        [pltpu.VMEM((3, D, D), BF16), pltpu.SemaphoreType.DMA((3, CHIPS))],
        rows * D * (FF + D), 20 << 20, (tbl, mlow, dexp, mix, ain),
    )


def up_own(tbl, mlow, dexp, mix, ain, got):
    rows = mlow.shape[0]
    shape = sds((CHIPS // 2, 48, 2 * D + HALF), BF16)
    return call(
        up_own_kernel, "up_own", (3,), up_specs(rows, 0) + [ANY], [whole_spec(shape.shape)] * 2, [shape, shape],
        [pltpu.VMEM((D, D), BF16), pltpu.VMEM((D, 2 * D + HALF), BF16), pltpu.SemaphoreType.DMA((CHIPS,))],
        rows * D * (FF + D), 20 << 20, (tbl, mlow, dexp, mix, ain, got),
    )


def qkv_specs(rows, kind):
    def half(tbl):
        return jnp.where(kind == 0, tbl[CORE_AT], 1 - tbl[CORE_AT])

    return [pl.BlockSpec((rows, HALF), lambda i, tbl: (0, i)), pl.BlockSpec((rows, QKV), lambda i, tbl: (0, half(tbl)))]


def qkv_other(tbl, low, dqkv, first, sa, sb, weight, embed, ff, va, vb, up):
    rows = low.shape[0]
    slots = first.shape[0]
    return call(
        qkv_other_kernel, "qkv_other", (2,),
        qkv_specs(rows, 1) + [whole_spec((slots, D)), whole_spec((slots, 2 * QKV)), whole_spec((slots, 2 * QKV)), whole_spec((D, 2 * QKV)),
                              whole_spec((slots, TDIM)), whole_spec((8, D)), whole_spec((8, D)), whole_spec((8, D)),
                              whole_spec((4, D))],
        [whole_spec((D, 2 * TDIM)), ANY], [sds((D, 2 * TDIM), BF16), sds((CHIPS, 48, QKV + TDIM), BF16)],
        [pltpu.VMEM((2, HALF, QKV), BF16), pltpu.VMEM((D, 2 * TDIM), BF16), pltpu.SemaphoreType.DMA((2, CHIPS // 2)),
         pltpu.SemaphoreType.DMA((CHIPS,))],
        3 * rows * D * D, 20 << 20, (tbl, low, dqkv, first, sa, sb, weight, embed, ff, va, vb, up),
    )


def qkv_own(tbl, low, dqkv, small, got):
    rows = low.shape[0]
    shape = sds((CHIPS // 2, 48, QKV + TDIM), BF16)
    return call(
        qkv_own_kernel, "qkv_own", (2,), qkv_specs(rows, 0) + [whole_spec((D, 2 * TDIM)), ANY],
        [whole_spec(shape.shape)] * 2, [shape, shape],
        [pltpu.VMEM((HALF, QKV + TDIM), BF16), pltpu.VMEM((D, QKV + TDIM), BF16), pltpu.SemaphoreType.DMA((CHIPS,))],
        3 * rows * D * D, 20 << 20, (tbl, low, dqkv, small, got),
    )


def attention_backward(block, ain, mix, qkv, probs, weight, pick, before):
    rows = ain.shape[0]
    slots = pick.shape[1]
    return call(
        attention_backward_kernel, "attention_backward", (1,),
        [block_spec((BLOCK, D), block), block_spec((BLOCK, D), block), block_spec((BLOCK, 2 * QKV), block),
         block_spec((1, HEADS // 2, 4, 256, 256), block), pl.BlockSpec((D, D), lambda i, *_: (0, 4)),
         block_spec((BLOCK, slots), block)] + [ANY] * len(before),
        [block_spec((BLOCK, 2 * QKV), block), whole_spec((8, D)), whole_spec((slots, 2 * QKV))],
        [sds((rows, 2 * QKV), BF16), sds((8, D), F32), sds((slots, 2 * QKV), F32)],
        [pltpu.VMEM((BLOCK, D), BF16), pltpu.VMEM((HEADS // 2, 4, 1, 256), F32), pltpu.VMEM((2, 256, 256), F32),
         pltpu.VMEM((BLOCK, 128), F32), pltpu.VMEM((BLOCK, 128), F32)],
        4 * BLOCK * D * D, 20 << 20, (ain, mix, qkv, probs, weight, pick, *before), prefetch=0,
        alias={6 + i: i for i in range(len(before))},
    )


def input_gradient(df, dqkv, weight):
    rows = df.shape[0]
    tile = 256
    return call(
        input_grad_kernel, "input_grad", (rows // tile,),
        [rows_spec(tile, D), rows_spec(tile, 2 * QKV), whole_spec((D, 2 * QKV))], rows_spec(tile, D), sds((rows, D), F32), [],
        6 * rows * D * D, 20 << 20, (df, dqkv, weight), prefetch=0,
    )


def flip(n, even_bit, odd_bit):
    return [(i, i ^ (odd_bit if i & 1 else even_bit)) for i in range(n)]


def tiled_route(n):
    return {"core": flip(n, 1, 1), "z2": flip(n, 16, 16), "z1": flip(n, 8, 8), "a": flip(n, 2, 4), "b": flip(n, 4, 2)}


def tables(n):
    me = lax.axis_index("fsdp")
    core = me % 2
    chips = jnp.arange(CHIPS, dtype=jnp.int32)
    if n == 32:
        here = me // 2

        def order(kind):
            low, high = jnp.where(kind == 0, 1, 2), jnp.where(kind == 0, 2, 1)
            bits = (chips & 1) * 8 + ((chips >> 1) & 1) * 4 + ((chips >> 2) & 1) * low + (chips >> 3) * high
            return here ^ bits

        def place(kind):
            diff = here ^ chips
            x, y = diff & 1, (diff >> 1) & 1
            low, high = jnp.where(kind == 0, x, y), jnp.where(kind == 0, y, x)
            return (diff >> 3) + ((diff >> 2) & 1) * 2 + low * 4 + high * 8

        parts = [order(core), order(1 - core), place(core), place(1 - core)]
    else:
        parts = [chips] * 4
    return jnp.concatenate(parts + [jnp.full((16,), core, jnp.int32)]).astype(jnp.int32)


def own_half(halves, core):
    return jnp.where(core == 0, halves[0], halves[1]), jnp.where(core == 0, halves[1], halves[0])


def tie(*values):
    return lax.optimization_barrier(values)


def follow(first, *values):
    return lax.optimization_barrier((first,) + values)[1:]


def send_on(value, step, n):
    return lax.ppermute(value, "fsdp", perm=tiled_route(n)[step])


def halves_kernel(core_ref, q, k, v, o, up, down, time, columns, mine_a, mine_u, mine_d, theirs):
    core = core_ref[0]
    rows = q.shape[0]

    def half(ref, which, width):
        return ref[:, pl.ds(pl.multiple_of(which * width, 128), width)]

    for which, first in ((core, True), (1 - core, False)):
        tail = jnp.where(which == 0, time[...].astype(F32), columns[...].astype(F32)).astype(BF16)
        a = [half(q, which, HALF), half(k, which, HALF), half(v, which, HALF), tail]
        u = [half(up, which, FF // 2), half(o, which, HALF)]
        d = half(down, which, HALF)
        if first:
            mine_a[...] = jnp.concatenate(a, axis=1)
            mine_u[...] = jnp.concatenate(u, axis=1)
            mine_d[...] = d
        else:
            d = [d[rows * j : rows * j + rows, :] for j in range(d.shape[0] // rows)]
            theirs[...] = jnp.concatenate(a + u + d, axis=1)


def chip_shards(core, q, k, v, o, up, down, time, columns, n):
    rows = q.shape[0]
    down_rows = down.shape[0]
    widths = (QKV + TDIM, FF // 2 + HALF, HALF * down_rows // rows)
    args = (q, k, v, o, up, down, time, columns)
    shapes = [sds((rows, widths[0]), BF16), sds((rows, widths[1]), BF16), sds((down_rows, HALF), BF16), sds((rows, sum(widths)), BF16)]
    mine_a, mine_u, mine_d, theirs = call(
        halves_kernel, "halves", (1,), [whole_spec(item.shape) for item in args], [whole_spec(item.shape) for item in shapes],
        shapes, [], 1 << 10, 1 << 20, (core.reshape(1), *args),
    )
    got = send_on(theirs, "core", n)
    got_d = got[:, widths[0] + widths[1] :]
    got_d = jnp.concatenate([got_d[:, HALF * j : HALF * j + HALF] for j in range(down_rows // rows)], axis=0)
    shards = []
    for mine, came in ((mine_a, got[:, : widths[0]]), (mine_u, got[:, widths[0] : widths[0] + widths[1]]), (mine_d, got_d)):
        shards.append(jnp.concatenate(own_half((mine, came), core), axis=0)[None])
    return shards


def whole_gather(halves, core):
    full = [lax.all_gather(half, "fsdp", axis=0, tiled=True) for half in halves]
    full = [item.reshape(CHIPS, -1, item.shape[1]) for item in full]
    own, other = own_half(full, core)
    middle = CHIPS // 2
    return own[:middle], own[middle:], other[:middle], other[middle:]


def widen(held, step, n):
    return jnp.concatenate([held, send_on(held, step, n)], axis=0)


def add(left, right):
    return (left.astype(F32) + right.astype(F32)).astype(BF16)


def halve(keep, got):
    middle = keep.shape[0] // 2
    return add(keep[:middle], got[:middle]), add(keep[middle:], got[middle:])


def finish(keep, got, n):
    core = lax.axis_index("fsdp") % 2
    total = keep[0].astype(F32) + got[0].astype(F32)
    rows = total.shape[0] // 2
    mine, theirs = own_half((total[:rows], total[rows:]), core)
    got = send_on(theirs.astype(BF16), "core", n).astype(F32)
    return own_half((mine, got), core)


def whole_reduce(own, other, core):
    sums = []
    for item in own_half((own, other), core):
        item = item.reshape(-1, item.shape[2])
        sums.append(lax.psum_scatter(item, "fsdp", scatter_dimension=0, tiled=True).astype(F32))
    return sums


def sinusoid(steps):
    half = TDIM // 2
    freqs = jnp.exp(-math.log(10000.0) * jnp.arange(half, dtype=F32) / half)
    angles = steps.astype(F32)[:, None] * freqs[None, :]
    return jnp.concatenate([jnp.cos(angles), jnp.sin(angles)], axis=1)


def body(
    inputs, cotangent, lengths, timesteps, time_weight, time_bias, query_weight, query_bias, key_weight,
    value_weight, value_bias, out_weight, out_bias, mid_gain, mid_shift, up_weight, up_bias, down_weight,
    down_bias, last_gain, last_shift,
):
    n = lax.axis_size("fsdp")
    rows = inputs.shape[0]
    blocks = rows // BLOCK
    tbl = tables(n)
    shard = D // n

    vectors = [query_bias, value_bias, out_bias, mid_gain, mid_shift, down_bias, last_gain, last_shift, time_bias]
    vectors += [up_bias[shard * k : shard * (k + 1)] for k in range(FF // D)]
    lane = lax.broadcasted_iota(jnp.int32, (shard, TDIM), 1)
    columns = jnp.zeros((shard, TDIM), F32)
    for k, item in enumerate(vectors):
        columns = jnp.where(lane == k, item.astype(F32)[:, None], columns)
    columns = columns.astype(BF16)
    small_halves = [time_weight.T, columns]
    attn_halves = [
        jnp.concatenate(
            [w[:, HALF * h : HALF * h + HALF] for w in (query_weight, key_weight, value_weight)] + [small_halves[h]], axis=1
        )
        for h in range(2)
    ]
    up_halves = [
        jnp.concatenate([up_weight[:, FF // 2 * h : FF // 2 * (h + 1)], out_weight[:, HALF * h : HALF * h + HALF]], axis=1)
        for h in range(2)
    ]
    down_halves = [down_weight[:, :HALF], down_weight[:, HALF:]]

    core = lax.axis_index("fsdp") % 2
    tiled = n == 32

    def slot_arrays(lengths, timesteps):
        ends = jnp.cumsum(lengths, axis=1)
        position = jnp.arange(BLOCK, dtype=jnp.int32)
        owner = jnp.sum((position[None, :, None] >= ends[:, None, :]).astype(jnp.int32), axis=2)
        slot_of = (owner + SLOTS * jnp.arange(blocks, dtype=jnp.int32)[:, None]).reshape(rows, 1)
        pick = (slot_of == lax.broadcasted_iota(jnp.int32, (rows, blocks * SLOTS), 1)).astype(BF16)
        segr = slot_of.reshape(blocks, 1, BLOCK).astype(F32)
        embed_in = sinusoid(timesteps.reshape(-1)).astype(BF16)
        return pick, segr, embed_in

    if tiled:
        a0, u0, d0 = chip_shards(
            core, query_weight, key_weight, value_weight, out_weight, up_weight, down_weight, time_weight.T, columns, n
        )
        a0 = widen(a0, "z2", n)
        pick, segr, embed_in = slot_arrays(*follow(a0, lengths, timesteps))
        a0 = widen(a0, "z1", n)
        (u0,) = follow(a0, u0)
        a0 = widen(a0, "a", n)
        u0 = widen(u0, "z2", n)
        a0, u0 = tie(a0, u0)
        a1 = send_on(a0, "b", n)
        a2 = send_on(a0, "core", n)
        u0 = widen(u0, "z1", n)
        a1, u0, d0, tbl, pick, segr, embed_in = tie(a1, u0, d0, tbl, pick, segr, embed_in)
        a3 = send_on(a1, "core", n)
        u_got = send_on(u0, "a", n)
        d_got = send_on(d0, "z2", n)
        hidden, low, qkv, vec, weight = project(tbl, inputs, pick, embed_in, (a0, a1, a2, a3))
        qkv, u0, u_got, d0, d_got = tie(qkv, u0, u_got, d0, d_got)
        u0 = jnp.concatenate([u0, u_got], axis=0)
        d0 = jnp.concatenate([d0, d_got], axis=0)
        u1 = send_on(u0, "b", n)
        d_got = send_on(d0, "z1", n)
        u2 = send_on(u0, "core", n)
        parts = attend(0, qkv, pick, segr, ())
        *parts, qkv, u0, u2, d0, d_got = tie(*parts, qkv, u0, u2, d0, d_got)
        d0 = jnp.concatenate([d0, d_got], axis=0)
        d_got = send_on(d0, "a", n)
        mix, probs = attend(1, qkv, pick, segr, parts)
        mix, u1, d0, d_got = tie(mix, u1, d0, d_got)
        u3 = send_on(u1, "core", n)
        d0 = jnp.concatenate([d0, d_got], axis=0)
        d1 = send_on(d0, "b", n)
        d2 = send_on(d0, "core", n)
        up_offset = vec[9:13].reshape(FF // D, n, shard).transpose(1, 0, 2).reshape(1, FF)
        n1, i1, act, slope, mlow, up_full = expand(tbl, hidden, mix, vec, up_offset, (u0, u1, u2, u3))
        act, d1 = tie(act, d1)
        d3 = send_on(d1, "core", n)
        down_pieces = (d0, d1, d2, d3)
    else:
        pick, segr, embed_in = slot_arrays(lengths, timesteps)
        hidden, low, qkv, vec, weight = project(tbl, inputs, pick, embed_in, whole_gather(attn_halves, core))
        mix, probs = attend(1, qkv, pick, segr, attend(0, qkv, pick, segr, ()))
        up_offset = vec[9:13].reshape(FF // D, n, shard).transpose(1, 0, 2).reshape(1, FF)
        n1, i1, act, slope, mlow, up_full = expand(tbl, hidden, mix, vec, up_offset, whole_gather(up_halves, core))
        down_pieces = whole_gather(down_halves, core)

    res, dexp, din, df, ain, ff_vecs, up_vec, slot_first = contract(
        tbl, n1, i1, cotangent, vec, act, slope, up_full, pick, down_pieces
    )
    up_vec = up_vec.reshape(n, FF // D, shard).transpose(1, 0, 2).reshape(FF // D, D)
    d_own, d_other = down_grad(tbl, act, din)
    mlow, d_own, d_other = tie(mlow, d_own, d_other)
    u_other = up_other(tbl, mlow, dexp, mix, ain)
    if tiled:
        d_got = send_on(d_other, "core", n)
        u_other, d_own, d_got, mlow, up_vec = tie(u_other, d_own, d_got, mlow, up_vec)
        u_got = send_on(u_other, "core", n)
        d_keep, d_away = halve(d_own, d_got)
        d_keep, d_away, u_got = tie(d_keep, d_away, u_got)
        d_got = send_on(d_away, "b", n)
        u_keep, u_away = up_own(tbl, mlow, dexp, mix, ain, u_got)
        ain, u_keep, u_away = tie(ain, u_keep, u_away)
        u_got = send_on(u_away, "b", n)
        dqkv, vg0, slot0 = attention_backward(0, ain, mix, qkv, probs, up_full, pick, ())
        dqkv, d_keep, d_got = tie(dqkv, d_keep, d_got)
        d_keep, d_away = halve(d_keep, d_got)
        ain, dqkv, d_keep, d_away = tie(ain, dqkv, d_keep, d_away)
        d_got = send_on(d_away, "a", n)
        dqkv, vg1, slot1 = attention_backward(1, ain, mix, qkv, probs, up_full, pick, (dqkv,))
        dqkv, d_keep, d_got, u_keep, u_got = tie(dqkv, d_keep, d_got, u_keep, u_got)
        u_keep, u_away = halve(u_keep, u_got)
        d_keep, d_away = halve(d_keep, d_got)
        low, dqkv, d_keep, d_away, u_keep, u_away = tie(low, dqkv, d_keep, d_away, u_keep, u_away)
        u_got = send_on(u_away, "a", n)
        d_got = send_on(d_away, "z1", n)
        small, q_other = qkv_other(
            tbl, low, dqkv, slot_first, slot0, slot1, weight, embed_in, ff_vecs, vg0, vg1, up_vec
        )
        q_other, u_keep, u_got, d_keep, d_got, low = tie(q_other, u_keep, u_got, d_keep, d_got, low)
        q_got = send_on(q_other, "core", n)
        u_keep, u_away = halve(u_keep, u_got)
        d_keep, d_away = halve(d_keep, d_got)
        q_got, u_keep, u_away, d_keep, d_away = tie(q_got, u_keep, u_away, d_keep, d_away)
        u_got = send_on(u_away, "z1", n)
        q_keep, q_away = qkv_own(tbl, low, dqkv, small, q_got)
        df, q_keep, q_away, u_keep, u_got = tie(df, q_keep, q_away, u_keep, u_got)
        q_got = send_on(q_away, "b", n)
        u_keep, u_away = halve(u_keep, u_got)
        df, d_away, u_keep, u_away = tie(df, d_away, u_keep, u_away)
        d_got = send_on(d_away, "z2", n)
        u_got = send_on(u_away, "z2", n)
        input_grad = input_gradient(df, dqkv, weight)
        input_grad, q_keep, q_got = tie(input_grad, q_keep, q_got)
        q_keep, q_away = halve(q_keep, q_got)
        u_keep, u_got, d_keep, d_got = follow(q_away, u_keep, u_got, d_keep, d_got)
        q_got = send_on(q_away, "a", n)
        down_sum = finish(d_keep, d_got, n)
        q_keep, q_away = halve(q_keep, q_got)
        q_got = send_on(q_away, "z1", n)
        up_sum = finish(u_keep, u_got, n)
        q_keep, q_away = halve(q_keep, q_got)
        q_got = send_on(q_away, "z2", n)
        qkv_sum = finish(q_keep, q_got, n)
    else:
        dqkv, vg0, slot0 = attention_backward(0, ain, mix, qkv, probs, up_full, pick, ())
        dqkv, vg1, slot1 = attention_backward(1, ain, mix, qkv, probs, up_full, pick, (dqkv,))
        small, q_other = qkv_other(
            tbl, low, dqkv, slot_first, slot0, slot1, weight, embed_in, ff_vecs, vg0, vg1, up_vec
        )
        input_grad = input_gradient(df, dqkv, weight)
        down_sum = whole_reduce(d_own, d_other, core)
        zero_u, zero_q = jnp.zeros_like(u_other), jnp.zeros_like(q_other)
        u_own = jnp.concatenate(up_own(tbl, mlow, dexp, mix, ain, zero_u), axis=0)
        q_own = jnp.concatenate(qkv_own(tbl, low, dqkv, small, zero_q), axis=0)
        up_sum = whole_reduce(u_own, u_other, core)
        qkv_sum = whole_reduce(q_own, q_other, core)
    def both(pair, start, stop):
        return jnp.concatenate([half[:, start:stop] for half in pair], axis=1)

    out_query = both(qkv_sum, 0, HALF)
    out_key = both(qkv_sum, HALF, 2 * HALF)
    out_value = both(qkv_sum, 2 * HALF, QKV)
    out_up = both(up_sum, 0, 2 * D)
    out_out = both(up_sum, 2 * D, 2 * D + HALF)
    out_down = both(down_sum, 0, HALF)
    out_time = qkv_sum[0][:, QKV:].T
    v = qkv_sum[1][:, QKV : QKV + 13].T
    v_up = v[9:13].reshape(-1)
    return (
        res, input_grad, out_time, out_query, out_key, out_value, out_out, out_up, out_down,
        v[0], v[1], v[2], v[8], v[6], v[7], v_up, v[5], v[3], v[4],
    )


def solution(mesh):
    row, col, vec = P("fsdp", None), P(None, "fsdp"), P("fsdp")
    in_specs = (
        row, row, row, row, col, vec, row, vec, row, row, vec, row, vec, vec, vec, row, vec, row, vec, vec, vec,
    )
    out_specs = (row, row, col, row, row, row, row, row, row) + (vec,) * 10
    return jax.shard_map(body, mesh=mesh, in_specs=in_specs, out_specs=out_specs, check_vma=False)
```

```python
import functools
import math

import jax
import jax.numpy as jnp
from jax import lax
from jax.experimental import pallas as pl
from jax.experimental.pallas import tpu as pltpu
from jax.sharding import PartitionSpec as P

D = 768
HEAD = 64
HEADS = 12
FF = 3072
TDIM = 128
SLOTS = 8
BLOCK = 512
HALF = D // 2
QKV = 3 * HALF
CHIPS = 16
EPS = 1e-05
NEG = -1e30
HIGH = lax.Precision.HIGHEST
SQRT_HALF = 0.7071067811865476
INV_ROOT_TAU = 0.3989422804014327
HALF_LOG = -0.5 / math.log(2.0)
WINDOWS = (0, 64, 192, 256)
F32 = jnp.float32
BF16 = jnp.bfloat16
ANY = pl.BlockSpec(memory_space=pl.ANY)
OWN_ROW, OTHER_ROW, OWN_POS, OTHER_POS, CORE_AT = 0, 16, 32, 48, 64


def nn(left, right):
    return lax.dot_general(left, right, (((1,), (0,)), ((), ())), preferred_element_type=F32)


def nt(left, right):
    return lax.dot_general(left, right, (((1,), (1,)), ((), ())), preferred_element_type=F32)


def tn(left, right):
    return lax.dot_general(left, right, (((0,), (0,)), ((), ())), preferred_element_type=F32)


def in_halves(product, left, right):
    middle = left.shape[0] // 2
    return jnp.concatenate([product(left[:middle], right), product(left[middle:], right)], axis=0)


def mean(values):
    return jnp.sum(values, axis=-1, keepdims=True) * (1.0 / D)


def normalize(values):
    center = values - mean(values)
    inverse = lax.rsqrt(mean(center * center) + EPS)
    return center * inverse, inverse


def norm_back(grad, normed, inverse):
    return inverse * (grad - mean(grad) - normed * mean(grad * normed))


def column_sum(values):
    return jnp.sum(values, axis=0, keepdims=True)


def piece_copies(tbl, refs, weight, sems, rows, parts):
    own_low, own_high, other_low, other_high = refs
    core = tbl[CORE_AT]
    copies = []
    for kind, (low, high) in enumerate(((own_low, own_high), (other_low, other_high))):
        half = core if kind == 0 else 1 - core
        for j in range(CHIPS):
            piece = (low if j < CHIPS // 2 else high).at[j % (CHIPS // 2)]
            at = pl.ds(pl.multiple_of(tbl[kind * CHIPS + j] * rows, rows), rows)
            for k, (start, width, base) in enumerate(parts):
                cols = pl.ds(pl.multiple_of(base + half * width, 128), width)
                copies.append(
                    pltpu.make_async_copy(piece.at[:, pl.ds(start, width)], weight.at[at, cols], sems.at[k, kind * CHIPS + j])
                )
    return copies


def lane_masks():
    lane = lax.broadcasted_iota(jnp.int32, (1, 2 * HEAD), 1)
    first = jnp.where(lane < HEAD, 1.0, 0.0)
    return first.astype(BF16), (1.0 - first).astype(BF16), lane < HEAD


def split_bf16(values):
    high = values.astype(BF16)
    rest = values - high.astype(F32)
    return high, rest.astype(BF16), rest


def project_kernel(
    tbl, x_ref, pick_ref, embed_ref, own_low, own_high, other_low, other_high,
    hidden_ref, low_ref, qkv_ref, vec_ref, w_ref, weight, offset, factor, sems, out_sem,
):
    step = pl.program_id(0)
    save = pltpu.make_async_copy(weight.at[:, pl.ds(0, 2 * QKV)], w_ref, out_sem.at[0])

    @pl.when(step == 0)
    def _():
        parts = ((0, QKV, 0), (QKV, TDIM, 2 * QKV))
        copies = piece_copies(tbl, (own_low, own_high, other_low, other_high), weight, sems, 48, parts)
        for copy in copies:
            copy.start()
        for copy in copies:
            copy.wait()
        save.start()
        vec_ref[...] = weight[:, 2 * QKV + TDIM :].astype(F32).T[:16, :]
        offset[...] = jnp.zeros_like(offset)
        factor[...] = jnp.ones_like(factor)
        for half in range(2):
            cols = slice(HALF * half, HALF * half + HALF)
            at = QKV * half
            offset[:, at : at + HALF] = vec_ref[0:1, cols]
            offset[:, at + 2 * HALF : at + QKV] = vec_ref[1:2, cols]
            factor[:, at : at + HALF] = jnp.full((1, HALF), HEAD**-0.5, F32)

    slots = nt(embed_ref[...], weight[:, 2 * QKV : 2 * QKV + TDIM]) + vec_ref[8:9, :]
    high, middle, rest = split_bf16(slots)
    low = (rest - middle.astype(F32)).astype(BF16)
    picks = pick_ref[...]
    slot = nn(jnp.concatenate([picks, picks, picks], axis=1), jnp.concatenate([high, middle, low], axis=0))
    hidden_ref[...] = x_ref[...].astype(F32) + slot
    low_ref[...] = hidden_ref[...].astype(BF16)

    for j in range(3):
        at = slice(j * D, j * D + D)
        y = nn(low_ref[...], weight[:, at]) + offset[:, at]
        qkv_ref[:, at] = (y.astype(BF16).astype(F32) * factor[:, at]).astype(BF16)

    @pl.when(step == pl.num_programs(0) - 1)
    def _():
        save.wait()


def attend_kernel(block, qkv_ref, pick_ref, segr_ref, *rest):
    mix_ref, probs_ref, bias, scores, held, sems = rest[-6:]
    slot = lax.broadcasted_iota(jnp.int32, pick_ref.shape, 1).astype(F32)
    owner = jnp.sum(pick_ref[...].astype(F32) * slot, axis=1, keepdims=True)
    for t in range(4):
        same = owner[WINDOWS[t] : WINDOWS[t] + 256, :] == segr_ref[0, :, 128 * t : 128 * t + 128]
        bias[t] = jnp.where(same, 0.0, NEG)
    first, second, _ = lane_masks()

    def operands(p, t):
        at = pl.multiple_of((p // 3) * QKV + (p % 3) * 128, 128)
        window = slice(WINDOWS[t], WINDOWS[t] + 256)
        return at, window

    def scores_of(p, t):
        at, window = operands(p, t)
        q = qkv_ref[128 * t : 128 * t + 128, pl.ds(at, 128)]
        k = qkv_ref[window, pl.ds(at + HALF, 128)]
        both = jnp.concatenate([q * first, q * second], axis=0)
        s = in_halves(nt, k, both) + jnp.concatenate([bias[t], bias[t]], axis=1)
        scores[t % 2] = s
        return jnp.max(s, axis=0, keepdims=True)

    def out_copy(p):
        return pltpu.make_async_copy(held.at[p % 2], probs_ref.at[block, p], sems.at[p % 2])

    def pair(p, peak):
        @pl.when(p >= 2)
        def _():
            out_copy(p - 2).wait()

        for t in range(4):
            ahead = scores_of(p, t + 1) if t < 3 else scores_of(jnp.minimum(p + 1, HEADS // 2 - 1), 0)
            at, window = operands(p, t)
            v = qkv_ref[window, pl.ds(at + 2 * HALF, 128)]
            e = jnp.exp(scores[t % 2] - peak)
            probs = (e * (1.0 / jnp.sum(e, axis=0, keepdims=True))).astype(BF16)
            held[p % 2, t] = probs
            turned = v.T
            out = jnp.concatenate([nn(turned[:HEAD], probs[:, :128]), nn(turned[HEAD:], probs[:, 128:])], axis=0)
            mix_ref[128 * t : 128 * t + 128, pl.ds(pl.multiple_of(p * 128, 128), 128)] = out.T.astype(BF16)
            peak = ahead
        out_copy(p).start()
        return peak

    lax.fori_loop(0, HEADS // 2, pair, scores_of(0, 0))
    out_copy(HEADS // 2 - 2).wait()
    out_copy(HEADS // 2 - 1).wait()

def expand_kernel(
    tbl, hidden_ref, mix_ref, vec_ref, upb_ref, ua, ub, uc, ud,
    n1_ref, i1_ref, act_ref, slope_ref, mlow_ref, up_ref, up, wide, sems, out_sem,
):
    step = pl.program_id(0)
    save = pltpu.make_async_copy(up, up_ref, out_sem.at[0])
    both = piece_copies(tbl, (ua, ub, uc, ud), up, sems, 48, ((FF // 2, HALF, FF), (0, FF // 2, 0)))
    copies = both[0::2], both[1::2]

    @pl.when(step == 0)
    def _():
        for copy in copies[0] + copies[1]:
            copy.start()
        for copy in copies[0]:
            copy.wait()

    normed, inverse = normalize(hidden_ref[...] + nn(mix_ref[...], up[:, FF:]) + vec_ref[2:3, :])
    n1_ref[...] = normed
    i1_ref[...] = inverse
    mlow_ref[...] = (normed * vec_ref[3:4, :] + vec_ref[4:5, :]).astype(BF16)

    def expand(j):
        at = slice(j * D, j * D + D)
        wide[j % 2] = nn(mlow_ref[...], up[:, at]) + upb_ref[:, at]

    def activate(j):
        at = slice(j * D, j * D + D)
        u = wide[j % 2]
        scaled = u * SQRT_HALF
        twice = 1.0 + lax.erf(scaled)
        act_ref[:, at] = ((u * 0.5) * twice).astype(BF16)
        slope_ref[:, at] = (0.5 * twice + (u * INV_ROOT_TAU) * jnp.exp2((u * u) * HALF_LOG)).astype(BF16)

    @pl.when(step == 0)
    def _():
        for copy in copies[1]:
            copy.wait()
        save.start()

    expand(0)
    for j in range(FF // D):
        if j + 1 < FF // D:
            expand(j + 1)
        activate(j)

    @pl.when(step == pl.num_programs(0) - 1)
    def _():
        save.wait()


def contract_kernel(
    tbl, n1_ref, i1_ref, cot_ref, vec_ref, act_ref, slope_ref, up_ref, pick_ref, da, db, dc, dd,
    res_ref, dexp_ref, din_ref, df_ref, ain_ref, vg_ref, gup_ref, slot_ref, down, up, wide, sems, up_sem,
):
    step = pl.program_id(0)
    fetch = pltpu.make_async_copy(up_ref.at[:, pl.ds(0, FF)], up, up_sem.at[0])

    @pl.when(step == 0)
    def _():
        copies = piece_copies(tbl, (da, db, dc, dd), down, sems, FF // CHIPS, ((0, HALF, 0),))
        for copy in copies:
            copy.start()
        for copy in copies:
            copy.wait()
        fetch.start()
        vg_ref[...] = jnp.zeros_like(vg_ref)
        gup_ref[...] = jnp.zeros_like(gup_ref)
        slot_ref[...] = jnp.zeros_like(slot_ref)

    def vec(i):
        return vec_ref[i : i + 1, :]

    second = n1_ref[...] * vec(3) + vec(4) + nn(act_ref[...], down[...]) + vec(5)
    normed2, inverse2 = normalize(second)
    res_ref[...] = (normed2 * vec(6) + vec(7)).astype(BF16)
    upstream = cot_ref[...].astype(F32)
    vg_ref[0:1, :] += column_sum(upstream * normed2)
    vg_ref[1:2, :] += column_sum(upstream)
    d_second = norm_back(upstream * vec(6), normed2, inverse2)
    down_in = d_second.astype(BF16)
    din_ref[...] = down_in
    vg_ref[2:3, :] += column_sum(down_in.astype(F32))

    def contract(j):
        wide[j % 2] = nt(din_ref[...], down[j * D : j * D + D, :])

    @pl.when(step == 0)
    def _():
        fetch.wait()

    contract(0)
    for j in range(FF // D):
        if j + 1 < FF // D:
            contract(j + 1)
        at = slice(j * D, j * D + D)
        d_exp = (wide[j % 2] * slope_ref[:, at].astype(F32)).astype(BF16)
        dexp_ref[:, at] = d_exp
        gup_ref[:, at] += column_sum(d_exp.astype(F32))
    d_middle = nt(dexp_ref[...], up[...]) + d_second
    normed1 = n1_ref[...]
    vg_ref[3:4, :] += column_sum(d_middle * normed1)
    vg_ref[4:5, :] += column_sum(d_middle)
    d_first = norm_back(d_middle * vec(3), normed1, i1_ref[...])
    df_ref[...] = d_first
    attn_in = d_first.astype(BF16)
    ain_ref[...] = attn_in
    vg_ref[5:6, :] += column_sum(attn_in.astype(F32))
    rest = (d_first - attn_in.astype(F32)).astype(BF16)
    slot_ref[...] += tn(pick_ref[...], attn_in) + tn(pick_ref[...], rest)


def down_grad_kernel(tbl, act_ref, din_ref, own, other, hold, sems):
    step = pl.program_id(0)
    core = tbl[CORE_AT]
    rows = FF // CHIPS
    hold[step] = tn(act_ref[...], din_ref[...]).astype(BF16)

    def copies(j):
        made = []
        for k in range(4):
            chip = 4 * j + k
            for kind, (target, table) in enumerate(((own, OWN_POS), (other, OTHER_POS))):
                half = core if kind == 0 else 1 - core
                src = hold.at[j, pl.ds(k * rows, rows), pl.ds(pl.multiple_of(half * HALF, HALF), HALF)]
                made.append(pltpu.make_async_copy(src, target.at[tbl[table + chip]], sems.at[j, 2 * k + kind]))
        return made

    for copy in copies(step):
        copy.start()

    @pl.when(step == pl.num_programs(0) - 1)
    def _():
        for j in range(4):
            for copy in copies(j):
                copy.wait()


def product_for(step, half, mlow_ref, dexp_ref, mix_all, ain_all, mix, ain, sems, give):
    fetches = [
        pltpu.make_async_copy(mix_all, mix, sems.at[0]),
        pltpu.make_async_copy(ain_all.at[:, pl.ds(pl.multiple_of(half * HALF, HALF), HALF)], ain, sems.at[1]),
    ]

    @pl.when(step == 0)
    def _():
        for fetch in fetches:
            fetch.start()

    @pl.when(step < 2)
    def _():
        give(tn(mlow_ref[...], dexp_ref[...]), pl.ds(pl.multiple_of(step * D, D), D), D)

    @pl.when(step == 2)
    def _():
        for fetch in fetches:
            fetch.wait()
        give(tn(mix[...], ain[...]), pl.ds(2 * D, HALF), HALF)


def up_other_kernel(tbl, mlow_ref, dexp_ref, mix_all, ain_all, other, hold, mix, ain, sems, fetch_sems):
    step = pl.program_id(0)

    def copies(j, width):
        made = []
        for chip in range(CHIPS):
            src = hold.at[j, pl.ds(48 * chip, 48), pl.ds(0, width)]
            cols = pl.ds(pl.multiple_of(j * D, D), width)
            made.append(pltpu.make_async_copy(src, other.at[tbl[OTHER_POS + chip], :, cols], sems.at[j, chip]))
        return made

    def give(grad, cols, width):
        hold[step, :, :width] = grad.astype(BF16)
        for copy in copies(step, width):
            copy.start()

    product_for(step, 1 - tbl[CORE_AT], mlow_ref, dexp_ref, mix_all, ain_all, mix, ain, fetch_sems, give)

    @pl.when(step == 2)
    def _():
        for j in range(3):
            for copy in copies(j, D if j < 2 else HALF):
                copy.wait()


def arrivals(tbl, got, came, rows, sems):
    made = []
    for chip in range(CHIPS):
        dst = came.at[pl.ds(rows * chip, rows), :]
        made.append(pltpu.make_async_copy(got.at[tbl[OWN_POS + chip]], dst, sems.at[chip]))
    return made


def leave(tbl, src, first, count, keep, away, cols):
    def one(k, carry):
        at = tbl[OWN_POS + first + k]
        rows = src[pl.ds(pl.multiple_of(48 * k, 48), 48), :]

        @pl.when(at < CHIPS // 2)
        def _():
            keep[at, :, cols] = rows

        @pl.when(at >= CHIPS // 2)
        def _():
            away[at - CHIPS // 2, :, cols] = rows

        return carry

    lax.fori_loop(0, count, one, 0)


def up_own_kernel(tbl, mlow_ref, dexp_ref, mix_all, ain_all, got, keep, away, hold, came, mix, ain, came_sems, fetch_sems):
    step = pl.program_id(0)

    @pl.when(step == 0)
    def _():
        for copy in arrivals(tbl, got, came, 48, came_sems):
            copy.start()
        for copy in arrivals(tbl, got, came, 48, came_sems):
            copy.wait()

    def give(grad, cols, width):
        hold[:, :width] = (grad + came[:, cols].astype(F32)).astype(BF16)
        leave(tbl, hold.at[:, pl.ds(0, width)], 0, CHIPS, keep, away, cols)

    product_for(step, tbl[CORE_AT], mlow_ref, dexp_ref, mix_all, ain_all, mix, ain, fetch_sems, give)


def attention_backward_kernel(block, ain_ref, mix_ref, qkv_all, probs_all, w_ref, pick_ref, *rest):
    dqkv_ref, slot_ref, d_mix, delta, d_probs, dk, dv, qkv_ref, probs_ref, sems = rest[-10:]
    fetches = [
        pltpu.make_async_copy(qkv_all.at[pl.ds(block * BLOCK, BLOCK), :], qkv_ref, sems.at[0]),
        pltpu.make_async_copy(probs_all.at[block], probs_ref, sems.at[1]),
    ]
    for fetch in fetches:
        fetch.start()
    d_mix[...] = nt(ain_ref[...], w_ref[...]).astype(BF16)
    product = d_mix[...].astype(F32) * mix_ref[...].astype(F32)
    high, low, _ = split_bf16(product)
    head = lax.broadcasted_iota(jnp.int32, (16, D), 0)
    column = lax.broadcasted_iota(jnp.int32, (16, D), 1)
    ones = jnp.where(column // HEAD == head, 1.0, 0.0).astype(BF16)
    dots = nt(ones, high) + nt(ones, low)
    for p in range(HEADS // 2):
        for t in range(4):
            rows = slice(128 * t, 128 * t + 128)
            delta[p, t] = jnp.concatenate([dots[2 * p : 2 * p + 1, rows], dots[2 * p + 1 : 2 * p + 2, rows]], axis=1)
    first, second, choose = lane_masks()

    def offsets(p):
        return pl.multiple_of((p // 3) * QKV + (p % 3) * 128, 128)

    def outs_of(p, t):
        do = d_mix[128 * t : 128 * t + 128, pl.ds(pl.multiple_of(p * 128, 128), 128)]
        return jnp.concatenate([do * first, do * second], axis=0)

    def d_probs_of(p, t):
        v = qkv_ref[WINDOWS[t] : WINDOWS[t] + 256, pl.ds(offsets(p) + 2 * HALF, 128)]
        d_probs[t % 2] = in_halves(nt, v, outs_of(p, t))

    def pair(p, carry):
        at = offsets(p)
        dk[...] = jnp.zeros_like(dk)
        dv[...] = jnp.zeros_like(dv)
        for t in range(4):
            if t < 3:
                d_probs_of(p, t + 1)
            else:
                d_probs_of(jnp.minimum(p + 1, HEADS // 2 - 1), 0)
            window = slice(WINDOWS[t], WINDOWS[t] + 256)
            q = qkv_ref[128 * t : 128 * t + 128, pl.ds(at, 128)]
            k = qkv_ref[window, pl.ds(at + HALF, 128)]
            queries = jnp.concatenate([q * first, q * second], axis=0)
            probs = probs_ref[p, t]
            dv[window, :] += in_halves(nn, probs, outs_of(p, t))
            scores = (probs.astype(F32) * (d_probs[t % 2] - delta[p, t])).astype(BF16)
            dk[window, :] += in_halves(nn, scores, queries)
            dq = jnp.where(choose, tn(scores[:, :128], k), tn(scores[:, 128:], k)) * HEAD**-0.5
            dqkv_ref[128 * t : 128 * t + 128, pl.ds(at, 128)] = dq.astype(BF16)
        dqkv_ref[:, pl.ds(at + HALF, 128)] = dk[...].astype(BF16)
        dqkv_ref[:, pl.ds(at + 2 * HALF, 128)] = dv[...].astype(BF16)
        return carry

    for fetch in fetches:
        fetch.wait()
    d_probs_of(0, 0)
    lax.fori_loop(0, HEADS // 2, pair, 0)
    slot_ref[...] = tn(pick_ref[...], dqkv_ref[...])


def small_grads(first_ref, sa_ref, sb_ref, w_ref, embed_ref, ff_ref, up_ref):
    second = sa_ref[...] + sb_ref[...]
    high, low, _ = split_bf16(second)
    biases = column_sum(second)
    query = jnp.concatenate([biases[:, :HALF], biases[:, QKV : QKV + HALF]], axis=1)
    value = jnp.concatenate([biases[:, 2 * HALF : QKV], biases[:, QKV + 2 * HALF :]], axis=1)
    both = nt(jnp.concatenate([high, low], axis=0), w_ref[...])
    slots = first_ref[...] + both[: high.shape[0]] + both[high.shape[0] :]
    slot_low = slots.astype(BF16)
    rows = [column_sum(slot_low.astype(F32)), query, value, ff_ref[0:6, :], up_ref[0:4, :]]
    rows.append(jnp.zeros((TDIM - 13, D), F32))
    vectors = jnp.concatenate(rows, axis=0).T
    return jnp.concatenate([tn(slot_low, embed_ref[...]), vectors], axis=1).astype(BF16)


def qkv_other_kernel(
    tbl, low_ref, dqkv_ref, first_ref, sa_ref, sb_ref, w_all, embed_ref, ff_ref, up_ref,
    small_ref, other, hold, extra, w_ref, sems, small_sems, w_sem,
):
    step = pl.program_id(0)
    off = 1 - tbl[CORE_AT]

    def small_copies():
        made = []
        for chip in range(CHIPS):
            src = extra.at[pl.ds(48 * chip, 48), pl.ds(pl.multiple_of(off * TDIM, TDIM), TDIM)]
            dst = other.at[tbl[OTHER_POS + chip], :, pl.ds(QKV, TDIM)]
            made.append(pltpu.make_async_copy(src, dst, small_sems.at[chip]))
        return made

    fetch = pltpu.make_async_copy(w_all, w_ref, w_sem.at[0])

    @pl.when(step == 0)
    def _():
        fetch.start()

    @pl.when(step == 1)
    def _():
        fetch.wait()
        small = small_grads(first_ref, sa_ref, sb_ref, w_ref, embed_ref, ff_ref, up_ref)
        small_ref[...] = small
        extra[...] = small
        for copy in small_copies():
            copy.start()

    hold[step] = tn(low_ref[...], dqkv_ref[...]).astype(BF16)

    def copies(j):
        made = []
        for k in range(CHIPS // 2):
            src = hold.at[j, pl.ds(48 * k, 48), :]
            at = tbl[OTHER_POS + j * (CHIPS // 2) + k]
            made.append(pltpu.make_async_copy(src, other.at[at, :, pl.ds(0, QKV)], sems.at[j, k]))
        return made

    for copy in copies(step):
        copy.start()

    @pl.when(step == 1)
    def _():
        for j in range(2):
            for copy in copies(j):
                copy.wait()
        for copy in small_copies():
            copy.wait()


def qkv_own_kernel(tbl, low_ref, dqkv_ref, small_ref, got, keep, away, hold, came, came_sems):
    step = pl.program_id(0)

    @pl.when(step == 0)
    def _():
        for copy in arrivals(tbl, got, came, 48, came_sems):
            copy.start()
        for copy in arrivals(tbl, got, came, 48, came_sems):
            copy.wait()

    rows = pl.ds(pl.multiple_of(step * HALF, HALF), HALF)
    cols = pl.ds(pl.multiple_of(tbl[CORE_AT] * TDIM, TDIM), TDIM)
    hold[:, :QKV] = (tn(low_ref[...], dqkv_ref[...]) + came[rows, :QKV].astype(F32)).astype(BF16)
    hold[:, QKV:] = (small_ref[rows, cols].astype(F32) + came[rows, QKV:].astype(F32)).astype(BF16)
    leave(tbl, hold, step * (CHIPS // 2), CHIPS // 2, keep, away, pl.ds(0, QKV + TDIM))


def input_grad_kernel(df_ref, dqkv_ref, w_ref, ig_ref):
    ig_ref[...] = df_ref[...] + nt(dqkv_ref[...], w_ref[...])


def call(kernel, name, grid, in_specs, out_specs, out_shape, scratch, flops, moved, args, prefetch=1, alias=None):
    return pl.pallas_call(
        kernel,
        name=name,
        grid_spec=pltpu.PrefetchScalarGridSpec(
            num_scalar_prefetch=prefetch, grid=grid, in_specs=in_specs, out_specs=out_specs, scratch_shapes=scratch
        ),
        out_shape=out_shape,
        input_output_aliases=alias or {},
        compiler_params=pltpu.CompilerParams(dimension_semantics=("arbitrary",) * len(grid), vmem_limit_bytes=63 << 20),
        cost_estimate=pl.CostEstimate(flops=flops, bytes_accessed=moved, transcendentals=0),
    )(*args)


def rows_spec(rows, cols):
    return pl.BlockSpec((rows, cols), lambda i, *_: (i, 0))


def whole_spec(shape):
    return pl.BlockSpec(shape, lambda i, *_: (0,) * len(shape))


def cols_spec(rows, cols, top):
    return pl.BlockSpec((rows, cols), lambda i, *_: (0, jnp.minimum(i, top)))


def sds(shape, dtype):
    return jax.ShapeDtypeStruct(shape, dtype)


def block_spec(shape, block):
    return pl.BlockSpec(shape, lambda i, *_: (block,) + (0,) * (len(shape) - 1))


def project(tbl, x, pick, embed, pieces):
    rows = x.shape[0]
    slots = pick.shape[1]
    return call(
        project_kernel, "project", (rows // BLOCK,),
        [rows_spec(BLOCK, D), rows_spec(BLOCK, slots), whole_spec((slots, TDIM))] + [ANY] * 4,
        [rows_spec(BLOCK, D), rows_spec(BLOCK, D), rows_spec(BLOCK, 2 * QKV), whole_spec((16, D)), ANY],
        [sds((rows, D), F32), sds((rows, D), BF16), sds((rows, 2 * QKV), BF16), sds((16, D), F32), sds((D, 2 * QKV), BF16)],
        [pltpu.VMEM((D, 2 * QKV + 2 * TDIM), BF16), pltpu.VMEM((1, 2 * QKV), F32), pltpu.VMEM((1, 2 * QKV), F32),
         pltpu.SemaphoreType.DMA((2, 32)), pltpu.SemaphoreType.DMA((1,))],
        6 * rows * D * D, 20 << 20, (tbl, x, pick, embed, *pieces),
    )


def attend(block, qkv, pick, segr, before):
    rows = qkv.shape[0]
    return call(
        functools.partial(attend_kernel, block), "attend", (1,),
        [block_spec((BLOCK, 2 * QKV), block), block_spec((BLOCK, pick.shape[1]), block),
         block_spec((1, 1, BLOCK), block)] + [ANY] * len(before),
        [block_spec((BLOCK, D), block), ANY],
        [sds((rows, D), BF16), sds((rows // BLOCK, HEADS // 2, 4, 256, 256), BF16)],
        [pltpu.VMEM((4, 256, 128), F32), pltpu.VMEM((2, 256, 256), F32), pltpu.VMEM((2, 4, 256, 256), BF16),
         pltpu.SemaphoreType.DMA((2,))],
        4 * BLOCK * D * D, 20 << 20, (qkv, pick, segr, *before), prefetch=0,
        alias={3 + i: i for i in range(len(before))},
    )


def expand(tbl, hidden, mix, vec, upb, up):
    rows = mix.shape[0]
    tile = 256
    return call(
        expand_kernel, "expand", (rows // tile,),
        [rows_spec(tile, D), rows_spec(tile, D), whole_spec((16, D)), whole_spec((1, FF))] + [ANY] * 4,
        [rows_spec(tile, D), rows_spec(tile, 1), rows_spec(tile, FF), rows_spec(tile, FF), rows_spec(tile, D), ANY],
        [sds((rows, D), F32), sds((rows, 1), F32), sds((rows, FF), BF16), sds((rows, FF), BF16), sds((rows, D), BF16),
         sds((D, FF + D), BF16)],
        [pltpu.VMEM((D, FF + D), BF16), pltpu.VMEM((2, tile, D), F32), pltpu.SemaphoreType.DMA((2, 32)),
         pltpu.SemaphoreType.DMA((1,))],
        2 * rows * D * (FF + D), 20 << 20, (tbl, hidden, mix, vec, upb, *up),
    )


def contract(tbl, n1, i1, cot, vec, act, slope, up, pick, down):
    rows = n1.shape[0]
    tile = 256
    slots = pick.shape[1]
    return call(
        contract_kernel, "contract", (rows // tile,),
        [rows_spec(tile, D), rows_spec(tile, 1), rows_spec(tile, D), whole_spec((16, D)), rows_spec(tile, FF),
         rows_spec(tile, FF), ANY, rows_spec(tile, slots)] + [ANY] * 4,
        [rows_spec(tile, D), rows_spec(tile, FF), rows_spec(tile, D), rows_spec(tile, D), rows_spec(tile, D),
         whole_spec((8, D)), whole_spec((1, FF)), whole_spec((slots, D))],
        [sds((rows, D), BF16), sds((rows, FF), BF16), sds((rows, D), BF16), sds((rows, D), F32), sds((rows, D), BF16),
         sds((8, D), F32), sds((1, FF), F32), sds((slots, D), F32)],
        [pltpu.VMEM((FF, D), BF16), pltpu.VMEM((D, FF), BF16), pltpu.VMEM((2, tile, D), F32), pltpu.SemaphoreType.DMA((1, 32)),
         pltpu.SemaphoreType.DMA((1,))],
        6 * rows * D * FF, 20 << 20, (tbl, n1, i1, cot, vec, act, slope, up, pick, *down),
    )


def down_grad(tbl, act, din):
    rows = act.shape[0]
    shape = sds((CHIPS, FF // CHIPS, HALF), BF16)
    return call(
        down_grad_kernel, "down_grad", (4,), [cols_spec(rows, D, 3), whole_spec((rows, D))], [ANY, ANY], [shape, shape],
        [pltpu.VMEM((4, D, D), BF16), pltpu.SemaphoreType.DMA((4, 8))],
        2 * rows * D * FF, 20 << 20, (tbl, act, din),
    )


def up_specs(rows, kind):
    def half(tbl):
        return jnp.where(kind == 0, tbl[CORE_AT], 1 - tbl[CORE_AT])

    return [whole_spec((rows, D)), pl.BlockSpec((rows, D), lambda i, tbl: (0, 2 * half(tbl) + jnp.minimum(i, 1))),
            ANY, ANY]


def up_other(tbl, mlow, dexp, mix, ain):
    rows = mlow.shape[0]
    return call(
        up_other_kernel, "up_other", (3,), up_specs(rows, 1), ANY, sds((CHIPS, 48, 2 * D + HALF), BF16),
        [pltpu.VMEM((3, D, D), BF16), pltpu.VMEM((rows, D), BF16), pltpu.VMEM((rows, HALF), BF16),
         pltpu.SemaphoreType.DMA((3, CHIPS)), pltpu.SemaphoreType.DMA((2,))],
        rows * D * (FF + D), 20 << 20, (tbl, mlow, dexp, mix, ain),
    )


def up_own(tbl, mlow, dexp, mix, ain, got):
    rows = mlow.shape[0]
    shape = sds((CHIPS // 2, 48, 2 * D + HALF), BF16)
    return call(
        up_own_kernel, "up_own", (3,), up_specs(rows, 0) + [ANY], [whole_spec(shape.shape)] * 2, [shape, shape],
        [pltpu.VMEM((D, D), BF16), pltpu.VMEM((D, 2 * D + HALF), BF16), pltpu.VMEM((rows, D), BF16),
         pltpu.VMEM((rows, HALF), BF16), pltpu.SemaphoreType.DMA((CHIPS,)), pltpu.SemaphoreType.DMA((2,))],
        rows * D * (FF + D), 20 << 20, (tbl, mlow, dexp, mix, ain, got),
    )


def qkv_specs(rows, kind):
    def half(tbl):
        return jnp.where(kind == 0, tbl[CORE_AT], 1 - tbl[CORE_AT])

    return [pl.BlockSpec((rows, HALF), lambda i, tbl: (0, i)), pl.BlockSpec((rows, QKV), lambda i, tbl: (0, half(tbl)))]


def qkv_other(tbl, low, dqkv, first, sa, sb, weight, embed, ff, up):
    rows = low.shape[0]
    slots = first.shape[0]
    return call(
        qkv_other_kernel, "qkv_other", (2,),
        qkv_specs(rows, 1) + [whole_spec((slots, D)), whole_spec((slots, 2 * QKV)), whole_spec((slots, 2 * QKV)), ANY,
                              whole_spec((slots, TDIM)), whole_spec((8, D)), whole_spec((4, D))],
        [whole_spec((D, 2 * TDIM)), ANY], [sds((D, 2 * TDIM), BF16), sds((CHIPS, 48, QKV + TDIM), BF16)],
        [pltpu.VMEM((2, HALF, QKV), BF16), pltpu.VMEM((D, 2 * TDIM), BF16), pltpu.VMEM((D, 2 * QKV), BF16),
         pltpu.SemaphoreType.DMA((2, CHIPS // 2)), pltpu.SemaphoreType.DMA((CHIPS,)), pltpu.SemaphoreType.DMA((1,))],
        3 * rows * D * D, 20 << 20, (tbl, low, dqkv, first, sa, sb, weight, embed, ff, up),
    )


def qkv_own(tbl, low, dqkv, small, got):
    rows = low.shape[0]
    shape = sds((CHIPS // 2, 48, QKV + TDIM), BF16)
    return call(
        qkv_own_kernel, "qkv_own", (2,), qkv_specs(rows, 0) + [whole_spec((D, 2 * TDIM)), ANY],
        [whole_spec(shape.shape)] * 2, [shape, shape],
        [pltpu.VMEM((HALF, QKV + TDIM), BF16), pltpu.VMEM((D, QKV + TDIM), BF16), pltpu.SemaphoreType.DMA((CHIPS,))],
        3 * rows * D * D, 20 << 20, (tbl, low, dqkv, small, got),
    )


def attention_backward(block, ain, mix, qkv, probs, weight, pick, before):
    rows = ain.shape[0]
    slots = pick.shape[1]
    return call(
        functools.partial(attention_backward_kernel, block), "attention_backward", (1,),
        [block_spec((BLOCK, D), block), block_spec((BLOCK, D), block), ANY, ANY, pl.BlockSpec((D, D), lambda i, *_: (0, 4)),
         block_spec((BLOCK, slots), block)] + [ANY] * len(before),
        [block_spec((BLOCK, 2 * QKV), block), whole_spec((slots, 2 * QKV))],
        [sds((rows, 2 * QKV), BF16), sds((slots, 2 * QKV), F32)],
        [pltpu.VMEM((BLOCK, D), BF16), pltpu.VMEM((HEADS // 2, 4, 1, 256), F32), pltpu.VMEM((2, 256, 256), F32),
         pltpu.VMEM((BLOCK, 128), F32), pltpu.VMEM((BLOCK, 128), F32), pltpu.VMEM((BLOCK, 2 * QKV), BF16),
         pltpu.VMEM((HEADS // 2, 4, 256, 256), BF16), pltpu.SemaphoreType.DMA((2,))],
        4 * BLOCK * D * D, 20 << 20, (ain, mix, qkv, probs, weight, pick, *before), prefetch=0,
        alias={6 + i: i for i in range(len(before))},
    )


def input_gradient(df, dqkv, weight):
    rows = df.shape[0]
    tile = 256
    return call(
        input_grad_kernel, "input_grad", (rows // tile,),
        [rows_spec(tile, D), rows_spec(tile, 2 * QKV), whole_spec((D, 2 * QKV))], rows_spec(tile, D), sds((rows, D), F32), [],
        6 * rows * D * D, 20 << 20, (df, dqkv, weight), prefetch=0,
    )


def flip(n, even_bit, odd_bit):
    return [(i, i ^ (odd_bit if i & 1 else even_bit)) for i in range(n)]


def tiled_route(n):
    return {"core": flip(n, 1, 1), "z2": flip(n, 16, 16), "z1": flip(n, 8, 8), "a": flip(n, 2, 4), "b": flip(n, 4, 2)}


def tables(n):
    me = lax.axis_index("fsdp")
    core = me % 2
    chips = jnp.arange(CHIPS, dtype=jnp.int32)
    if n == 32:
        here = me // 2

        def order(kind):
            low, high = jnp.where(kind == 0, 1, 2), jnp.where(kind == 0, 2, 1)
            bits = (chips & 1) * 8 + ((chips >> 1) & 1) * 4 + ((chips >> 2) & 1) * low + (chips >> 3) * high
            return here ^ bits

        def place(kind):
            diff = here ^ chips
            x, y = diff & 1, (diff >> 1) & 1
            low, high = jnp.where(kind == 0, x, y), jnp.where(kind == 0, y, x)
            return (diff >> 3) + ((diff >> 2) & 1) * 2 + low * 4 + high * 8

        parts = [order(core), order(1 - core), place(core), place(1 - core)]
    else:
        parts = [chips] * 4
    return jnp.concatenate(parts + [jnp.full((16,), core, jnp.int32)]).astype(jnp.int32)


def own_half(halves, core):
    return jnp.where(core == 0, halves[0], halves[1]), jnp.where(core == 0, halves[1], halves[0])


def tie(*values):
    return lax.optimization_barrier(values)


def follow(first, *values):
    return lax.optimization_barrier((first,) + values)[1:]


def send_on(value, step, n):
    return lax.ppermute(value, "fsdp", perm=tiled_route(n)[step])


def halves_kernel(core_ref, q, k, v, o, up, down, time, columns, mine_a, mine_u, mine_d, theirs):
    core = core_ref[0]
    rows = q.shape[0]

    def half(ref, which, width):
        return ref[:, pl.ds(pl.multiple_of(which * width, 128), width)]

    for which, first in ((core, True), (1 - core, False)):
        tail = jnp.where(which == 0, time[...].astype(F32), columns[...].astype(F32)).astype(BF16)
        a = [half(q, which, HALF), half(k, which, HALF), half(v, which, HALF), tail]
        u = [half(up, which, FF // 2), half(o, which, HALF)]
        d = half(down, which, HALF)
        if first:
            mine_a[...] = jnp.concatenate(a, axis=1)
            mine_u[...] = jnp.concatenate(u, axis=1)
            mine_d[...] = d
        else:
            d = [d[rows * j : rows * j + rows, :] for j in range(d.shape[0] // rows)]
            theirs[...] = jnp.concatenate(a + u + d, axis=1)


def chip_shards(core, q, k, v, o, up, down, time, columns, n):
    rows = q.shape[0]
    down_rows = down.shape[0]
    widths = (QKV + TDIM, FF // 2 + HALF, HALF * down_rows // rows)
    args = (q, k, v, o, up, down, time, columns)
    shapes = [sds((rows, widths[0]), BF16), sds((rows, widths[1]), BF16), sds((down_rows, HALF), BF16), sds((rows, sum(widths)), BF16)]
    mine_a, mine_u, mine_d, theirs = call(
        halves_kernel, "halves", (1,), [whole_spec(item.shape) for item in args], [whole_spec(item.shape) for item in shapes],
        shapes, [], 1 << 10, 1 << 20, (core.reshape(1), *args),
    )
    got = send_on(theirs, "core", n)
    got_d = got[:, widths[0] + widths[1] :]
    got_d = jnp.concatenate([got_d[:, HALF * j : HALF * j + HALF] for j in range(down_rows // rows)], axis=0)
    shards = []
    for mine, came in ((mine_a, got[:, : widths[0]]), (mine_u, got[:, widths[0] : widths[0] + widths[1]]), (mine_d, got_d)):
        shards.append(jnp.concatenate(own_half((mine, came), core), axis=0)[None])
    return shards


def whole_gather(halves, core):
    full = [lax.all_gather(half, "fsdp", axis=0, tiled=True) for half in halves]
    full = [item.reshape(CHIPS, -1, item.shape[1]) for item in full]
    own, other = own_half(full, core)
    middle = CHIPS // 2
    return own[:middle], own[middle:], other[:middle], other[middle:]


def widen(held, step, n):
    return jnp.concatenate([held, send_on(held, step, n)], axis=0)


def add(left, right):
    return (left.astype(F32) + right.astype(F32)).astype(BF16)


def halve(keep, got):
    middle = keep.shape[0] // 2
    return add(keep[:middle], got[:middle]), add(keep[middle:], got[middle:])


def finish(keep, got, n):
    core = lax.axis_index("fsdp") % 2
    total = keep[0].astype(F32) + got[0].astype(F32)
    rows = total.shape[0] // 2
    mine, theirs = own_half((total[:rows], total[rows:]), core)
    got = send_on(theirs.astype(BF16), "core", n).astype(F32)
    return own_half((mine, got), core)


def whole_reduce(own, other, core):
    sums = []
    for item in own_half((own, other), core):
        item = item.reshape(-1, item.shape[2])
        sums.append(lax.psum_scatter(item, "fsdp", scatter_dimension=0, tiled=True).astype(F32))
    return sums


def sinusoid(steps):
    half = TDIM // 2
    freqs = jnp.exp(-math.log(10000.0) * jnp.arange(half, dtype=F32) / half)
    angles = steps.astype(F32)[:, None] * freqs[None, :]
    return jnp.concatenate([jnp.cos(angles), jnp.sin(angles)], axis=1)


def body(
    inputs, cotangent, lengths, timesteps, time_weight, time_bias, query_weight, query_bias, key_weight,
    value_weight, value_bias, out_weight, out_bias, mid_gain, mid_shift, up_weight, up_bias, down_weight,
    down_bias, last_gain, last_shift,
):
    n = lax.axis_size("fsdp")
    rows = inputs.shape[0]
    blocks = rows // BLOCK
    tbl = tables(n)
    shard = D // n

    vectors = [query_bias, value_bias, out_bias, mid_gain, mid_shift, down_bias, last_gain, last_shift, time_bias]
    vectors += [up_bias[shard * k : shard * (k + 1)] for k in range(FF // D)]
    lane = lax.broadcasted_iota(jnp.int32, (shard, TDIM), 1)
    columns = jnp.zeros((shard, TDIM), F32)
    for k, item in enumerate(vectors):
        columns = jnp.where(lane == k, item.astype(F32)[:, None], columns)
    columns = columns.astype(BF16)
    small_halves = [time_weight.T, columns]
    attn_halves = [
        jnp.concatenate(
            [w[:, HALF * h : HALF * h + HALF] for w in (query_weight, key_weight, value_weight)] + [small_halves[h]], axis=1
        )
        for h in range(2)
    ]
    up_halves = [
        jnp.concatenate([up_weight[:, FF // 2 * h : FF // 2 * (h + 1)], out_weight[:, HALF * h : HALF * h + HALF]], axis=1)
        for h in range(2)
    ]
    down_halves = [down_weight[:, :HALF], down_weight[:, HALF:]]

    core = lax.axis_index("fsdp") % 2
    tiled = n == 32

    def slot_arrays(lengths, timesteps):
        ends = jnp.cumsum(lengths, axis=1)
        position = jnp.arange(BLOCK, dtype=jnp.int32)
        owner = jnp.sum((position[None, :, None] >= ends[:, None, :]).astype(jnp.int32), axis=2)
        slot_of = (owner + SLOTS * jnp.arange(blocks, dtype=jnp.int32)[:, None]).reshape(rows, 1)
        pick = (slot_of == lax.broadcasted_iota(jnp.int32, (rows, blocks * SLOTS), 1)).astype(BF16)
        segr = slot_of.reshape(blocks, 1, BLOCK).astype(F32)
        embed_in = sinusoid(timesteps.reshape(-1)).astype(BF16)
        return pick, segr, embed_in

    if tiled:
        a0, u0, d0 = chip_shards(
            core, query_weight, key_weight, value_weight, out_weight, up_weight, down_weight, time_weight.T, columns, n
        )
        a0 = widen(a0, "z2", n)
        pick, segr, embed_in = slot_arrays(*follow(a0, lengths, timesteps))
        a0 = widen(a0, "z1", n)
        (u0,) = follow(a0, u0)
        a0 = widen(a0, "a", n)
        u0 = widen(u0, "z2", n)
        a0, u0 = tie(a0, u0)
        a1 = send_on(a0, "b", n)
        a2 = send_on(a0, "core", n)
        u0 = widen(u0, "z1", n)
        a1, u0, d0, tbl, pick, segr, embed_in = tie(a1, u0, d0, tbl, pick, segr, embed_in)
        a3 = send_on(a1, "core", n)
        u_got = send_on(u0, "a", n)
        d_got = send_on(d0, "z2", n)
        hidden, low, qkv, vec, weight = project(tbl, inputs, pick, embed_in, (a0, a1, a2, a3))
        qkv, u0, u_got, d0, d_got = tie(qkv, u0, u_got, d0, d_got)
        u0 = jnp.concatenate([u0, u_got], axis=0)
        d0 = jnp.concatenate([d0, d_got], axis=0)
        u1 = send_on(u0, "b", n)
        d_got = send_on(d0, "z1", n)
        u2 = send_on(u0, "core", n)
        parts = attend(0, qkv, pick, segr, ())
        *parts, qkv, u0, u2, d0, d_got = tie(*parts, qkv, u0, u2, d0, d_got)
        d0 = jnp.concatenate([d0, d_got], axis=0)
        d_got = send_on(d0, "a", n)
        mix, probs = attend(1, qkv, pick, segr, parts)
        mix, u1, d0, d_got = tie(mix, u1, d0, d_got)
        u3 = send_on(u1, "core", n)
        d0 = jnp.concatenate([d0, d_got], axis=0)
        d1 = send_on(d0, "b", n)
        d2 = send_on(d0, "core", n)
        up_offset = vec[9:13].reshape(FF // D, n, shard).transpose(1, 0, 2).reshape(1, FF)
        n1, i1, act, slope, mlow, up_full = expand(tbl, hidden, mix, vec, up_offset, (u0, u1, u2, u3))
        act, d1 = tie(act, d1)
        d3 = send_on(d1, "core", n)
        down_pieces = (d0, d1, d2, d3)
    else:
        pick, segr, embed_in = slot_arrays(lengths, timesteps)
        hidden, low, qkv, vec, weight = project(tbl, inputs, pick, embed_in, whole_gather(attn_halves, core))
        mix, probs = attend(1, qkv, pick, segr, attend(0, qkv, pick, segr, ()))
        up_offset = vec[9:13].reshape(FF // D, n, shard).transpose(1, 0, 2).reshape(1, FF)
        n1, i1, act, slope, mlow, up_full = expand(tbl, hidden, mix, vec, up_offset, whole_gather(up_halves, core))
        down_pieces = whole_gather(down_halves, core)

    res, dexp, din, df, ain, ff_vecs, up_vec, slot_first = contract(
        tbl, n1, i1, cotangent, vec, act, slope, up_full, pick, down_pieces
    )
    up_vec = up_vec.reshape(n, FF // D, shard).transpose(1, 0, 2).reshape(FF // D, D)
    d_own, d_other = down_grad(tbl, act, din)
    mlow, d_own, d_other = tie(mlow, d_own, d_other)
    u_other = up_other(tbl, mlow, dexp, mix, ain)
    if tiled:
        d_got = send_on(d_other, "core", n)
        u_other, d_own, d_got, mlow, up_vec = tie(u_other, d_own, d_got, mlow, up_vec)
        u_got = send_on(u_other, "core", n)
        d_keep, d_away = halve(d_own, d_got)
        d_keep, d_away, u_got = tie(d_keep, d_away, u_got)
        d_got = send_on(d_away, "b", n)
        u_keep, u_away = up_own(tbl, mlow, dexp, mix, ain, u_got)
        ain, u_keep, u_away = tie(ain, u_keep, u_away)
        u_got = send_on(u_away, "b", n)
        dqkv, slot0 = attention_backward(0, ain, mix, qkv, probs, up_full, pick, ())
        dqkv, d_keep, d_got = tie(dqkv, d_keep, d_got)
        d_keep, d_away = halve(d_keep, d_got)
        ain, dqkv, d_keep, d_away = tie(ain, dqkv, d_keep, d_away)
        d_got = send_on(d_away, "a", n)
        dqkv, slot1 = attention_backward(1, ain, mix, qkv, probs, up_full, pick, (dqkv,))
        dqkv, d_keep, d_got, u_keep, u_got = tie(dqkv, d_keep, d_got, u_keep, u_got)
        u_keep, u_away = halve(u_keep, u_got)
        d_keep, d_away = halve(d_keep, d_got)
        low, dqkv, d_keep, d_away, u_keep, u_away = tie(low, dqkv, d_keep, d_away, u_keep, u_away)
        u_got = send_on(u_away, "a", n)
        d_got = send_on(d_away, "z1", n)
        small, q_other = qkv_other(
            tbl, low, dqkv, slot_first, slot0, slot1, weight, embed_in, ff_vecs, up_vec
        )
        q_other, u_keep, u_got, d_keep, d_got, low = tie(q_other, u_keep, u_got, d_keep, d_got, low)
        q_got = send_on(q_other, "core", n)
        u_keep, u_away = halve(u_keep, u_got)
        d_keep, d_away = halve(d_keep, d_got)
        q_got, u_keep, u_away, d_keep, d_away = tie(q_got, u_keep, u_away, d_keep, d_away)
        u_got = send_on(u_away, "z1", n)
        q_keep, q_away = qkv_own(tbl, low, dqkv, small, q_got)
        df, q_keep, q_away, u_keep, u_got = tie(df, q_keep, q_away, u_keep, u_got)
        q_got = send_on(q_away, "b", n)
        u_keep, u_away = halve(u_keep, u_got)
        df, d_away, u_keep, u_away = tie(df, d_away, u_keep, u_away)
        d_got = send_on(d_away, "z2", n)
        u_got = send_on(u_away, "z2", n)
        input_grad = input_gradient(df, dqkv, weight)
        input_grad, q_keep, q_got = tie(input_grad, q_keep, q_got)
        q_keep, q_away = halve(q_keep, q_got)
        u_keep, u_got, d_keep, d_got = follow(q_away, u_keep, u_got, d_keep, d_got)
        q_got = send_on(q_away, "a", n)
        down_sum = finish(d_keep, d_got, n)
        q_keep, q_away = halve(q_keep, q_got)
        q_got = send_on(q_away, "z1", n)
        up_sum = finish(u_keep, u_got, n)
        q_keep, q_away = halve(q_keep, q_got)
        q_got = send_on(q_away, "z2", n)
        qkv_sum = finish(q_keep, q_got, n)
    else:
        dqkv, slot0 = attention_backward(0, ain, mix, qkv, probs, up_full, pick, ())
        dqkv, slot1 = attention_backward(1, ain, mix, qkv, probs, up_full, pick, (dqkv,))
        small, q_other = qkv_other(
            tbl, low, dqkv, slot_first, slot0, slot1, weight, embed_in, ff_vecs, up_vec
        )
        input_grad = input_gradient(df, dqkv, weight)
        down_sum = whole_reduce(d_own, d_other, core)
        zero_u, zero_q = jnp.zeros_like(u_other), jnp.zeros_like(q_other)
        u_own = jnp.concatenate(up_own(tbl, mlow, dexp, mix, ain, zero_u), axis=0)
        q_own = jnp.concatenate(qkv_own(tbl, low, dqkv, small, zero_q), axis=0)
        up_sum = whole_reduce(u_own, u_other, core)
        qkv_sum = whole_reduce(q_own, q_other, core)
    def both(pair, start, stop):
        return jnp.concatenate([half[:, start:stop] for half in pair], axis=1)

    out_query = both(qkv_sum, 0, HALF)
    out_key = both(qkv_sum, HALF, 2 * HALF)
    out_value = both(qkv_sum, 2 * HALF, QKV)
    out_up = both(up_sum, 0, 2 * D)
    out_out = both(up_sum, 2 * D, 2 * D + HALF)
    out_down = both(down_sum, 0, HALF)
    out_time = qkv_sum[0][:, QKV:].T
    v = qkv_sum[1][:, QKV : QKV + 13].T
    v_up = v[9:13].reshape(-1)
    return (
        res, input_grad, out_time, out_query, out_key, out_value, out_out, out_up, out_down,
        v[0], v[1], v[2], v[8], v[6], v[7], v_up, v[5], v[3], v[4],
    )


def solution(mesh):
    row, col, vec = P("fsdp", None), P(None, "fsdp"), P("fsdp")
    in_specs = (
        row, row, row, row, col, vec, row, vec, row, row, vec, row, vec, vec, vec, row, vec, row, vec, vec, vec,
    )
    out_specs = (row, row, col, row, row, row, row, row, row) + (vec,) * 10
    return jax.shard_map(body, mesh=mesh, in_specs=in_specs, out_specs=out_specs, check_vma=False)
```

```python
import functools
import math

import jax
import jax.numpy as jnp
from jax import lax
from jax.experimental import pallas as pl
from jax.experimental.pallas import tpu as pltpu
from jax.sharding import PartitionSpec as P

D = 768
HEAD = 64
HEADS = 12
FF = 3072
TDIM = 128
SLOTS = 8
BLOCK = 512
HALF = D // 2
QKV = 3 * HALF
CHIPS = 16
EPS = 1e-05
NEG = -1e30
HIGH = lax.Precision.HIGHEST
SQRT_HALF = 0.7071067811865476
INV_ROOT_TAU = 0.3989422804014327
HALF_LOG = -0.5 / math.log(2.0)
WINDOWS = (0, 64, 192, 256)
F32 = jnp.float32
BF16 = jnp.bfloat16
ANY = pl.BlockSpec(memory_space=pl.ANY)
OWN_ROW, OTHER_ROW, OWN_POS, OTHER_POS, CORE_AT = 0, 16, 32, 48, 64


def nn(left, right):
    return lax.dot_general(left, right, (((1,), (0,)), ((), ())), preferred_element_type=F32)


def nt(left, right):
    return lax.dot_general(left, right, (((1,), (1,)), ((), ())), preferred_element_type=F32)


def tn(left, right):
    return lax.dot_general(left, right, (((0,), (0,)), ((), ())), preferred_element_type=F32)


def in_halves(product, left, right):
    middle = left.shape[0] // 2
    return jnp.concatenate([product(left[:middle], right), product(left[middle:], right)], axis=0)


def mean(values):
    return jnp.sum(values, axis=-1, keepdims=True) * (1.0 / D)


def normalize(values):
    center = values - mean(values)
    inverse = lax.rsqrt(mean(center * center) + EPS)
    return center * inverse, inverse


def norm_back(grad, normed, inverse):
    return inverse * (grad - mean(grad) - normed * mean(grad * normed))


def column_sum(values):
    return jnp.sum(values, axis=0, keepdims=True)


def piece_copies(tbl, refs, weight, sems, rows, parts):
    own_low, own_high, other_low, other_high = refs
    core = tbl[CORE_AT]
    copies = []
    for kind, (low, high) in enumerate(((own_low, own_high), (other_low, other_high))):
        half = core if kind == 0 else 1 - core
        for j in range(CHIPS):
            piece = (low if j < CHIPS // 2 else high).at[j % (CHIPS // 2)]
            at = pl.ds(pl.multiple_of(tbl[kind * CHIPS + j] * rows, rows), rows)
            for k, (start, width, base) in enumerate(parts):
                cols = pl.ds(pl.multiple_of(base + half * width, 128), width)
                copies.append(
                    pltpu.make_async_copy(piece.at[:, pl.ds(start, width)], weight.at[at, cols], sems.at[k, kind * CHIPS + j])
                )
    return copies


def lane_masks():
    lane = lax.broadcasted_iota(jnp.int32, (1, 2 * HEAD), 1)
    first = jnp.where(lane < HEAD, 1.0, 0.0)
    return first.astype(BF16), (1.0 - first).astype(BF16), lane < HEAD


def split_bf16(values):
    high = values.astype(BF16)
    rest = values - high.astype(F32)
    return high, rest.astype(BF16), rest


def with_slots(x_ref, pick_ref, slots):
    high, middle, rest = split_bf16(slots)
    low = (rest - middle.astype(F32)).astype(BF16)
    picks = pick_ref[...]
    slot = nn(jnp.concatenate([picks, picks, picks], axis=1), jnp.concatenate([high, middle, low], axis=0))
    return x_ref[...].astype(F32) + slot


def project_kernel(
    tbl, x_ref, pick_ref, embed_ref, own_low, own_high, other_low, other_high,
    low_ref, qkv_ref, vec_ref, slots_ref, w_ref, weight, offset, factor, sems, out_sem,
):
    step = pl.program_id(0)
    save = pltpu.make_async_copy(weight.at[:, pl.ds(0, 2 * QKV)], w_ref, out_sem.at[0])

    @pl.when(step == 0)
    def _():
        parts = ((0, QKV, 0), (QKV, TDIM, 2 * QKV))
        copies = piece_copies(tbl, (own_low, own_high, other_low, other_high), weight, sems, 48, parts)
        for copy in copies:
            copy.start()
        for copy in copies:
            copy.wait()
        save.start()
        vec_ref[...] = weight[:, 2 * QKV + TDIM :].astype(F32).T[:16, :]
        offset[...] = jnp.zeros_like(offset)
        factor[...] = jnp.ones_like(factor)
        for half in range(2):
            cols = slice(HALF * half, HALF * half + HALF)
            at = QKV * half
            offset[:, at : at + HALF] = vec_ref[0:1, cols]
            offset[:, at + 2 * HALF : at + QKV] = vec_ref[1:2, cols]
            factor[:, at : at + HALF] = jnp.full((1, HALF), HEAD**-0.5, F32)

    slots = nt(embed_ref[...], weight[:, 2 * QKV : 2 * QKV + TDIM]) + vec_ref[8:9, :]
    slots_ref[...] = slots
    low_ref[...] = with_slots(x_ref, pick_ref, slots).astype(BF16)

    for j in range(3):
        at = slice(j * D, j * D + D)
        y = nn(low_ref[...], weight[:, at]) + offset[:, at]
        qkv_ref[:, at] = (y.astype(BF16).astype(F32) * factor[:, at]).astype(BF16)

    @pl.when(step == pl.num_programs(0) - 1)
    def _():
        save.wait()


def attend_kernel(block, qkv_ref, pick_ref, segr_ref, *rest):
    mix_ref, probs_ref, bias, scores, held, sems = rest[-6:]
    slot = lax.broadcasted_iota(jnp.int32, pick_ref.shape, 1).astype(F32)
    owner = jnp.sum(pick_ref[...].astype(F32) * slot, axis=1, keepdims=True)
    for t in range(4):
        same = owner[WINDOWS[t] : WINDOWS[t] + 256, :] == segr_ref[0, :, 128 * t : 128 * t + 128]
        bias[t] = jnp.where(same, 0.0, NEG)
    first, second, _ = lane_masks()

    def operands(p, t):
        at = pl.multiple_of((p // 3) * QKV + (p % 3) * 128, 128)
        window = slice(WINDOWS[t], WINDOWS[t] + 256)
        return at, window

    def scores_of(p, t):
        at, window = operands(p, t)
        q = qkv_ref[128 * t : 128 * t + 128, pl.ds(at, 128)]
        k = qkv_ref[window, pl.ds(at + HALF, 128)]
        both = jnp.concatenate([q * first, q * second], axis=0)
        s = in_halves(nt, k, both) + jnp.concatenate([bias[t], bias[t]], axis=1)
        scores[t % 2] = s
        return jnp.max(s, axis=0, keepdims=True)

    def out_copy(p):
        return pltpu.make_async_copy(held.at[p % 2], probs_ref.at[block, p], sems.at[p % 2])

    def pair(p, peak):
        @pl.when(p >= 2)
        def _():
            out_copy(p - 2).wait()

        for t in range(4):
            ahead = scores_of(p, t + 1) if t < 3 else scores_of(jnp.minimum(p + 1, HEADS // 2 - 1), 0)
            at, window = operands(p, t)
            v = qkv_ref[window, pl.ds(at + 2 * HALF, 128)]
            e = jnp.exp(scores[t % 2] - peak)
            probs = (e * (1.0 / jnp.sum(e, axis=0, keepdims=True))).astype(BF16)
            held[p % 2, t] = probs
            turned = v.T
            out = jnp.concatenate([nn(turned[:HEAD], probs[:, :128]), nn(turned[HEAD:], probs[:, 128:])], axis=0)
            mix_ref[128 * t : 128 * t + 128, pl.ds(pl.multiple_of(p * 128, 128), 128)] = out.T.astype(BF16)
            peak = ahead
        out_copy(p).start()
        return peak

    lax.fori_loop(0, HEADS // 2, pair, scores_of(0, 0))
    out_copy(HEADS // 2 - 2).wait()
    out_copy(HEADS // 2 - 1).wait()

def expand_kernel(
    tbl, x_ref, pick_ref, slots_ref, mix_ref, vec_ref, upb_ref, ua, ub, uc, ud,
    n1_ref, i1_ref, act_ref, slope_ref, mlow_ref, up_ref, up, wide, sems, out_sem,
):
    step = pl.program_id(0)
    save = pltpu.make_async_copy(up, up_ref, out_sem.at[0])
    both = piece_copies(tbl, (ua, ub, uc, ud), up, sems, 48, ((FF // 2, HALF, FF), (0, FF // 2, 0)))
    copies = both[0::2], both[1::2]

    @pl.when(step == 0)
    def _():
        for copy in copies[0] + copies[1]:
            copy.start()
        for copy in copies[0]:
            copy.wait()

    normed, inverse = normalize(with_slots(x_ref, pick_ref, slots_ref[...]) + nn(mix_ref[...], up[:, FF:]) + vec_ref[2:3, :])
    n1_ref[...] = normed
    i1_ref[...] = inverse
    mlow_ref[...] = (normed * vec_ref[3:4, :] + vec_ref[4:5, :]).astype(BF16)

    def expand(j):
        at = slice(j * D, j * D + D)
        wide[j % 2] = nn(mlow_ref[...], up[:, at]) + upb_ref[:, at]

    def activate(j):
        at = slice(j * D, j * D + D)
        u = wide[j % 2]
        scaled = u * SQRT_HALF
        twice = 1.0 + lax.erf(scaled)
        act_ref[:, at] = ((u * 0.5) * twice).astype(BF16)
        slope_ref[:, at] = (0.5 * twice + (u * INV_ROOT_TAU) * jnp.exp2((u * u) * HALF_LOG)).astype(BF16)

    @pl.when(step == 0)
    def _():
        for copy in copies[1]:
            copy.wait()
        save.start()

    expand(0)
    for j in range(FF // D):
        if j + 1 < FF // D:
            expand(j + 1)
        activate(j)

    @pl.when(step == pl.num_programs(0) - 1)
    def _():
        save.wait()


def contract_kernel(
    tbl, n1_ref, i1_ref, cot_ref, vec_ref, act_ref, slope_ref, up_ref, pick_ref, da, db, dc, dd,
    res_ref, dexp_ref, din_ref, df_ref, ain_ref, vg_ref, gup_ref, slot_ref, down, up, wide, sems, up_sem,
):
    step = pl.program_id(0)
    fetch = pltpu.make_async_copy(up_ref.at[:, pl.ds(0, FF)], up, up_sem.at[0])

    @pl.when(step == 0)
    def _():
        copies = piece_copies(tbl, (da, db, dc, dd), down, sems, FF // CHIPS, ((0, HALF, 0),))
        for copy in copies:
            copy.start()
        for copy in copies:
            copy.wait()
        fetch.start()
        vg_ref[...] = jnp.zeros_like(vg_ref)
        gup_ref[...] = jnp.zeros_like(gup_ref)
        slot_ref[...] = jnp.zeros_like(slot_ref)

    def vec(i):
        return vec_ref[i : i + 1, :]

    second = n1_ref[...] * vec(3) + vec(4) + nn(act_ref[...], down[...]) + vec(5)
    normed2, inverse2 = normalize(second)
    res_ref[...] = (normed2 * vec(6) + vec(7)).astype(BF16)
    upstream = cot_ref[...].astype(F32)
    vg_ref[0:1, :] += column_sum(upstream * normed2)
    vg_ref[1:2, :] += column_sum(upstream)
    d_second = norm_back(upstream * vec(6), normed2, inverse2)
    down_in = d_second.astype(BF16)
    din_ref[...] = down_in
    vg_ref[2:3, :] += column_sum(down_in.astype(F32))

    def contract(j):
        wide[j % 2] = nt(din_ref[...], down[j * D : j * D + D, :])

    @pl.when(step == 0)
    def _():
        fetch.wait()

    contract(0)
    for j in range(FF // D):
        if j + 1 < FF // D:
            contract(j + 1)
        at = slice(j * D, j * D + D)
        d_exp = (wide[j % 2] * slope_ref[:, at].astype(F32)).astype(BF16)
        dexp_ref[:, at] = d_exp
        gup_ref[:, at] += column_sum(d_exp.astype(F32))
    d_middle = nt(dexp_ref[...], up[...]) + d_second
    normed1 = n1_ref[...]
    vg_ref[3:4, :] += column_sum(d_middle * normed1)
    vg_ref[4:5, :] += column_sum(d_middle)
    d_first = norm_back(d_middle * vec(3), normed1, i1_ref[...])
    df_ref[...] = d_first
    attn_in = d_first.astype(BF16)
    ain_ref[...] = attn_in
    vg_ref[5:6, :] += column_sum(attn_in.astype(F32))
    rest = (d_first - attn_in.astype(F32)).astype(BF16)
    slot_ref[...] += tn(pick_ref[...], attn_in) + tn(pick_ref[...], rest)


def down_grad_kernel(tbl, act_ref, din_ref, own, other, hold, sems):
    step = pl.program_id(0)
    core = tbl[CORE_AT]
    rows = FF // CHIPS
    hold[step] = tn(act_ref[...], din_ref[...]).astype(BF16)

    def copies(j):
        made = []
        for k in range(4):
            chip = 4 * j + k
            for kind, (target, table) in enumerate(((own, OWN_POS), (other, OTHER_POS))):
                half = core if kind == 0 else 1 - core
                src = hold.at[j, pl.ds(k * rows, rows), pl.ds(pl.multiple_of(half * HALF, HALF), HALF)]
                made.append(pltpu.make_async_copy(src, target.at[tbl[table + chip]], sems.at[j, 2 * k + kind]))
        return made

    for copy in copies(step):
        copy.start()

    @pl.when(step == pl.num_programs(0) - 1)
    def _():
        for j in range(4):
            for copy in copies(j):
                copy.wait()


def product_for(step, half, mlow_ref, dexp_ref, mix_all, ain_all, mix, ain, sems, give):
    fetches = [
        pltpu.make_async_copy(mix_all, mix, sems.at[0]),
        pltpu.make_async_copy(ain_all.at[:, pl.ds(pl.multiple_of(half * HALF, HALF), HALF)], ain, sems.at[1]),
    ]

    @pl.when(step == 0)
    def _():
        for fetch in fetches:
            fetch.start()

    @pl.when(step < 2)
    def _():
        give(tn(mlow_ref[...], dexp_ref[...]), pl.ds(pl.multiple_of(step * D, D), D), D)

    @pl.when(step == 2)
    def _():
        for fetch in fetches:
            fetch.wait()
        give(tn(mix[...], ain[...]), pl.ds(2 * D, HALF), HALF)


def up_other_kernel(tbl, mlow_ref, dexp_ref, mix_all, ain_all, other, hold, mix, ain, sems, fetch_sems):
    step = pl.program_id(0)

    def copies(j, width):
        made = []
        for chip in range(CHIPS):
            src = hold.at[j, pl.ds(48 * chip, 48), pl.ds(0, width)]
            cols = pl.ds(pl.multiple_of(j * D, D), width)
            made.append(pltpu.make_async_copy(src, other.at[tbl[OTHER_POS + chip], :, cols], sems.at[j, chip]))
        return made

    def give(grad, cols, width):
        hold[step, :, :width] = grad.astype(BF16)
        for copy in copies(step, width):
            copy.start()

    product_for(step, 1 - tbl[CORE_AT], mlow_ref, dexp_ref, mix_all, ain_all, mix, ain, fetch_sems, give)

    @pl.when(step == 2)
    def _():
        for j in range(3):
            for copy in copies(j, D if j < 2 else HALF):
                copy.wait()


def arrivals(tbl, got, came, rows, sems):
    made = []
    for chip in range(CHIPS):
        dst = came.at[pl.ds(rows * chip, rows), :]
        made.append(pltpu.make_async_copy(got.at[tbl[OWN_POS + chip]], dst, sems.at[chip]))
    return made


def leave(tbl, src, first, count, keep, away, cols):
    def one(k, carry):
        at = tbl[OWN_POS + first + k]
        rows = src[pl.ds(pl.multiple_of(48 * k, 48), 48), :]

        @pl.when(at < CHIPS // 2)
        def _():
            keep[at, :, cols] = rows

        @pl.when(at >= CHIPS // 2)
        def _():
            away[at - CHIPS // 2, :, cols] = rows

        return carry

    lax.fori_loop(0, count, one, 0)


def up_own_kernel(tbl, mlow_ref, dexp_ref, mix_all, ain_all, got, keep, away, hold, came, mix, ain, came_sems, fetch_sems):
    step = pl.program_id(0)

    @pl.when(step == 0)
    def _():
        for copy in arrivals(tbl, got, came, 48, came_sems):
            copy.start()
        for copy in arrivals(tbl, got, came, 48, came_sems):
            copy.wait()

    def give(grad, cols, width):
        hold[:, :width] = (grad + came[:, cols].astype(F32)).astype(BF16)
        leave(tbl, hold.at[:, pl.ds(0, width)], 0, CHIPS, keep, away, cols)

    product_for(step, tbl[CORE_AT], mlow_ref, dexp_ref, mix_all, ain_all, mix, ain, fetch_sems, give)


def attention_backward_kernel(block, ain_ref, mix_ref, qkv_all, probs_all, w_ref, pick_ref, *rest):
    dqkv_ref, slot_ref, d_mix, delta, d_probs, dk, dv, qkv_ref, probs_ref, sems = rest[-10:]
    fetches = [
        pltpu.make_async_copy(qkv_all.at[pl.ds(block * BLOCK, BLOCK), :], qkv_ref, sems.at[0]),
        pltpu.make_async_copy(probs_all.at[block], probs_ref, sems.at[1]),
    ]
    for fetch in fetches:
        fetch.start()
    d_mix[...] = nt(ain_ref[...], w_ref[...]).astype(BF16)
    product = d_mix[...].astype(F32) * mix_ref[...].astype(F32)
    high, low, _ = split_bf16(product)
    head = lax.broadcasted_iota(jnp.int32, (16, D), 0)
    column = lax.broadcasted_iota(jnp.int32, (16, D), 1)
    ones = jnp.where(column // HEAD == head, 1.0, 0.0).astype(BF16)
    dots = nt(ones, high) + nt(ones, low)
    for p in range(HEADS // 2):
        for t in range(4):
            rows = slice(128 * t, 128 * t + 128)
            delta[p, t] = jnp.concatenate([dots[2 * p : 2 * p + 1, rows], dots[2 * p + 1 : 2 * p + 2, rows]], axis=1)
    first, second, choose = lane_masks()

    def offsets(p):
        return pl.multiple_of((p // 3) * QKV + (p % 3) * 128, 128)

    def outs_of(p, t):
        do = d_mix[128 * t : 128 * t + 128, pl.ds(pl.multiple_of(p * 128, 128), 128)]
        return jnp.concatenate([do * first, do * second], axis=0)

    def d_probs_of(p, t):
        v = qkv_ref[WINDOWS[t] : WINDOWS[t] + 256, pl.ds(offsets(p) + 2 * HALF, 128)]
        d_probs[t % 2] = in_halves(nt, v, outs_of(p, t))

    def pair(p, carry):
        at = offsets(p)
        dk[...] = jnp.zeros_like(dk)
        dv[...] = jnp.zeros_like(dv)
        for t in range(4):
            if t < 3:
                d_probs_of(p, t + 1)
            else:
                d_probs_of(jnp.minimum(p + 1, HEADS // 2 - 1), 0)
            window = slice(WINDOWS[t], WINDOWS[t] + 256)
            q = qkv_ref[128 * t : 128 * t + 128, pl.ds(at, 128)]
            k = qkv_ref[window, pl.ds(at + HALF, 128)]
            queries = jnp.concatenate([q * first, q * second], axis=0)
            probs = probs_ref[p, t]
            dv[window, :] += in_halves(nn, probs, outs_of(p, t))
            scores = (probs.astype(F32) * (d_probs[t % 2] - delta[p, t])).astype(BF16)
            dk[window, :] += in_halves(nn, scores, queries)
            dq = jnp.where(choose, tn(scores[:, :128], k), tn(scores[:, 128:], k)) * HEAD**-0.5
            dqkv_ref[128 * t : 128 * t + 128, pl.ds(at, 128)] = dq.astype(BF16)
        dqkv_ref[:, pl.ds(at + HALF, 128)] = dk[...].astype(BF16)
        dqkv_ref[:, pl.ds(at + 2 * HALF, 128)] = dv[...].astype(BF16)
        return carry

    for fetch in fetches:
        fetch.wait()
    d_probs_of(0, 0)
    lax.fori_loop(0, HEADS // 2, pair, 0)
    slot_ref[...] = tn(pick_ref[...], dqkv_ref[...])


def small_grads(first_ref, sa_ref, sb_ref, w_ref, embed_ref, ff_ref, up_ref):
    second = sa_ref[...] + sb_ref[...]
    high, low, _ = split_bf16(second)
    biases = column_sum(second)
    query = jnp.concatenate([biases[:, :HALF], biases[:, QKV : QKV + HALF]], axis=1)
    value = jnp.concatenate([biases[:, 2 * HALF : QKV], biases[:, QKV + 2 * HALF :]], axis=1)
    both = nt(jnp.concatenate([high, low], axis=0), w_ref[...])
    slots = first_ref[...] + both[: high.shape[0]] + both[high.shape[0] :]
    slot_low = slots.astype(BF16)
    rows = [column_sum(slot_low.astype(F32)), query, value, ff_ref[0:6, :], up_ref[0:4, :]]
    rows.append(jnp.zeros((TDIM - 13, D), F32))
    vectors = jnp.concatenate(rows, axis=0).T
    return jnp.concatenate([tn(slot_low, embed_ref[...]), vectors], axis=1).astype(BF16)


def qkv_other_kernel(
    tbl, low_ref, dqkv_ref, first_ref, sa_ref, sb_ref, w_all, embed_ref, ff_ref, up_ref,
    small_ref, other, hold, extra, w_ref, sems, small_sems, w_sem,
):
    step = pl.program_id(0)
    off = 1 - tbl[CORE_AT]

    def small_copies():
        made = []
        for chip in range(CHIPS):
            src = extra.at[pl.ds(48 * chip, 48), pl.ds(pl.multiple_of(off * TDIM, TDIM), TDIM)]
            dst = other.at[tbl[OTHER_POS + chip], :, pl.ds(QKV, TDIM)]
            made.append(pltpu.make_async_copy(src, dst, small_sems.at[chip]))
        return made

    fetch = pltpu.make_async_copy(w_all, w_ref, w_sem.at[0])

    @pl.when(step == 0)
    def _():
        fetch.start()

    @pl.when(step == 1)
    def _():
        fetch.wait()
        small = small_grads(first_ref, sa_ref, sb_ref, w_ref, embed_ref, ff_ref, up_ref)
        small_ref[...] = small
        extra[...] = small
        for copy in small_copies():
            copy.start()

    hold[step] = tn(low_ref[...], dqkv_ref[...]).astype(BF16)

    def copies(j):
        made = []
        for k in range(CHIPS // 2):
            src = hold.at[j, pl.ds(48 * k, 48), :]
            at = tbl[OTHER_POS + j * (CHIPS // 2) + k]
            made.append(pltpu.make_async_copy(src, other.at[at, :, pl.ds(0, QKV)], sems.at[j, k]))
        return made

    for copy in copies(step):
        copy.start()

    @pl.when(step == 1)
    def _():
        for j in range(2):
            for copy in copies(j):
                copy.wait()
        for copy in small_copies():
            copy.wait()


def qkv_own_kernel(tbl, low_ref, dqkv_ref, small_ref, got, keep, away, hold, came, came_sems):
    step = pl.program_id(0)

    @pl.when(step == 0)
    def _():
        for copy in arrivals(tbl, got, came, 48, came_sems):
            copy.start()
        for copy in arrivals(tbl, got, came, 48, came_sems):
            copy.wait()

    rows = pl.ds(pl.multiple_of(step * HALF, HALF), HALF)
    cols = pl.ds(pl.multiple_of(tbl[CORE_AT] * TDIM, TDIM), TDIM)
    hold[:, :QKV] = (tn(low_ref[...], dqkv_ref[...]) + came[rows, :QKV].astype(F32)).astype(BF16)
    hold[:, QKV:] = (small_ref[rows, cols].astype(F32) + came[rows, QKV:].astype(F32)).astype(BF16)
    leave(tbl, hold, step * (CHIPS // 2), CHIPS // 2, keep, away, pl.ds(0, QKV + TDIM))


def input_grad_kernel(df_ref, dqkv_ref, w_ref, ig_ref):
    ig_ref[...] = df_ref[...] + nt(dqkv_ref[...], w_ref[...])


def call(kernel, name, grid, in_specs, out_specs, out_shape, scratch, flops, moved, args, prefetch=1, alias=None):
    return pl.pallas_call(
        kernel,
        name=name,
        grid_spec=pltpu.PrefetchScalarGridSpec(
            num_scalar_prefetch=prefetch, grid=grid, in_specs=in_specs, out_specs=out_specs, scratch_shapes=scratch
        ),
        out_shape=out_shape,
        input_output_aliases=alias or {},
        compiler_params=pltpu.CompilerParams(dimension_semantics=("arbitrary",) * len(grid), vmem_limit_bytes=63 << 20),
        cost_estimate=pl.CostEstimate(flops=flops, bytes_accessed=moved, transcendentals=0),
    )(*args)


def rows_spec(rows, cols):
    return pl.BlockSpec((rows, cols), lambda i, *_: (i, 0))


def whole_spec(shape):
    return pl.BlockSpec(shape, lambda i, *_: (0,) * len(shape))


def cols_spec(rows, cols, top):
    return pl.BlockSpec((rows, cols), lambda i, *_: (0, jnp.minimum(i, top)))


def sds(shape, dtype):
    return jax.ShapeDtypeStruct(shape, dtype)


def block_spec(shape, block):
    return pl.BlockSpec(shape, lambda i, *_: (block,) + (0,) * (len(shape) - 1))


def project(tbl, x, pick, embed, pieces):
    rows = x.shape[0]
    slots = pick.shape[1]
    return call(
        project_kernel, "project", (rows // BLOCK,),
        [rows_spec(BLOCK, D), rows_spec(BLOCK, slots), whole_spec((slots, TDIM))] + [ANY] * 4,
        [rows_spec(BLOCK, D), rows_spec(BLOCK, 2 * QKV), whole_spec((16, D)), whole_spec((slots, D)), ANY],
        [sds((rows, D), BF16), sds((rows, 2 * QKV), BF16), sds((16, D), F32), sds((slots, D), F32), sds((D, 2 * QKV), BF16)],
        [pltpu.VMEM((D, 2 * QKV + 2 * TDIM), BF16), pltpu.VMEM((1, 2 * QKV), F32), pltpu.VMEM((1, 2 * QKV), F32),
         pltpu.SemaphoreType.DMA((2, 32)), pltpu.SemaphoreType.DMA((1,))],
        6 * rows * D * D, 20 << 20, (tbl, x, pick, embed, *pieces),
    )


def attend(block, qkv, pick, segr, before):
    rows = qkv.shape[0]
    return call(
        functools.partial(attend_kernel, block), "attend", (1,),
        [block_spec((BLOCK, 2 * QKV), block), block_spec((BLOCK, pick.shape[1]), block),
         block_spec((1, 1, BLOCK), block)] + [ANY] * len(before),
        [block_spec((BLOCK, D), block), ANY],
        [sds((rows, D), BF16), sds((rows // BLOCK, HEADS // 2, 4, 256, 256), BF16)],
        [pltpu.VMEM((4, 256, 128), F32), pltpu.VMEM((2, 256, 256), F32), pltpu.VMEM((2, 4, 256, 256), BF16),
         pltpu.SemaphoreType.DMA((2,))],
        4 * BLOCK * D * D, 20 << 20, (qkv, pick, segr, *before), prefetch=0,
        alias={3 + i: i for i in range(len(before))},
    )


def expand(tbl, x, pick, slots, mix, vec, upb, up):
    rows = mix.shape[0]
    tile = 256
    return call(
        expand_kernel, "expand", (rows // tile,),
        [rows_spec(tile, D), rows_spec(tile, pick.shape[1]), whole_spec(slots.shape), rows_spec(tile, D), whole_spec((16, D)),
         whole_spec((1, FF))] + [ANY] * 4,
        [rows_spec(tile, D), rows_spec(tile, 1), rows_spec(tile, FF), rows_spec(tile, FF), rows_spec(tile, D), ANY],
        [sds((rows, D), F32), sds((rows, 1), F32), sds((rows, FF), BF16), sds((rows, FF), BF16), sds((rows, D), BF16),
         sds((D, FF + D), BF16)],
        [pltpu.VMEM((D, FF + D), BF16), pltpu.VMEM((2, tile, D), F32), pltpu.SemaphoreType.DMA((2, 32)),
         pltpu.SemaphoreType.DMA((1,))],
        2 * rows * D * (FF + D), 20 << 20, (tbl, x, pick, slots, mix, vec, upb, *up),
    )


def contract(tbl, n1, i1, cot, vec, act, slope, up, pick, down):
    rows = n1.shape[0]
    tile = 256
    slots = pick.shape[1]
    return call(
        contract_kernel, "contract", (rows // tile,),
        [rows_spec(tile, D), rows_spec(tile, 1), rows_spec(tile, D), whole_spec((16, D)), rows_spec(tile, FF),
         rows_spec(tile, FF), ANY, rows_spec(tile, slots)] + [ANY] * 4,
        [rows_spec(tile, D), rows_spec(tile, FF), rows_spec(tile, D), rows_spec(tile, D), rows_spec(tile, D),
         whole_spec((8, D)), whole_spec((1, FF)), whole_spec((slots, D))],
        [sds((rows, D), BF16), sds((rows, FF), BF16), sds((rows, D), BF16), sds((rows, D), F32), sds((rows, D), BF16),
         sds((8, D), F32), sds((1, FF), F32), sds((slots, D), F32)],
        [pltpu.VMEM((FF, D), BF16), pltpu.VMEM((D, FF), BF16), pltpu.VMEM((2, tile, D), F32), pltpu.SemaphoreType.DMA((1, 32)),
         pltpu.SemaphoreType.DMA((1,))],
        6 * rows * D * FF, 20 << 20, (tbl, n1, i1, cot, vec, act, slope, up, pick, *down),
    )


def down_grad(tbl, act, din):
    rows = act.shape[0]
    shape = sds((CHIPS, FF // CHIPS, HALF), BF16)
    return call(
        down_grad_kernel, "down_grad", (4,), [cols_spec(rows, D, 3), whole_spec((rows, D))], [ANY, ANY], [shape, shape],
        [pltpu.VMEM((4, D, D), BF16), pltpu.SemaphoreType.DMA((4, 8))],
        2 * rows * D * FF, 20 << 20, (tbl, act, din),
    )


def up_specs(rows, kind):
    def half(tbl):
        return jnp.where(kind == 0, tbl[CORE_AT], 1 - tbl[CORE_AT])

    return [whole_spec((rows, D)), pl.BlockSpec((rows, D), lambda i, tbl: (0, 2 * half(tbl) + jnp.minimum(i, 1))),
            ANY, ANY]


def up_other(tbl, mlow, dexp, mix, ain):
    rows = mlow.shape[0]
    return call(
        up_other_kernel, "up_other", (3,), up_specs(rows, 1), ANY, sds((CHIPS, 48, 2 * D + HALF), BF16),
        [pltpu.VMEM((3, D, D), BF16), pltpu.VMEM((rows, D), BF16), pltpu.VMEM((rows, HALF), BF16),
         pltpu.SemaphoreType.DMA((3, CHIPS)), pltpu.SemaphoreType.DMA((2,))],
        rows * D * (FF + D), 20 << 20, (tbl, mlow, dexp, mix, ain),
    )


def up_own(tbl, mlow, dexp, mix, ain, got):
    rows = mlow.shape[0]
    shape = sds((CHIPS // 2, 48, 2 * D + HALF), BF16)
    return call(
        up_own_kernel, "up_own", (3,), up_specs(rows, 0) + [ANY], [whole_spec(shape.shape)] * 2, [shape, shape],
        [pltpu.VMEM((D, D), BF16), pltpu.VMEM((D, 2 * D + HALF), BF16), pltpu.VMEM((rows, D), BF16),
         pltpu.VMEM((rows, HALF), BF16), pltpu.SemaphoreType.DMA((CHIPS,)), pltpu.SemaphoreType.DMA((2,))],
        rows * D * (FF + D), 20 << 20, (tbl, mlow, dexp, mix, ain, got),
    )


def qkv_specs(rows, kind):
    def half(tbl):
        return jnp.where(kind == 0, tbl[CORE_AT], 1 - tbl[CORE_AT])

    return [pl.BlockSpec((rows, HALF), lambda i, tbl: (0, i)), pl.BlockSpec((rows, QKV), lambda i, tbl: (0, half(tbl)))]


def qkv_other(tbl, low, dqkv, first, sa, sb, weight, embed, ff, up):
    rows = low.shape[0]
    slots = first.shape[0]
    return call(
        qkv_other_kernel, "qkv_other", (2,),
        qkv_specs(rows, 1) + [whole_spec((slots, D)), whole_spec((slots, 2 * QKV)), whole_spec((slots, 2 * QKV)), ANY,
                              whole_spec((slots, TDIM)), whole_spec((8, D)), whole_spec((4, D))],
        [whole_spec((D, 2 * TDIM)), ANY], [sds((D, 2 * TDIM), BF16), sds((CHIPS, 48, QKV + TDIM), BF16)],
        [pltpu.VMEM((2, HALF, QKV), BF16), pltpu.VMEM((D, 2 * TDIM), BF16), pltpu.VMEM((D, 2 * QKV), BF16),
         pltpu.SemaphoreType.DMA((2, CHIPS // 2)), pltpu.SemaphoreType.DMA((CHIPS,)), pltpu.SemaphoreType.DMA((1,))],
        3 * rows * D * D, 20 << 20, (tbl, low, dqkv, first, sa, sb, weight, embed, ff, up),
    )


def qkv_own(tbl, low, dqkv, small, got):
    rows = low.shape[0]
    shape = sds((CHIPS // 2, 48, QKV + TDIM), BF16)
    return call(
        qkv_own_kernel, "qkv_own", (2,), qkv_specs(rows, 0) + [whole_spec((D, 2 * TDIM)), ANY],
        [whole_spec(shape.shape)] * 2, [shape, shape],
        [pltpu.VMEM((HALF, QKV + TDIM), BF16), pltpu.VMEM((D, QKV + TDIM), BF16), pltpu.SemaphoreType.DMA((CHIPS,))],
        3 * rows * D * D, 20 << 20, (tbl, low, dqkv, small, got),
    )


def attention_backward(block, ain, mix, qkv, probs, weight, pick, before):
    rows = ain.shape[0]
    slots = pick.shape[1]
    return call(
        functools.partial(attention_backward_kernel, block), "attention_backward", (1,),
        [block_spec((BLOCK, D), block), block_spec((BLOCK, D), block), ANY, ANY, pl.BlockSpec((D, D), lambda i, *_: (0, 4)),
         block_spec((BLOCK, slots), block)] + [ANY] * len(before),
        [block_spec((BLOCK, 2 * QKV), block), whole_spec((slots, 2 * QKV))],
        [sds((rows, 2 * QKV), BF16), sds((slots, 2 * QKV), F32)],
        [pltpu.VMEM((BLOCK, D), BF16), pltpu.VMEM((HEADS // 2, 4, 1, 256), F32), pltpu.VMEM((2, 256, 256), F32),
         pltpu.VMEM((BLOCK, 128), F32), pltpu.VMEM((BLOCK, 128), F32), pltpu.VMEM((BLOCK, 2 * QKV), BF16),
         pltpu.VMEM((HEADS // 2, 4, 256, 256), BF16), pltpu.SemaphoreType.DMA((2,))],
        4 * BLOCK * D * D, 20 << 20, (ain, mix, qkv, probs, weight, pick, *before), prefetch=0,
        alias={6 + i: i for i in range(len(before))},
    )


def input_gradient(df, dqkv, weight):
    rows = df.shape[0]
    tile = 256
    return call(
        input_grad_kernel, "input_grad", (rows // tile,),
        [rows_spec(tile, D), rows_spec(tile, 2 * QKV), whole_spec((D, 2 * QKV))], rows_spec(tile, D), sds((rows, D), F32), [],
        6 * rows * D * D, 20 << 20, (df, dqkv, weight), prefetch=0,
    )


def flip(n, even_bit, odd_bit):
    return [(i, i ^ (odd_bit if i & 1 else even_bit)) for i in range(n)]


def tiled_route(n):
    return {"core": flip(n, 1, 1), "z2": flip(n, 16, 16), "z1": flip(n, 8, 8), "a": flip(n, 2, 4), "b": flip(n, 4, 2)}


def tables(n):
    me = lax.axis_index("fsdp")
    core = me % 2
    chips = jnp.arange(CHIPS, dtype=jnp.int32)
    if n == 32:
        here = me // 2

        def order(kind):
            low, high = jnp.where(kind == 0, 1, 2), jnp.where(kind == 0, 2, 1)
            bits = (chips & 1) * 8 + ((chips >> 1) & 1) * 4 + ((chips >> 2) & 1) * low + (chips >> 3) * high
            return here ^ bits

        def place(kind):
            diff = here ^ chips
            x, y = diff & 1, (diff >> 1) & 1
            low, high = jnp.where(kind == 0, x, y), jnp.where(kind == 0, y, x)
            return (diff >> 3) + ((diff >> 2) & 1) * 2 + low * 4 + high * 8

        parts = [order(core), order(1 - core), place(core), place(1 - core)]
    else:
        parts = [chips] * 4
    return jnp.concatenate(parts + [jnp.full((16,), core, jnp.int32)]).astype(jnp.int32)


def own_half(halves, core):
    return jnp.where(core == 0, halves[0], halves[1]), jnp.where(core == 0, halves[1], halves[0])


def tie(*values):
    return lax.optimization_barrier(values)


def follow(first, *values):
    return lax.optimization_barrier((first,) + values)[1:]


def send_on(value, step, n):
    return lax.ppermute(value, "fsdp", perm=tiled_route(n)[step])


def halves_kernel(core_ref, q, k, v, o, up, down, time, columns, mine_a, mine_u, mine_d, theirs):
    core = core_ref[0]
    rows = q.shape[0]

    def half(ref, which, width):
        return ref[:, pl.ds(pl.multiple_of(which * width, 128), width)]

    for which, first in ((core, True), (1 - core, False)):
        tail = jnp.where(which == 0, time[...].astype(F32), columns[...].astype(F32)).astype(BF16)
        a = [half(q, which, HALF), half(k, which, HALF), half(v, which, HALF), tail]
        u = [half(up, which, FF // 2), half(o, which, HALF)]
        d = half(down, which, HALF)
        if first:
            mine_a[...] = jnp.concatenate(a, axis=1)
            mine_u[...] = jnp.concatenate(u, axis=1)
            mine_d[...] = d
        else:
            d = [d[rows * j : rows * j + rows, :] for j in range(d.shape[0] // rows)]
            theirs[...] = jnp.concatenate(a + u + d, axis=1)


def chip_shards(core, q, k, v, o, up, down, time, columns, n):
    rows = q.shape[0]
    down_rows = down.shape[0]
    widths = (QKV + TDIM, FF // 2 + HALF, HALF * down_rows // rows)
    args = (q, k, v, o, up, down, time, columns)
    shapes = [sds((rows, widths[0]), BF16), sds((rows, widths[1]), BF16), sds((down_rows, HALF), BF16), sds((rows, sum(widths)), BF16)]
    mine_a, mine_u, mine_d, theirs = call(
        halves_kernel, "halves", (1,), [whole_spec(item.shape) for item in args], [whole_spec(item.shape) for item in shapes],
        shapes, [], 1 << 10, 1 << 20, (core.reshape(1), *args),
    )
    got = send_on(theirs, "core", n)
    got_d = got[:, widths[0] + widths[1] :]
    got_d = jnp.concatenate([got_d[:, HALF * j : HALF * j + HALF] for j in range(down_rows // rows)], axis=0)
    shards = []
    for mine, came in ((mine_a, got[:, : widths[0]]), (mine_u, got[:, widths[0] : widths[0] + widths[1]]), (mine_d, got_d)):
        shards.append(jnp.concatenate(own_half((mine, came), core), axis=0)[None])
    return shards


def whole_gather(halves, core):
    full = [lax.all_gather(half, "fsdp", axis=0, tiled=True) for half in halves]
    full = [item.reshape(CHIPS, -1, item.shape[1]) for item in full]
    own, other = own_half(full, core)
    middle = CHIPS // 2
    return own[:middle], own[middle:], other[:middle], other[middle:]


def widen(held, step, n):
    return jnp.concatenate([held, send_on(held, step, n)], axis=0)


def add(left, right):
    return (left.astype(F32) + right.astype(F32)).astype(BF16)


def halve(keep, got):
    middle = keep.shape[0] // 2
    return add(keep[:middle], got[:middle]), add(keep[middle:], got[middle:])


def finish(keep, got, n):
    core = lax.axis_index("fsdp") % 2
    total = keep[0].astype(F32) + got[0].astype(F32)
    rows = total.shape[0] // 2
    mine, theirs = own_half((total[:rows], total[rows:]), core)
    got = send_on(theirs.astype(BF16), "core", n).astype(F32)
    return own_half((mine, got), core)


def whole_reduce(own, other, core):
    sums = []
    for item in own_half((own, other), core):
        item = item.reshape(-1, item.shape[2])
        sums.append(lax.psum_scatter(item, "fsdp", scatter_dimension=0, tiled=True).astype(F32))
    return sums


def sinusoid(steps):
    half = TDIM // 2
    freqs = jnp.exp(-math.log(10000.0) * jnp.arange(half, dtype=F32) / half)
    angles = steps.astype(F32)[:, None] * freqs[None, :]
    return jnp.concatenate([jnp.cos(angles), jnp.sin(angles)], axis=1)


def body(
    inputs, cotangent, lengths, timesteps, time_weight, time_bias, query_weight, query_bias, key_weight,
    value_weight, value_bias, out_weight, out_bias, mid_gain, mid_shift, up_weight, up_bias, down_weight,
    down_bias, last_gain, last_shift,
):
    n = lax.axis_size("fsdp")
    rows = inputs.shape[0]
    blocks = rows // BLOCK
    tbl = tables(n)
    shard = D // n

    vectors = [query_bias, value_bias, out_bias, mid_gain, mid_shift, down_bias, last_gain, last_shift, time_bias]
    vectors += [up_bias[shard * k : shard * (k + 1)] for k in range(FF // D)]
    lane = lax.broadcasted_iota(jnp.int32, (shard, TDIM), 1)
    columns = jnp.zeros((shard, TDIM), F32)
    for k, item in enumerate(vectors):
        columns = jnp.where(lane == k, item.astype(F32)[:, None], columns)
    columns = columns.astype(BF16)
    small_halves = [time_weight.T, columns]
    attn_halves = [
        jnp.concatenate(
            [w[:, HALF * h : HALF * h + HALF] for w in (query_weight, key_weight, value_weight)] + [small_halves[h]], axis=1
        )
        for h in range(2)
    ]
    up_halves = [
        jnp.concatenate([up_weight[:, FF // 2 * h : FF // 2 * (h + 1)], out_weight[:, HALF * h : HALF * h + HALF]], axis=1)
        for h in range(2)
    ]
    down_halves = [down_weight[:, :HALF], down_weight[:, HALF:]]

    core = lax.axis_index("fsdp") % 2
    tiled = n == 32

    def slot_arrays(lengths, timesteps):
        ends = jnp.cumsum(lengths, axis=1)
        position = jnp.arange(BLOCK, dtype=jnp.int32)
        owner = jnp.sum((position[None, :, None] >= ends[:, None, :]).astype(jnp.int32), axis=2)
        slot_of = (owner + SLOTS * jnp.arange(blocks, dtype=jnp.int32)[:, None]).reshape(rows, 1)
        pick = (slot_of == lax.broadcasted_iota(jnp.int32, (rows, blocks * SLOTS), 1)).astype(BF16)
        segr = slot_of.reshape(blocks, 1, BLOCK).astype(F32)
        embed_in = sinusoid(timesteps.reshape(-1)).astype(BF16)
        return pick, segr, embed_in

    if tiled:
        a0, u0, d0 = chip_shards(
            core, query_weight, key_weight, value_weight, out_weight, up_weight, down_weight, time_weight.T, columns, n
        )
        a0 = widen(a0, "z2", n)
        pick, segr, embed_in = slot_arrays(*follow(a0, lengths, timesteps))
        a0 = widen(a0, "z1", n)
        (u0,) = follow(a0, u0)
        a0 = widen(a0, "a", n)
        u0 = widen(u0, "z2", n)
        a0, u0 = tie(a0, u0)
        a1 = send_on(a0, "b", n)
        a2 = send_on(a0, "core", n)
        u0 = widen(u0, "z1", n)
        a1, u0, d0, tbl, pick, segr, embed_in = tie(a1, u0, d0, tbl, pick, segr, embed_in)
        a3 = send_on(a1, "core", n)
        u_got = send_on(u0, "a", n)
        d_got = send_on(d0, "z2", n)
        low, qkv, vec, slots, weight = project(tbl, inputs, pick, embed_in, (a0, a1, a2, a3))
        qkv, u0, u_got, d0, d_got = tie(qkv, u0, u_got, d0, d_got)
        u0 = jnp.concatenate([u0, u_got], axis=0)
        d0 = jnp.concatenate([d0, d_got], axis=0)
        u1 = send_on(u0, "b", n)
        d_got = send_on(d0, "z1", n)
        u2 = send_on(u0, "core", n)
        parts = attend(0, qkv, pick, segr, ())
        *parts, qkv, u0, u2, d0, d_got = tie(*parts, qkv, u0, u2, d0, d_got)
        d0 = jnp.concatenate([d0, d_got], axis=0)
        d_got = send_on(d0, "a", n)
        mix, probs = attend(1, qkv, pick, segr, parts)
        mix, u1, d0, d_got = tie(mix, u1, d0, d_got)
        u3 = send_on(u1, "core", n)
        d0 = jnp.concatenate([d0, d_got], axis=0)
        d1 = send_on(d0, "b", n)
        d2 = send_on(d0, "core", n)
        up_offset = vec[9:13].reshape(FF // D, n, shard).transpose(1, 0, 2).reshape(1, FF)
        n1, i1, act, slope, mlow, up_full = expand(tbl, inputs, pick, slots, mix, vec, up_offset, (u0, u1, u2, u3))
        act, d1 = tie(act, d1)
        d3 = send_on(d1, "core", n)
        down_pieces = (d0, d1, d2, d3)
    else:
        pick, segr, embed_in = slot_arrays(lengths, timesteps)
        low, qkv, vec, slots, weight = project(tbl, inputs, pick, embed_in, whole_gather(attn_halves, core))
        mix, probs = attend(1, qkv, pick, segr, attend(0, qkv, pick, segr, ()))
        up_offset = vec[9:13].reshape(FF // D, n, shard).transpose(1, 0, 2).reshape(1, FF)
        n1, i1, act, slope, mlow, up_full = expand(tbl, inputs, pick, slots, mix, vec, up_offset, whole_gather(up_halves, core))
        down_pieces = whole_gather(down_halves, core)

    res, dexp, din, df, ain, ff_vecs, up_vec, slot_first = contract(
        tbl, n1, i1, cotangent, vec, act, slope, up_full, pick, down_pieces
    )
    up_vec = up_vec.reshape(n, FF // D, shard).transpose(1, 0, 2).reshape(FF // D, D)
    d_own, d_other = down_grad(tbl, act, din)
    mlow, d_own, d_other = tie(mlow, d_own, d_other)
    u_other = up_other(tbl, mlow, dexp, mix, ain)
    if tiled:
        d_got = send_on(d_other, "core", n)
        u_other, d_own, d_got, mlow, up_vec = tie(u_other, d_own, d_got, mlow, up_vec)
        u_got = send_on(u_other, "core", n)
        d_keep, d_away = halve(d_own, d_got)
        d_keep, d_away, u_got = tie(d_keep, d_away, u_got)
        d_got = send_on(d_away, "b", n)
        u_keep, u_away = up_own(tbl, mlow, dexp, mix, ain, u_got)
        ain, u_keep, u_away = tie(ain, u_keep, u_away)
        u_got = send_on(u_away, "b", n)
        dqkv, slot0 = attention_backward(0, ain, mix, qkv, probs, up_full, pick, ())
        dqkv, d_keep, d_got = tie(dqkv, d_keep, d_got)
        d_keep, d_away = halve(d_keep, d_got)
        ain, dqkv, d_keep, d_away = tie(ain, dqkv, d_keep, d_away)
        d_got = send_on(d_away, "a", n)
        dqkv, slot1 = attention_backward(1, ain, mix, qkv, probs, up_full, pick, (dqkv,))
        dqkv, d_keep, d_got, u_keep, u_got = tie(dqkv, d_keep, d_got, u_keep, u_got)
        u_keep, u_away = halve(u_keep, u_got)
        d_keep, d_away = halve(d_keep, d_got)
        low, dqkv, d_keep, d_away, u_keep, u_away = tie(low, dqkv, d_keep, d_away, u_keep, u_away)
        u_got = send_on(u_away, "a", n)
        d_got = send_on(d_away, "z1", n)
        small, q_other = qkv_other(
            tbl, low, dqkv, slot_first, slot0, slot1, weight, embed_in, ff_vecs, up_vec
        )
        q_other, u_keep, u_got, d_keep, d_got, low = tie(q_other, u_keep, u_got, d_keep, d_got, low)
        q_got = send_on(q_other, "core", n)
        u_keep, u_away = halve(u_keep, u_got)
        d_keep, d_away = halve(d_keep, d_got)
        q_got, u_keep, u_away, d_keep, d_away = tie(q_got, u_keep, u_away, d_keep, d_away)
        u_got = send_on(u_away, "z1", n)
        q_keep, q_away = qkv_own(tbl, low, dqkv, small, q_got)
        df, q_keep, q_away, u_keep, u_got = tie(df, q_keep, q_away, u_keep, u_got)
        q_got = send_on(q_away, "b", n)
        u_keep, u_away = halve(u_keep, u_got)
        df, d_away, u_keep, u_away = tie(df, d_away, u_keep, u_away)
        d_got = send_on(d_away, "z2", n)
        u_got = send_on(u_away, "z2", n)
        input_grad = input_gradient(df, dqkv, weight)
        input_grad, q_keep, q_got = tie(input_grad, q_keep, q_got)
        q_keep, q_away = halve(q_keep, q_got)
        u_keep, u_got, d_keep, d_got = follow(q_away, u_keep, u_got, d_keep, d_got)
        q_got = send_on(q_away, "a", n)
        down_sum = finish(d_keep, d_got, n)
        q_keep, q_away = halve(q_keep, q_got)
        q_got = send_on(q_away, "z1", n)
        up_sum = finish(u_keep, u_got, n)
        q_keep, q_away = halve(q_keep, q_got)
        q_got = send_on(q_away, "z2", n)
        qkv_sum = finish(q_keep, q_got, n)
    else:
        dqkv, slot0 = attention_backward(0, ain, mix, qkv, probs, up_full, pick, ())
        dqkv, slot1 = attention_backward(1, ain, mix, qkv, probs, up_full, pick, (dqkv,))
        small, q_other = qkv_other(
            tbl, low, dqkv, slot_first, slot0, slot1, weight, embed_in, ff_vecs, up_vec
        )
        input_grad = input_gradient(df, dqkv, weight)
        down_sum = whole_reduce(d_own, d_other, core)
        zero_u, zero_q = jnp.zeros_like(u_other), jnp.zeros_like(q_other)
        u_own = jnp.concatenate(up_own(tbl, mlow, dexp, mix, ain, zero_u), axis=0)
        q_own = jnp.concatenate(qkv_own(tbl, low, dqkv, small, zero_q), axis=0)
        up_sum = whole_reduce(u_own, u_other, core)
        qkv_sum = whole_reduce(q_own, q_other, core)
    def both(pair, start, stop):
        return jnp.concatenate([half[:, start:stop] for half in pair], axis=1)

    out_query = both(qkv_sum, 0, HALF)
    out_key = both(qkv_sum, HALF, 2 * HALF)
    out_value = both(qkv_sum, 2 * HALF, QKV)
    out_up = both(up_sum, 0, 2 * D)
    out_out = both(up_sum, 2 * D, 2 * D + HALF)
    out_down = both(down_sum, 0, HALF)
    out_time = qkv_sum[0][:, QKV:].T
    v = qkv_sum[1][:, QKV : QKV + 13].T
    v_up = v[9:13].reshape(-1)
    return (
        res, input_grad, out_time, out_query, out_key, out_value, out_out, out_up, out_down,
        v[0], v[1], v[2], v[8], v[6], v[7], v_up, v[5], v[3], v[4],
    )


def solution(mesh):
    row, col, vec = P("fsdp", None), P(None, "fsdp"), P("fsdp")
    in_specs = (
        row, row, row, row, col, vec, row, vec, row, row, vec, row, vec, vec, vec, row, vec, row, vec, vec, vec,
    )
    out_specs = (row, row, col, row, row, row, row, row, row) + (vec,) * 10
    return jax.shard_map(body, mesh=mesh, in_specs=in_specs, out_specs=out_specs, check_vma=False)
```
